32 devices in a mesh: dp: 8 (over y, x, core), seq: 4 (over z).
Axes of the slice: x: 2, y: 2, z: 4, core: 2. Of those that a mesh axis runs over, the one named last changes fastest.
Arguments:
- tokens: bfloat16 [8, 512, 6, 768], P('dp', 'seq'), may hold values from -6 to 6
- kind: int32 [8], P('dp'), may hold values from 0 to 1, as said below
- ln1_gain: float32 [768], replicated, may hold values from 0.1 to 1.9
- w_in: bfloat16 [768, 2304], replicated, may hold values from -0.21875 to 0.21875
- short_taps: float32 [3, 2304], replicated, may hold values from -3 to 3
- cond_taps: float32 [3, 768], replicated, may hold values from -3 to 3
- w_cond: bfloat16 [768, 768], replicated, may hold values from -0.21875 to 0.21875
- cond_bias: float32 [768], replicated, may hold values from -3 to 3
- w_out: bfloat16 [768, 768], replicated, may hold values from -0.21875 to 0.21875
- ln2_gain: float32 [768], replicated, may hold values from 0.1 to 1.9
- w_gate: bfloat16 [768, 3072], replicated, may hold values from -0.21875 to 0.21875
- w_up: bfloat16 [768, 3072], replicated, may hold values from -0.21875 to 0.21875
- w_down: bfloat16 [3072, 768], replicated, may hold values from -0.109375 to 0.109375
- cotangent: bfloat16 [8, 512, 6, 768], P('dp', 'seq'), may hold values from -6 to 6
Outputs:
- layer_out: bfloat16 [8, 512, 6, 768], P('dp', 'seq')
- grad_tokens: bfloat16 [8, 512, 6, 768], P('dp', 'seq')
- grad_ln1: float32 [768], P('seq')
- grad_w_in: float32 [768, 2304], P('seq')
- grad_short_taps: float32 [3, 2304], P(None, 'seq')
- grad_cond_taps: float32 [3, 768], P(None, 'seq')
- grad_w_cond: float32 [768, 768], P('seq')
- grad_cond_bias: float32 [768], P('seq')
- grad_w_out: float32 [768, 768], P('seq')
- grad_ln2: float32 [768], P('seq')
- grad_gate: float32 [768, 3072], P('seq')
- grad_up: float32 [768, 3072], P('seq')
- grad_down: float32 [3072, 768], P('seq')
The draws below stay inside these ranges and needn't reach their ends.
Inputs may be any that keep to these rules, and one draw needn't show every extreme that they name: Exactly 4 groups have kind 1.
All inputs are finite; a program needn't handle non-finite values.
Results may differ from the reference program's by a relative error of at most 0.017.
Values may be sent and summed in bfloat16 or wider, within the bound.
A program may use at most 256 MiB of HBM per device.

```python
import jax
import jax.numpy as jnp
from jax import lax

D = 768
FF = 3072
SHORT = 128
LONG = 512
SLOTS = 6
GROUPS = 8


def draw_kind(key, part):
    order = jax.random.permutation(key, GROUPS)
    return (order < GROUPS // 2).astype(jnp.int32)


def shard_levels(own_key, extent, pieces, least, high):
    loudness, own = 1.0, jax.random.fold_in(own_key, 6)
    for axis_at, parts in pieces:
        draws = jnp.exp(jax.random.uniform(jax.random.fold_in(own, axis_at), (parts,), jnp.float32, least / len(pieces), high / len(pieces)))
        loudness = loudness * jnp.repeat(draws, extent[axis_at] // parts).reshape([-1 if axis == axis_at else 1 for axis in range(len(extent))])
    return loudness


def centred(key, shape, deviation, bound, split=(), held_as=jnp.bfloat16):
    gain = shard_levels(key, shape, split, -0.22, 0.18) if split else 1.0
    values = jax.random.normal(key, shape, jnp.float32) * deviation * gain
    return jnp.minimum(jnp.maximum(values, -bound), bound).astype(held_as)


def setup_inputs(seed: int = 0) -> dict:
    key_list = jax.random.split(jax.random.key(seed), 15)
    return {
        "tokens": centred(key_list[0], (GROUPS, LONG, SLOTS, D), 1.0, 6.0, ((0, 8), (1, 4))),
        "kind": draw_kind(jax.random.fold_in(key_list[14], 71), 0),
        "ln1_gain": jnp.clip(1.0 + 0.18 * jax.random.normal(key_list[2], (D,), jnp.float32), 0.1, 1.9),
        "w_in": centred(key_list[3], (D, 3 * D), D ** -0.5, 0.21875),
        "short_taps": centred(key_list[4], (3, 3 * D), 0.5, 3.0, (), jnp.float32),
        "cond_taps": centred(key_list[5], (3, D), 0.5, 3.0, (), jnp.float32),
        "w_cond": centred(key_list[6], (D, D), D ** -0.5, 0.21875),
        "cond_bias": centred(key_list[7], (D,), 0.5, 3.0, (), jnp.float32),
        "w_out": centred(key_list[8], (D, D), D ** -0.5, 0.21875),
        "ln2_gain": jnp.clip(1.0 + 0.18 * jax.random.normal(key_list[9], (D,), jnp.float32), 0.1, 1.9),
        "w_gate": centred(key_list[10], (D, FF), D ** -0.5, 0.21875),
        "w_up": centred(key_list[11], (D, FF), D ** -0.5, 0.21875),
        "w_down": centred(key_list[12], (FF, D), FF ** -0.5, 0.109375),
        "cotangent": centred(key_list[13], (GROUPS, LONG, SLOTS, D), 1.0, 6.0, ((0, 8), (1, 4))),
    }


@jax.custom_vjp
def low(v):
    return lax.optimization_barrier(v.astype(jnp.bfloat16)).astype(jnp.float32)

@jax.custom_vjp
def low_back(v):
    return v

def low_keep(v):
    return (low(v), None)

def low_pass(kept, grad):
    return (grad,)

def back_keep(v):
    return (v, None)

def back_low(kept, grad):
    return (low(grad),)
low.defvjp(low_keep, low_pass)
low_back.defvjp(back_keep, back_low)
highest = lax.Precision.HIGHEST
epsilon = 1e-05

def norm_rows(values, scale_gain):
    row_mean = lax.optimization_barrier(jnp.mean(values, axis=-1, keepdims=True))
    centered = values - row_mean
    variance = lax.optimization_barrier(jnp.mean(centered * centered, axis=-1, keepdims=True))
    return centered * lax.rsqrt(variance + epsilon) * scale_gain

def causal_conv(field, taps, offset):
    result = taps[0] * field
    for lag_step in (1, 2):
        moved = jnp.pad(field, ((0, 0), (lag_step, 0), (0, 0)))[:, :-lag_step]
        valid = (offset >= lag_step).astype(jnp.float32)[None, :, None]
        result = result + taps[lag_step] * moved * valid
    return result

def spectral_mix(signal, cond_field, w_cond, cond_bias, span_len):
    slot_count, positions, channels = signal.shape
    shaped_signal = signal.reshape(slot_count, positions // span_len, span_len, channels)
    shaped_cond = cond_field.reshape(slot_count, positions // span_len, span_len, channels)
    cond_spec = jnp.fft.fft(shaped_cond, axis=2)
    real_part = jnp.real(cond_spec)
    imag_part = jnp.imag(cond_spec)
    power_spec = (real_part * real_part + imag_part * imag_part) / span_len
    features = low(jnp.log1p(power_spec))
    pre_tanh = low_back(jnp.einsum('abfc,cd->abfd', features, w_cond, precision=highest) + cond_bias)
    spectral_gain = 1.0 + jnp.tanh(pre_tanh)
    mixed_spec = spectral_gain * jnp.fft.fft(shaped_signal, axis=2)
    return jnp.real(jnp.fft.ifft(mixed_spec, axis=2)).reshape(slot_count, positions, channels)

def group_forward(group_tokens, long_flag, params):
    ln1_gain, w_in, short_taps, cond_taps, w_cond, cond_bias, w_out, ln2_gain, w_gate, w_up, w_down = params
    model_width = group_tokens.shape[-1]
    positions = jnp.arange(LONG, dtype=jnp.int32)
    offset = jnp.where(long_flag == 1, positions, positions % SHORT)
    normed_one = low(norm_rows(group_tokens, ln1_gain))
    projected = low_back(low(jnp.einsum('spd,de->spe', normed_one, w_in, precision=highest)))
    conv_out = causal_conv(projected, short_taps, offset)
    query_conv = conv_out[:, :, :model_width]
    key_conv = conv_out[:, :, model_width:2 * model_width]
    value_low = low(conv_out[:, :, 2 * model_width:])
    cond_field = low(causal_conv(value_low, cond_taps, offset))
    signal = low(key_conv * value_low)
    long_mix = spectral_mix(signal, cond_field, w_cond, cond_bias, LONG)
    short_mix = spectral_mix(signal, cond_field, w_cond, cond_bias, SHORT)
    filtered = low_back(jnp.where(long_flag == 1, long_mix, short_mix))
    mixed = low(query_conv * filtered)
    hidden_one = group_tokens + low_back(jnp.einsum('spd,de->spe', mixed, w_out, precision=highest))
    normed_two = low(norm_rows(hidden_one, ln2_gain))
    gate_pre = low_back(jnp.einsum('spd,df->spf', normed_two, w_gate, precision=highest))
    up_proj = low_back(jnp.einsum('spd,df->spf', normed_two, w_up, precision=highest))
    hidden_act = low(jax.nn.silu(gate_pre) * up_proj)
    return hidden_one + jnp.einsum('spf,fd->spd', hidden_act, w_down, precision=highest)

def reference(tokens, kind, ln1_gain, w_in, short_taps, cond_taps, w_cond, cond_bias, w_out, ln2_gain, w_gate, w_up, w_down, cotangent):
    params = tuple((weight_item.astype(jnp.float32) for weight_item in (ln1_gain, w_in, short_taps, cond_taps, w_cond, cond_bias, w_out, ln2_gain, w_gate, w_up, w_down)))
    zero_totals = jax.tree.map(jnp.zeros_like, params)

    def one_group(totals, inputs):
        group_tokens, group_cot, long_flag = inputs
        tokens_f = jnp.transpose(group_tokens.astype(jnp.float32), (1, 0, 2))
        cot_f = jnp.transpose(group_cot.astype(jnp.float32), (1, 0, 2))
        result, pullback = jax.vjp(lambda tok_in, par_in: group_forward(tok_in, long_flag, par_in), tokens_f, params)
        grad_in, grad_params = pullback(cot_f)
        totals = jax.tree.map(lambda running, adding: running + adding, totals, grad_params)
        out_rows = jnp.transpose(result, (1, 0, 2)).astype(jnp.bfloat16)
        grad_rows = jnp.transpose(grad_in, (1, 0, 2)).astype(jnp.bfloat16)
        return (totals, (out_rows, grad_rows))
    totals, (layer_out, grad_tokens) = lax.scan(one_group, zero_totals, (tokens, cotangent, kind))
    return (layer_out, grad_tokens, totals[0], totals[1], totals[2], totals[3], totals[4], totals[5], totals[6], totals[7], totals[8], totals[9], totals[10])
```

```python
import functools
import math

import jax
import jax.numpy as jnp
from jax import lax
from jax.experimental import pallas as pl
from jax.experimental.pallas import tpu as pltpu
from jax.sharding import PartitionSpec as P

BF = jnp.bfloat16
F32 = jnp.float32
MESH = pl.DeviceIdType.MESH
EPS = 1e-05
CB = 256
FC = 384
RB = 256
VMEM_LIMIT = 60 * 2**20


def mm(a, b):
    return jnp.dot(a, b, preferred_element_type=F32)


def mm_nt(a, b):
    return lax.dot_general(a, b, (((1,), (1,)), ((), ())), preferred_element_type=F32)


def mm_tn(a, b):
    return lax.dot_general(a, b, (((0,), (0,)), ((), ())), preferred_element_type=F32)


def unit_rows(x):
    mean = jnp.mean(x, axis=-1, keepdims=True)
    centered = x - mean
    r = lax.rsqrt(jnp.mean(centered * centered, axis=-1, keepdims=True) + EPS)
    return centered * r, r


def unit_back(g, u, r, gain):
    e = g * gain
    return r * (
        e - jnp.mean(e, axis=-1, keepdims=True) - u * jnp.mean(e * u, axis=-1, keepdims=True)
    )


def lanes(ref, width):
    m = ref[...]
    return jnp.concatenate([m] * (width // m.shape[1]), axis=1)


def down(a, j):
    return pltpu.roll(a, j, axis=0)


def up(a, j):
    return pltpu.roll(a, a.shape[0] - j, axis=0)


def conv(a, taps, m1, m2):
    return taps[0:1] * a + taps[1:2] * (down(a, 1) * m1) + taps[2:3] * (down(a, 2) * m2)


def conv_back(g, taps, m1, m2):
    return taps[0:1] * g + taps[1:2] * up(g * m1, 1) + taps[2:3] * up(g * m2, 2)


def tap_sums(g, a, m1, m2):
    return jnp.concatenate(
        [
            jnp.sum(g * a, axis=0, keepdims=True),
            jnp.sum(g * (down(a, 1) * m1), axis=0, keepdims=True),
            jnp.sum(g * (down(a, 2) * m2), axis=0, keepdims=True),
        ],
        axis=0,
    )


def cols_at(c, width, base=0):
    return pl.ds(pl.multiple_of(base + c * width, 128), width)


def wave_tables(is_long, short, span_long, freqs):
    i = jnp.arange(freqs, dtype=jnp.int32)[:, None]
    t = jnp.arange(span_long, dtype=jnp.int32)[None, :]
    blocks, half = span_long // short, short // 2 + 1
    f_short, b_short = i % half, i // half
    phase = jnp.where(
        is_long, (i * t) % span_long, ((f_short * (t % short)) % short) * blocks
    )
    kept = jnp.where(is_long, i <= span_long // 2, (b_short < blocks) & (t // short == b_short))
    angle = phase.astype(F32) * (2.0 * math.pi / span_long)
    kept_f = kept.astype(F32)
    table = jnp.concatenate([jnp.cos(angle) * kept_f, jnp.sin(angle) * kept_f], axis=0)
    once = jnp.where(
        is_long, (i == 0) | (i == span_long // 2), (f_short == 0) | (f_short == short // 2)
    )
    used = jnp.where(is_long, i <= span_long // 2, b_short < blocks)
    mult = jnp.where(used, jnp.where(once, 1.0, 2.0), 0.0).astype(F32)
    table = table.astype(BF)
    return table, table.T, jnp.broadcast_to(mult, (freqs, 128))


def reshard_in_kernel(tok_ref, cot_ref, xs_ref, cs_ref, local_sem, send_sem, recv_sem):
    dp, me = lax.axis_index("dp"), lax.axis_index("seq")
    n = lax.axis_size("seq")
    rows = tok_ref.shape[1]
    barrier = pltpu.get_barrier_semaphore()
    for k in range(1, n):
        pl.semaphore_signal(
            barrier, inc=1, device_id=(dp, lax.rem(me + k, n)), device_id_type=MESH
        )
    pl.semaphore_wait(barrier, n - 1)
    at = pl.ds(pl.multiple_of(me * rows, rows), rows)
    half_at = pl.ds(pl.multiple_of(n * rows + lax.rem(me, 2) * rows, rows), rows)

    def copies(k, peer):
        moves = [
            (tok_ref.at[peer], xs_ref.at[0, at]),
            (tok_ref.at[n + peer // 2], xs_ref.at[1, at]),
            (cot_ref.at[peer], cs_ref.at[at]),
            (cot_ref.at[n + peer // 2], cs_ref.at[half_at]),
        ]
        if k == 0:
            return [
                pltpu.make_async_copy(s, d, local_sem.at[j]) for j, (s, d) in enumerate(moves)
            ]
        return [
            pltpu.make_async_remote_copy(
                src_ref=s,
                dst_ref=d,
                send_sem=send_sem.at[j, k],
                recv_sem=recv_sem.at[j, k],
                device_id=(dp, peer),
                device_id_type=MESH,
            )
            for j, (s, d) in enumerate(moves)
        ]

    peers = [lax.rem(me + k, n) for k in range(n)]
    sources = [lax.rem(me + n - k, n) for k in range(n)]
    sends_half = [lax.rem(p, 2) == me // 2 for p in peers]
    gets_half = [lax.rem(me, 2) == s // 2 for s in sources]
    all_copies = [copies(k, peers[k]) for k in range(n)]
    for j in range(3):
        for k in range(n):
            all_copies[k][j].start()
    for k in range(n):
        pl.when(sends_half[k])(all_copies[k][3].start)
    for j in range(3):
        for k in range(n):
            all_copies[k][j].wait()
    pl.when(sends_half[0])(all_copies[0][3].wait)
    for k in range(1, n):
        pl.when(sends_half[k])(all_copies[k][3].wait_send)
        pl.when(gets_half[k])(all_copies[k][3].wait_recv)


def reshard_in(tok, cot):
    slots, rows, d = tok.shape
    n = lax.axis_size("seq")
    any_spec = pl.BlockSpec(memory_space=pl.ANY)
    return pl.pallas_call(
        reshard_in_kernel,
        name="reshard_in",
        out_shape=(
            jax.ShapeDtypeStruct((2, n * rows, d), BF),
            jax.ShapeDtypeStruct((n * rows + n * rows // 2, d), BF),
        ),
        in_specs=[any_spec] * 2,
        out_specs=(any_spec, any_spec),
        scratch_shapes=[
            pltpu.SemaphoreType.DMA((4,)),
            pltpu.SemaphoreType.DMA((4, n)),
            pltpu.SemaphoreType.DMA((4, n)),
        ],
        compiler_params=pltpu.CompilerParams(collective_id=0, has_side_effects=True),
    )(tok, cot)


def fwd_kernel(
    isp_ref, x_ref, g1_ref, win_ref, st_ref, ct_ref, wc_ref, cb_ref, w_ref, wt_ref,
    m1_ref, m2_ref, mult_ref,
    proj_ref, mixed_ref, filt_ref, xs_ref, xc_ref, th_ref, feat_ref,
    n1_s, q_s,
):
    t, d = n1_s.shape
    f = th_ref.shape[1]
    isp = isp_ref[0]

    @pl.loop(0, t // 128)
    def _(r):
        rows = pl.ds(pl.multiple_of(r * 128, 128), 128)
        u, _ = unit_rows(x_ref[0, rows, :].astype(F32))
        n1_s[rows, :] = (u * g1_ref[...]).astype(BF)

    @pl.loop(0, d // CB)
    def _(c):
        m1, m2 = lanes(m1_ref, CB), lanes(m2_ref, CB)
        own = cols_at(c, CB)

        def part(k):
            cols = cols_at(c, CB, k * d)
            p = mm(n1_s[...], win_ref[:, cols]).astype(BF)
            proj_ref[0, :, cols] = p
            return conv(p.astype(F32), st_ref[:, cols], m1, m2)

        q_s[:, own] = part(0)
        key = part(1)
        value = part(2).astype(BF)
        value_f = value.astype(F32)
        signal = (key * value_f).astype(BF)
        xs_ref[0, :, own] = mm(w_ref[...], signal).astype(BF)
        cond = conv(value_f, ct_ref[:, own], m1, m2).astype(BF)
        xc = mm(w_ref[...], cond)
        xc_ref[0, :, own] = xc.astype(BF)
        power = (xc[:f] * xc[:f] + xc[f:] * xc[f:]) * isp
        feat_ref[0, :, own] = jnp.log1p(power).astype(BF)

    @pl.loop(0, d // CB)
    def _(c):
        own = cols_at(c, CB)
        th = jnp.tanh(mm(feat_ref[0], wc_ref[:, own]) + cb_ref[:, own])
        th_ref[0, :, own] = th
        g = (1.0 + th) * (lanes(mult_ref, CB) * isp)
        xs = xs_ref[0, :, own].astype(F32)
        y = jnp.concatenate([(g * xs[:f]).astype(BF), (g * xs[f:]).astype(BF)], axis=0)
        filt = mm(wt_ref[...], y)
        filt_ref[0, :, own] = filt.astype(BF)
        mixed_ref[0, :, own] = (q_s[:, own] * filt).astype(BF)


def whole(shape):
    return pl.BlockSpec(shape, lambda *_: (0,) * len(shape), pipeline_mode=pl.Buffered(1))


def per_slot(shape):
    return pl.BlockSpec((1,) + shape, lambda s, *_: (s,) + (0,) * len(shape))


def mix_forward(isp, xs, g1, w_in, st, ct, w_cond, cb, table, table_t, m1, m2, mult):
    _, t, d = xs.shape
    f2 = table.shape[0]
    f = f2 // 2
    return pl.pallas_call(
        fwd_kernel,
        name="mix_forward",
        grid=(2,),
        out_shape=(
            jax.ShapeDtypeStruct((2, t, 3 * d), BF),
            jax.ShapeDtypeStruct((2, t, d), BF),
            jax.ShapeDtypeStruct((2, t, d), BF),
            jax.ShapeDtypeStruct((2, f2, d), BF),
            jax.ShapeDtypeStruct((2, f2, d), BF),
            jax.ShapeDtypeStruct((2, f, d), F32),
            jax.ShapeDtypeStruct((2, f, d), BF),
        ),
        in_specs=[
            pl.BlockSpec(memory_space=pltpu.SMEM),
            per_slot((t, d)),
            whole((1, d)),
            whole((d, 3 * d)),
            whole((3, 3 * d)),
            whole((3, d)),
            whole((d, d)),
            whole((1, d)),
            whole((f2, t)),
            whole((t, f2)),
            whole((t, 128)),
            whole((t, 128)),
            whole((f, 128)),
        ],
        out_specs=(
            per_slot((t, 3 * d)),
            per_slot((t, d)),
            per_slot((t, d)),
            per_slot((f2, d)),
            per_slot((f2, d)),
            per_slot((f, d)),
            per_slot((f, d)),
        ),
        scratch_shapes=[pltpu.VMEM((t, d), BF), pltpu.VMEM((t, d), F32)],
        compiler_params=pltpu.CompilerParams(vmem_limit_bytes=VMEM_LIMIT),
    )(isp, xs, g1, w_in, st, ct, w_cond, cb, table, table_t, m1, m2, mult)


def add_into(dst, src):
    dst[...] = (dst[...].astype(F32) + src[...].astype(F32)).astype(dst.dtype)


def back_kernel(side, *refs):
    (
        isp_ref, mixed_h, xs_h, cot_h, wo_h, g2_ref, wg_h, wu_h, wd_h,
        proj_h, filt_h, ss_h, cs_h, th_h, feat_h,
        st_ref, ct_ref, wc_h, tab_h, tabt_h, m1_ref, m2_ref, mult_ref, g1_ref, win_h,
        lay6_h, gtok6_h, odg_h, odu_h, odd_h, ow_h, small_out,
        a_s, b_s, u_s, r_s, n2_s, n2t_s, cot_s, mix_s, gmix_s, gm_s,
        act_s, gg_s, gu_s, wcol_s, wd_s, wo_s, wc_s, tab_s, tabt_s,
        sbg_s, sbu_s, sbd_s, cg_s, cu_s, cd_s, g1g_s, g1u_s, g1d_s, g2g_s, g2u_s, g2d_s,
        g3g_s, g3u_s, g3d_s,
        proj_s, filt_s, ss_s, cs_s, th_s, feat_s, gpre_s, gprem_s,
        c2_s, own2_s, g12_s, g22_s, g32_s, small_s, sgot_s, ssum_s,
        load_sem, w_sem, send_sem, recv_sem, local_sem,
    ) = refs
    n, d = n2_s.shape
    t = gm_s.shape[1]
    f = th_s.shape[0]
    isp = isp_ref[0]
    fc = gg_s.shape[1]
    quarter = d // 4
    step48 = d // 16

    dp, me = lax.axis_index("dp"), lax.axis_index("seq")
    core = lax.rem(dp, 2)
    x = lax.rem(lax.rem(dp // 2, side), 2)
    y = lax.rem(dp // (2 * side), 2)
    at_core = (dp + 1 - 2 * core, me)
    at_x = (dp + 2 - 4 * x, me)
    at_y = (dp + 2 * side - 4 * side * y, me)
    at_xy = (dp + 2 - 4 * x + 2 * side - 4 * side * y, me)
    at_z = [(dp, lax.rem(me + k, 4)) for k in range(1, 4)]
    half = lax.rem(me, 2)
    at_pair = (dp, me + 1 - 2 * half)
    own = core * 4 + x * 2 + y

    row_moves = lambda src, dst: [
        (src.at[0], dst.at[pl.ds(0, t)]),
        (src.at[1, pl.ds(pl.multiple_of(half * RB, RB), RB)], dst.at[pl.ds(t, RB)]),
    ]
    moves = (
        row_moves(mixed_h, mix_s)
        + row_moves(xs_h, gmix_s)
        + [(wo_h, wo_s), (cot_h, cot_s)]
        + [(tab_h, tab_s), (tabt_h, tabt_s), (wc_h, wc_s), (proj_h, proj_s)]
    )
    loads = [
        pltpu.make_async_copy(s, e, load_sem.at[j]) for j, (s, e) in enumerate(moves)
    ]
    slot_moves = [(filt_h, filt_s), (ss_h, ss_s), (th_h, th_s), (cs_h, cs_s), (feat_h, feat_s)]
    slot_load = lambda slot, j: pltpu.make_async_copy(
        slot_moves[j][0].at[slot], slot_moves[j][1], load_sem.at[len(moves) + j]
    )

    def chunk_of(s):
        if isinstance(s, int):
            return 2 * s + 1 - core if s < 4 else 2 * (s - 4) + core
        return jnp.where(s < 4, 2 * s + 1 - core, 2 * (s - 4) + core)

    def weights(s):
        cols = pl.ds(pl.multiple_of(chunk_of(s) * fc, 128), fc)
        b = s % 2 if isinstance(s, int) else lax.rem(s, 2)
        return [
            pltpu.make_async_copy(wg_h.at[:, cols], wcol_s.at[b], w_sem.at[0, b]),
            pltpu.make_async_copy(wu_h.at[:, cols], wcol_s.at[2 + b], w_sem.at[1, b]),
            pltpu.make_async_copy(wd_h.at[cols, :], wd_s.at[b], w_sem.at[2, b]),
        ]

    def win_col(j):
        return 3 * (1 - core) + j if j < 3 else 3 * core + j - 3

    def win_load(j):
        cols = pl.ds(pl.multiple_of(win_col(j) * fc, 128), fc)
        return pltpu.make_async_copy(win_h.at[:, cols], wcol_s.at[j % 4], w_sem.at[3, j % 4])

    for c in loads[:6]:
        c.start()
    for c in weights(0):
        c.start()
    for c in loads[6:]:
        c.start()
    for j in range(5):
        slot_load(0, j).start()

    barrier = pltpu.get_barrier_semaphore()
    everyone = [at_core, at_x, at_y, at_xy] + at_z
    for peer in everyone:
        pl.semaphore_signal(barrier, inc=1, device_id=peer, device_id_type=MESH)
    pl.semaphore_wait(barrier, len(everyone))

    def remote(src, dst, peer, j):
        return pltpu.make_async_remote_copy(
            src_ref=src,
            dst_ref=dst,
            send_sem=send_sem.at[j],
            recv_sem=recv_sem.at[j],
            device_id=peer,
            device_id_type=MESH,
        )

    def each(copies, what):
        for c in copies:
            getattr(c, what)()

    C, X1, X2, Z, G, GC = 0, 12, 36, 48, 57, 66
    C2, X12, X22, Z2, G2, GC2 = 69, 74, 86, 90, 93, 96
    LAY, GTOK, PAIR, SMALL = 97, 103, 109, 110

    def core_copies(s):
        pairs = ((sbg_s, cg_s), (sbu_s, cu_s), (sbd_s, cd_s))
        return [remote(a, b.at[s], at_core, C + 4 * j + s) for j, (a, b) in enumerate(pairs)]

    each(loads[:6], "wait")
    for i in range(n // RB):
        rows = slice(i * RB, (i + 1) * RB)
        hid = gmix_s[rows, :].astype(F32) + mm(mix_s[rows, :], wo_s[...])
        a_s[rows, :] = hid
        u, r = unit_rows(hid)
        u_s[rows, :] = u
        r_s[rows, :] = jnp.broadcast_to(r, (RB, 128))
        n2 = u * g2_ref[...]
        n2_s[rows, :] = n2.astype(BF)
        n2t_s[:, rows] = n2.T.astype(BF)
    b_s[...] = jnp.zeros_like(b_s)

    triples = ((cg_s, g1g_s, g2g_s, g3g_s), (cu_s, g1u_s, g2u_s, g3u_s), (cd_s, g1d_s, g2d_s, g3d_s))

    def x1_sem(j, q, i):
        return X1 + 8 * j + 2 * q + i

    def first_stage(i):
        a, b = i // 2, lax.rem(i, 2)
        for j in range(2):
            held, got = triples[j][:2]
            for q in range(4):
                if q % 2 == 0:
                    copy = remote(held.at[i, q], got.at[q, b], at_x, x1_sem(j, q, b))
                    pl.when(a != x)(copy.start)
                else:
                    copy = remote(held.at[i, q], got.at[q, a], at_y, x1_sem(j, q, a))
                    pl.when(b != y)(copy.start)

        @pl.when(b == 0)
        def _():
            for e in range(2):
                remote(cd_s.at[i, 2 - 2 * x + e], g1d_s.at[i, e], at_x, x1_sem(2, i, e)).start()

        @pl.when(b == 1)
        def _():
            for e in range(2):
                remote(cd_s.at[i, 2 * e + 1 - y], g1d_s.at[i, e], at_y, x1_sem(2, i, e)).start()

    @pl.loop(0, 8)
    def _(s):
        b = lax.rem(s, 2)
        each(weights(s), "wait")

        @pl.when(s < 7)
        def _():
            each(weights(s + 1), "start")

        @pl.loop(0, n // RB)
        def _(i):
            rows = pl.ds(pl.multiple_of(i * RB, RB), RB)
            n2 = n2_s[rows, :]
            pre = mm(n2, wcol_s[b])
            lin = mm(n2, wcol_s[2 + b])
            g_act = mm_nt(cot_s[rows, :], wd_s[b])
            sg = 1.0 / (1.0 + jnp.exp(-pre))
            silu = pre * sg
            act = (silu * lin).astype(BF)
            act_s[rows, :] = act
            g_up = (g_act * silu).astype(BF)
            gu_s[rows, :] = g_up
            g_gate = (g_act * lin * sg * (1.0 + pre * (1.0 - sg))).astype(BF)
            gg_s[rows, :] = g_gate
            a_s[rows, :] += mm(act, wd_s[b])
            b_s[rows, :] += mm_nt(g_gate, wcol_s[b]) + mm_nt(g_up, wcol_s[2 + b])

        @pl.when((s > 0) & (s < 5))
        def _():
            each(core_copies(s - 1), "wait_send")

        @pl.when(s >= 4)
        def _():
            each(core_copies(s - 4), "wait_recv")

        @pl.loop(0, 4)
        def _(q):
            lhs = n2t_s[pl.ds(pl.multiple_of(q * quarter, quarter), quarter), :]
            dg = mm(lhs, gg_s[...])
            du = mm(lhs, gu_s[...])

            @pl.when(s < 4)
            def _():
                sbg_s[q] = dg.astype(BF)
                sbu_s[q] = du.astype(BF)

            @pl.when(s >= 4)
            def _():
                cg_s[s - 4, q] = (cg_s[s - 4, q].astype(F32) + dg).astype(BF)
                cu_s[s - 4, q] = (cu_s[s - 4, q].astype(F32) + du).astype(BF)

        dd = mm_tn(act_s[...], cot_s[...])
        step = fc // 4

        @pl.when(s < 4)
        def _():
            for p in range(4):
                sbd_s[p] = dd[p * step : (p + 1) * step].astype(BF)
            each(core_copies(s), "start")

        @pl.when(s >= 4)
        def _():
            for p in range(4):
                cd_s[s - 4, p] = (
                    cd_s[s - 4, p].astype(F32) + dd[p * step : (p + 1) * step]
                ).astype(BF)
            first_stage(s - 4)

    for j in range(4):
        win_load(j).start()
    small_s[...] = jnp.zeros_like(small_s)
    for i in range(n // RB):
        rows = slice(i * RB, (i + 1) * RB)
        n2_s[rows, :] = a_s[rows, :].astype(BF)
        g, u = b_s[rows, :], u_s[rows, :]
        small_s[14:15, :] += jnp.sum(g * u, axis=0, keepdims=True)
        gh = cot_s[rows, :].astype(F32) + unit_back(g, u, r_s[rows, 0:1], g2_ref[...])
        gmix_s[rows, :] = gh.astype(BF)

    x_loads = [
        pltpu.make_async_copy(a, b, load_sem.at[15 + j])
        for j, (a, b) in enumerate(row_moves(xs_h, cot_s))
    ]
    each(x_loads, "start")
    half_at = pl.ds(pl.multiple_of(half * RB, RB), RB)
    gm_s[1, half_at, :] = mm_nt(gmix_s[t:, :], wo_s[...]).astype(BF)
    pair_copy = remote(gm_s.at[1, half_at], gm_s.at[1, half_at], at_pair, PAIR)
    pair_copy.start()

    rows128 = lay6_h.shape[1]
    peers = [lax.rem(me + k, 4) for k in range(4)]
    sources = [lax.rem(me + 4 - k, 4) for k in range(4)]
    sends_half = [half == p // 2 for p in peers]
    gets_half = [lax.rem(s, 2) == me // 2 for s in sources]

    def home(buf, out, base, k):
        at = pl.ds(pl.multiple_of(peers[k] * rows128, rows128), rows128)
        at2 = pl.ds(pl.multiple_of(t + lax.rem(peers[k], 2) * rows128, rows128), rows128)
        slots = (me, 4 + me // 2)
        if k == 0:
            j = 0 if base == LAY else 2
            return [
                pltpu.make_async_copy(buf.at[at], out.at[slots[0]], local_sem.at[j]),
                pltpu.make_async_copy(buf.at[at2], out.at[slots[1]], local_sem.at[j + 1]),
            ]
        return [
            remote(buf.at[at], out.at[slots[0]], at_z[k - 1], base + 2 * (k - 1)),
            remote(buf.at[at2], out.at[slots[1]], at_z[k - 1], base + 2 * (k - 1) + 1),
        ]

    def home_start(buf, out, base):
        for k in range(4):
            full, part = home(buf, out, base, k)
            full.start()
            pl.when(sends_half[k])(part.start)

    def home_wait(buf, out, base):
        for k in range(4):
            full, part = home(buf, out, base, k)
            full.wait()
            if k == 0:
                pl.when(sends_half[0])(part.wait)
            else:
                pl.when(sends_half[k])(part.wait_send)
                pl.when(gets_half[k])(part.wait_recv)

    home_start(n2_s, lay6_h, LAY)

    for i in range(t // RB):
        rows = slice(i * RB, (i + 1) * RB)
        gm_s[0, rows, :] = mm_nt(gmix_s[rows, :], wo_s[...]).astype(BF)

    def out_half(which):
        cols = pl.ds(pl.multiple_of(which * fc, 128), fc)
        return mm_tn(mix_s[...], gmix_s[:, cols])

    def put_quarters(dst, value):
        for q in range(4):
            dst[q] = value[q * quarter : (q + 1) * quarter].astype(BF)

    def second_core(c, buf):
        return remote(buf, c2_s.at[c], at_core, C2 + c)

    put_quarters(sbg_s, out_half(1 - core))
    second_core(0, sbg_s).start()
    put_quarters(own2_s.at[0], out_half(core))

    def stage_x1_end():
        for j, (held, got, got2, _) in enumerate(triples):
            for q in range(4):
                for i in range(2):
                    remote(got.at[q, i], got.at[q, i], at_x, x1_sem(j, q, i)).wait()

        @pl.loop(0, 4)
        def _(i):
            q, e = 2 * (i // 2), lax.rem(i, 2)
            for held, got, _, _ in triples[:2]:
                add_into(got.at[q, e], held.at[2 * x + e, q])
                add_into(got.at[q + 1, e], held.at[2 * e + y, q + 1])
            add_into(g1d_s.at[q, e], cd_s.at[q, 2 * x + e])
            add_into(g1d_s.at[q + 1, e], cd_s.at[q + 1, 2 * e + y])

    def x2_copies():
        out = []
        for j, (_, got, got2, _) in enumerate(triples):
            for q in range(4):
                if q % 2 == 0:
                    out.append(remote(got.at[q, 1 - y], got2.at[q], at_y, X2 + 4 * j + q))
                else:
                    out.append(remote(got.at[q, 1 - x], got2.at[q], at_x, X2 + 4 * j + q))
        return out

    def stage_x2_end():
        each(x2_copies(), "wait")

        @pl.loop(0, 2)
        def _(i):
            for _, got, got2, _ in triples:
                add_into(got2.at[2 * i], got.at[2 * i, y])
                add_into(got2.at[2 * i + 1], got.at[2 * i + 1, x])

    def z_copies():
        return [
            remote(got2.at[peers[k]], got3.at[k - 1], at_z[k - 1], Z + 3 * j + k - 1)
            for j, (_, _, got2, got3) in enumerate(triples)
            for k in range(1, 4)
        ]

    def stage_z_end():
        each(z_copies(), "wait")
        for _, _, got2, got3 in triples:
            total = got2[me].astype(F32)
            for k in range(3):
                total += got3[k].astype(F32)
            got2[me] = total.astype(BF)

    outs = (odg_h, odu_h, odd_h)

    def gather_copies():
        return [
            remote(got2.at[me], out.at[own], peer, G + 3 * j + k)
            for j, ((_, _, got2, _), out) in enumerate(zip(triples, outs))
            for k, peer in enumerate((at_x, at_y, at_xy))
        ]

    def gather_local():
        return [
            pltpu.make_async_copy(tr[2].at[me], out.at[own], local_sem.at[4 + j])
            for j, (tr, out) in enumerate(zip(triples, outs))
        ]

    here = pl.ds(4 * core, 4)

    def gather_core():
        return [remote(out.at[here], out.at[here], at_core, GC + j) for j, out in enumerate(outs)]

    each(loads[6:], "wait")

    @pl.loop(0, 2)
    def _(slot):
        share = jnp.where(slot == 0, 1.0, 0.5)
        for j in range(3):
            slot_load(slot, j).wait()
        pl.when(slot == 1)(pair_copy.wait)

        @pl.loop(0, d // CB)
        def _(c):
            m1, m2 = lanes(m1_ref, CB), lanes(m2_ref, CB)
            mult = lanes(mult_ref, CB)
            cols = cols_at(c, CB)
            query = conv(proj_s[slot, :, cols].astype(F32), st_ref[:, cols], m1, m2)
            gm = gm_s[slot, :, cols].astype(F32)
            a_s[0:t, cols] = gm * filt_s[:, cols].astype(F32)
            spec = mm(tab_s[...], (gm * query).astype(BF)) * isp
            ss = ss_s[:, cols].astype(F32)
            th = th_s[:, cols]
            g_gain = spec[:f] * ss[:f] + spec[f:] * ss[f:]
            g_pre = (g_gain * (1.0 - th * th)).astype(BF)
            gpre_s[:, cols] = g_pre
            weighted = g_pre.astype(F32) * mult
            gprem_s[:, cols] = weighted.astype(BF)
            small_s[13:14, cols] += share * jnp.sum(weighted, axis=0, keepdims=True)
            g = (1.0 + th) * mult
            yy = jnp.concatenate(
                [(g * spec[:f]).astype(BF), (g * spec[f:]).astype(BF)], axis=0
            )
            b_s[0:t, cols] = mm(tabt_s[...], yy)

        @pl.when(slot == 0)
        def _():
            for j in range(3):
                slot_load(1, j).start()
            stage_x1_end()
            each(x2_copies(), "start")

        for j in range(3, 5):
            slot_load(slot, j).wait()

        @pl.loop(0, d // CB)
        def _(c):
            m1, m2 = lanes(m1_ref, CB), lanes(m2_ref, CB)
            cols = cols_at(c, CB)
            g_feat = mm_nt(gpre_s[...], wc_s[cols, :])
            xc = cs_s[:, cols].astype(F32)
            power = (xc[:f] * xc[:f] + xc[f:] * xc[f:]) * isp
            g_pow = g_feat / (1.0 + power) * (lanes(mult_ref, CB) * (2.0 * isp))
            yy = jnp.concatenate(
                [(g_pow * xc[:f]).astype(BF), (g_pow * xc[f:]).astype(BF)], axis=0
            )
            g_cond = mm(tabt_s[...], yy)
            dwc = share * mm_tn(feat_s[:, cols], gprem_s[...])

            @pl.when(slot == 0)
            def _():
                u_s[cols, :] = dwc

            @pl.when(slot == 1)
            def _():
                u_s[cols, :] += dwc

            def finish(part, g_conv, p):
                at = cols_at(c, CB, part * d)
                sums = share * tap_sums(g_conv, p, m1, m2)
                for j in range(3):
                    row = 1 + 3 * j + part
                    small_s[row : row + 1, cols] += sums[j : j + 1]
                proj_s[slot, :, at] = conv_back(g_conv, st_ref[:, at], m1, m2).astype(BF)

            finish(0, a_s[0:t, cols], proj_s[slot, :, cols].astype(F32))
            key_cols, value_cols = cols_at(c, CB, d), cols_at(c, CB, 2 * d)
            p_value = proj_s[slot, :, value_cols].astype(F32)
            value = conv(p_value, st_ref[:, value_cols], m1, m2).astype(BF).astype(F32)
            g_sig = b_s[0:t, cols]
            p_key = proj_s[slot, :, key_cols].astype(F32)
            key = conv(p_key, st_ref[:, key_cols], m1, m2)
            finish(1, g_sig * value, p_key)
            sums = share * tap_sums(g_cond, value, m1, m2)
            for j in range(3):
                small_s[10 + j : 11 + j, cols] += sums[j : j + 1]
            finish(2, g_sig * key + conv_back(g_cond, ct_ref[:, cols], m1, m2), p_value)

        @pl.when(slot == 0)
        def _():
            for j in range(3, 5):
                slot_load(1, j).start()
            stage_x2_end()
            each(z_copies(), "start")

    def cond_half(dst, which):
        cols = pl.ds(pl.multiple_of(which * fc, 128), fc)
        for q in range(4):
            dst[q] = u_s[q * quarter : (q + 1) * quarter, cols].astype(BF)

    cond_half(sbu_s, 1 - core)
    second_core(1, sbu_s).start()
    cond_half(own2_s.at[1], core)

    each(x_loads, "wait")
    for i in range(n // RB):
        rows = slice(i * RB, (i + 1) * RB)
        u, r = unit_rows(cot_s[rows, :].astype(F32))
        a_s[rows, :] = u
        r_s[rows, :] = jnp.broadcast_to(r, (RB, 128))
        n2t_s[:, rows] = (u * g1_ref[...]).T.astype(BF)
    b_s[...] = jnp.zeros_like(b_s)

    def proj_step(j, put):
        cols = pl.ds(pl.multiple_of(win_col(j) * fc, 128), fc)
        win_load(j).wait()
        w = wcol_s.at[j % 4]
        blocks = [
            proj_s.at[0, pl.ds(0, RB), cols],
            proj_s.at[0, pl.ds(RB, RB), cols],
            proj_s.at[1, half_at, cols],
        ]
        for i, gp in enumerate(blocks):
            b_s[i * RB : (i + 1) * RB, :] += mm_nt(gp[...], w[...])

        @pl.loop(0, 4)
        def _(q):
            rows = pl.ds(pl.multiple_of(q * quarter, quarter), quarter)
            dw = jnp.zeros((quarter, fc), F32)
            for i, gp in enumerate(blocks):
                dw += mm(n2t_s[rows, i * RB : (i + 1) * RB], gp[...])
            put(q, dw)

        if j < 2:
            win_load(j + 4).start()

    second_core(0, sbg_s).wait_send()
    second_core(1, sbu_s).wait_send()

    def put_g(q, dw):
        sbg_s[q] = dw.astype(BF)

    def put_u(q, dw):
        sbu_s[q] = dw.astype(BF)

    def put_own(q, dw):
        own2_s[2, q] = dw.astype(BF)

    proj_step(0, put_g)
    second_core(2, sbg_s).start()
    proj_step(1, put_u)
    second_core(3, sbu_s).start()
    proj_step(2, put_own)
    second_core(4, own2_s.at[2]).start()

    stage_z_end()
    each(gather_copies(), "start")
    each(gather_local(), "start")

    def x12_copies(first, count, base):
        cs = pl.ds(first, count)
        out = []
        for q in range(4):
            if q % 2 == 0:
                rows = pl.ds(pl.multiple_of((2 - 2 * x) * step48, step48), 2 * step48)
                out.append(
                    remote(c2_s.at[cs, q, rows], g12_s.at[cs, q], at_x, base + q)
                )
            else:
                for e in range(2):
                    rows = pl.ds(pl.multiple_of((2 * e + 1 - y) * step48, step48), step48)
                    to = pl.ds(e * step48, step48)
                    out.append(
                        remote(c2_s.at[cs, q, rows], g12_s.at[cs, q, to], at_y, base + (q if e == 0 else 4 + q // 2))
                    )
        return out

    for c in range(2):
        remote(c2_s.at[c], c2_s.at[c], at_core, C2 + c).wait_recv()

        @pl.loop(0, 4)
        def _(q, c=c):
            add_into(c2_s.at[c, q], own2_s.at[c, q])

    each(x12_copies(0, 2, X12), "start")

    def own_put(c):
        def put(q, dw):
            c2_s[c, q] = (c2_s[c, q].astype(F32) + dw).astype(BF)

        return put

    for c in range(3):
        remote(c2_s.at[2 + c], c2_s.at[2 + c], at_core, C2 + 2 + c).wait_recv()
        proj_step(3 + c, own_put(2 + c))
    each(x12_copies(2, 3, X12 + 6), "start")

    each(gather_copies(), "wait")
    each(gather_local(), "wait")
    each(gather_core(), "start")

    for i in range(n // RB):
        rows = slice(i * RB, (i + 1) * RB)
        g, u = b_s[rows, :], a_s[rows, :]
        small_s[0:1, :] += jnp.sum(g * u, axis=0, keepdims=True)
        mix_s[rows, :] = (
            gmix_s[rows, :].astype(F32) + unit_back(g, u, r_s[rows, 0:1], g1_ref[...])
        ).astype(BF)
    home_start(mix_s, gtok6_h, GTOK)

    small_c = remote(small_s, sgot_s.at[0], at_core, SMALL)
    small_c.start()
    each([second_core(2, sbg_s), second_core(3, sbu_s), second_core(4, own2_s.at[2])], "wait_send")

    each(x12_copies(0, 2, X12), "wait")
    each(x12_copies(2, 3, X12 + 6), "wait")

    @pl.loop(0, 5)
    def _(c):
        for q in range(4):
            if q % 2 == 0:
                rows = pl.ds(pl.multiple_of(2 * x * step48, step48), 2 * step48)
                add_into(g12_s.at[c, q], c2_s.at[c, q, rows])
            else:
                for e in range(2):
                    rows = pl.ds(pl.multiple_of((2 * e + y) * step48, step48), step48)
                    add_into(g12_s.at[c, q, pl.ds(e * step48, step48)], c2_s.at[c, q, rows])

    def x22_copies():
        out = []
        for q in range(4):
            e, peer = (1 - y, at_y) if q % 2 == 0 else (1 - x, at_x)
            rows = pl.ds(pl.multiple_of(e * step48, step48), step48)
            out.append(remote(g12_s.at[:, q, rows], g22_s.at[q], peer, X22 + q))
        return out

    each(x22_copies(), "start")
    small_c.wait()
    ssum_s[0] = small_s[...] + sgot_s[0]
    small_x = remote(ssum_s.at[0], sgot_s.at[1], at_x, SMALL + 1)
    small_x.start()
    each(x22_copies(), "wait")

    @pl.loop(0, 5)
    def _(c):
        for q in range(4):
            e = y if q % 2 == 0 else x
            rows = pl.ds(pl.multiple_of(e * step48, step48), step48)
            add_into(g22_s.at[q, c], g12_s.at[c, q, rows])

    z2_copies = [
        remote(g22_s.at[peers[k]], g32_s.at[k - 1], at_z[k - 1], Z2 + k - 1) for k in range(1, 4)
    ]
    each(z2_copies, "start")
    small_x.wait()
    ssum_s[1] = ssum_s[0] + sgot_s[1]
    small_y = remote(ssum_s.at[1], sgot_s.at[2], at_y, SMALL + 2)
    small_y.start()
    small_y.wait()
    ssum_s[2] = ssum_s[1] + sgot_s[2]
    small_z = [
        remote(ssum_s.at[2], sgot_s.at[2 + k], at_z[k - 1], SMALL + 2 + k) for k in range(1, 4)
    ]
    each(small_z, "start")
    each(gather_core(), "wait")
    each(z2_copies, "wait")

    @pl.loop(0, 5)
    def _(c):
        total = g22_s[me, c].astype(F32)
        for k in range(3):
            total += g32_s[k, c].astype(F32)
        g22_s[me, c] = total.astype(BF)

    g2_copies = [
        remote(g22_s.at[me], ow_h.at[own], peer, G2 + k)
        for k, peer in enumerate((at_x, at_y, at_xy))
    ]
    g2_local = pltpu.make_async_copy(g22_s.at[me], ow_h.at[own], local_sem.at[7])
    each(g2_copies, "start")
    g2_local.start()
    each(small_z, "wait")
    small_out[...] = ssum_s[2] + sgot_s[3] + sgot_s[4] + sgot_s[5]
    each(g2_copies, "wait")
    g2_local.wait()
    last = remote(ow_h.at[here], ow_h.at[here], at_core, GC2)
    last.start()
    home_wait(n2_s, lay6_h, LAY)
    home_wait(mix_s, gtok6_h, GTOK)
    last.wait()


def back(
    side, slots, isp, mixed, xs, cot, w_out, g2, w_gate, w_up, w_down,
    proj, filt, ss, cs, th, feat, st, ct, w_cond, table, table_t, m1, m2, mult, g1, w_in,
):
    n, d = cot.shape
    t = xs.shape[1]
    f2 = table.shape[0]
    f = f2 // 2
    hbm = pl.BlockSpec(memory_space=pl.ANY)
    vm = pl.BlockSpec(memory_space=pltpu.VMEM)
    smem = pl.BlockSpec(memory_space=pltpu.SMEM)
    b = lambda *s: pltpu.VMEM(s, BF)
    g = lambda *s: pltpu.VMEM(s, F32)
    q4, fd = d // 4, FC // 4
    return pl.pallas_call(
        functools.partial(back_kernel, side),
        name="back",
        out_shape=(
            jax.ShapeDtypeStruct((slots, t // 4, d), BF),
            jax.ShapeDtypeStruct((slots, t // 4, d), BF),
            jax.ShapeDtypeStruct((8, q4, FC), BF),
            jax.ShapeDtypeStruct((8, q4, FC), BF),
            jax.ShapeDtypeStruct((8, fd, d), BF),
            jax.ShapeDtypeStruct((8, 5, d // 16, FC), BF),
            jax.ShapeDtypeStruct((16, d), F32),
        ),
        in_specs=[smem, hbm, hbm, hbm, hbm, vm] + [hbm] * 9 + [vm, vm, hbm, hbm, hbm]
        + [vm, vm, vm, vm, hbm],
        out_specs=(hbm,) * 6 + (vm,),
        scratch_shapes=[
            g(n, d), g(n, d), g(n, d), g(n, 128),
            b(n, d), b(d, n), b(n, d), b(n, d), b(n, d), b(2, t, d),
            b(n, FC), b(n, FC), b(n, FC), b(4, d, FC), b(2, FC, d), b(d, d), b(d, d),
            b(f2, t), b(t, f2),
            b(4, q4, FC), b(4, q4, FC), b(4, fd, d),
            b(4, 4, q4, FC), b(4, 4, q4, FC), b(4, 4, fd, d),
            b(4, 2, q4, FC), b(4, 2, q4, FC), b(4, 2, fd, d),
            b(4, q4, FC), b(4, q4, FC), b(4, fd, d),
            b(3, q4, FC), b(3, q4, FC), b(3, fd, d),
            b(2, t, 3 * d), b(t, d), b(f2, d), b(f2, d), g(f, d), b(f, d), b(f, d), b(f, d),
            b(5, 4, q4, FC), b(3, 4, q4, FC), b(5, 4, d // 8, FC), b(4, 5, d // 16, FC),
            b(3, 5, d // 16, FC),
            g(16, d), g(6, 16, d), g(3, 16, d),
            pltpu.SemaphoreType.DMA((17,)),
            pltpu.SemaphoreType.DMA((4, 4)),
            pltpu.SemaphoreType.DMA((116,)),
            pltpu.SemaphoreType.DMA((116,)),
            pltpu.SemaphoreType.DMA((8,)),
        ],
        compiler_params=pltpu.CompilerParams(
            collective_id=1, has_side_effects=True, vmem_limit_bytes=65400 * 1024
        ),
    )(
        isp, mixed, xs, cot, w_out, g2, w_gate, w_up, w_down, proj, filt, ss, cs, th, feat,
        st, ct, w_cond, table, table_t, m1, m2, mult, g1, w_in,
    )


def on_device(
    tokens, kind, ln1_gain, w_in, short_taps, cond_taps, w_cond, cond_bias, w_out, ln2_gain,
    w_gate, w_up, w_down, cotangent,
):
    _, rows, slots, d = tokens.shape
    n = lax.axis_size("seq")
    dp_count = lax.axis_size("dp")
    rank = lax.axis_index("seq")
    span_long = rows * n
    is_long = kind[0] == 1

    freqs = -(-max(span_long // 2 + 1, n * (rows // 2 + 1)) // 16) * 16
    table, table_t, mult = wave_tables(is_long, rows, span_long, freqs)
    isp = jnp.where(is_long, 1.0 / span_long, 1.0 / rows).astype(F32).reshape(1)
    place = jnp.arange(span_long, dtype=jnp.int32)
    offset = jnp.where(is_long, place, place % rows)[:, None]
    m1 = jnp.broadcast_to((offset >= 1).astype(F32), (span_long, 128))
    m2 = jnp.broadcast_to((offset >= 2).astype(F32), (span_long, 128))

    tok6 = jnp.transpose(tokens[0], (1, 0, 2))
    cot6 = jnp.transpose(cotangent[0], (1, 0, 2))
    xs, cot = reshard_in(tok6, cot6)

    g1, g2 = ln1_gain.reshape(1, d), ln2_gain.reshape(1, d)
    proj, mixed, filt, sig_spec, cond_spec, th, feat = mix_forward(
        isp, xs, g1, w_in, short_taps, cond_taps, w_cond, cond_bias.reshape(1, d),
        table, table_t, m1, m2, mult,
    )
    side = math.isqrt(dp_count // 2)
    lay6, gtok6, dg, du, dd, dw, small = back(
        side, slots, isp, mixed, xs, cot, w_out, g2, w_gate, w_up, w_down,
        proj, filt, sig_spec, cond_spec, th, feat, short_taps, cond_taps, w_cond,
        table, table_t, m1, m2, mult, g1, w_in,
    )
    layer_out = jnp.transpose(lay6, (1, 0, 2))[None]
    grad_tokens = jnp.transpose(gtok6, (1, 0, 2))[None]

    sums = (dg, du, dd, dw)
    if dp_count > 8:
        groups = [
            [
                (y * side + x) * 2 + core
                for y in range(y0, side, 2)
                for x in range(x0, side, 2)
            ]
            for y0 in range(2)
            for x0 in range(2)
            for core in range(2)
        ]
        sums = [lax.psum(a.astype(F32), "dp", axis_index_groups=groups) for a in sums]
        small = lax.psum(small, "dp", axis_index_groups=groups)
    dg, du, dd, dw = (a.astype(F32) for a in sums)
    by_chunk = lambda a: jnp.transpose(
        a.reshape((2, 4) + a.shape[1:]), (2, 1, 0, 3)
    ).reshape(a.shape[1], -1)
    dw = dw.reshape((2, 4) + dw.shape[1:])
    by_core = lambda a: jnp.transpose(a, (1, 3, 0, 2, 4)).reshape(d // n, -1)
    part = lambda a, width: lax.dynamic_slice_in_dim(a, rank * width, width, a.ndim - 1)
    return (
        layer_out,
        grad_tokens,
        part(small[0], d // n),
        by_core(dw[:, :, 2:]),
        part(small[1:10].reshape(3, 3 * d), 3 * d // n),
        part(small[10:13], d // n),
        by_core(dw[:, :, 1:2]),
        part(small[13], d // n),
        by_core(dw[:, :, 0:1]),
        part(small[14], d // n),
        by_chunk(dg),
        by_chunk(du),
        dd.reshape(-1, d),
    )


def solution(mesh):
    rows = P("dp", "seq", None, None)
    return jax.shard_map(
        on_device,
        mesh=mesh,
        in_specs=(rows, P("dp")) + (P(),) * 11 + (rows,),
        out_specs=(
            rows,
            rows,
            P("seq"),
            P("seq", None),
            P(None, "seq"),
            P(None, "seq"),
            P("seq", None),
            P("seq"),
            P("seq", None),
            P("seq"),
            P("seq", None),
            P("seq", None),
            P("seq", None),
        ),
        check_vma=False,
    )
```

```python
import functools
import math

import jax
import jax.numpy as jnp
from jax import lax
from jax.experimental import pallas as pl
from jax.experimental.pallas import tpu as pltpu
from jax.sharding import PartitionSpec as P

BF = jnp.bfloat16
F32 = jnp.float32
MESH = pl.DeviceIdType.MESH
EPS = 1e-05
CB = 256
FC = 384
RB = 256
VMEM_LIMIT = 60 * 2**20


def mm(a, b):
    return jnp.dot(a, b, preferred_element_type=F32)


def mm_nt(a, b):
    return lax.dot_general(a, b, (((1,), (1,)), ((), ())), preferred_element_type=F32)


def mm_tn(a, b):
    return lax.dot_general(a, b, (((0,), (0,)), ((), ())), preferred_element_type=F32)


def unit_rows(x):
    mean = jnp.mean(x, axis=-1, keepdims=True)
    centered = x - mean
    r = lax.rsqrt(jnp.mean(centered * centered, axis=-1, keepdims=True) + EPS)
    return centered * r, r


def unit_back(g, u, r, gain):
    e = g * gain
    return r * (
        e - jnp.mean(e, axis=-1, keepdims=True) - u * jnp.mean(e * u, axis=-1, keepdims=True)
    )


def lanes(ref, width):
    m = ref[...]
    return jnp.concatenate([m] * (width // m.shape[1]), axis=1)


def down(a, j):
    return pltpu.roll(a, j, axis=0)


def up(a, j):
    return pltpu.roll(a, a.shape[0] - j, axis=0)


def conv(a, taps, m1, m2):
    return taps[0:1] * a + taps[1:2] * (down(a, 1) * m1) + taps[2:3] * (down(a, 2) * m2)


def conv_back(g, taps, m1, m2):
    return taps[0:1] * g + taps[1:2] * up(g * m1, 1) + taps[2:3] * up(g * m2, 2)


def tap_sums(g, a, m1, m2):
    return jnp.concatenate(
        [
            jnp.sum(g * a, axis=0, keepdims=True),
            jnp.sum(g * (down(a, 1) * m1), axis=0, keepdims=True),
            jnp.sum(g * (down(a, 2) * m2), axis=0, keepdims=True),
        ],
        axis=0,
    )


def cols_at(c, width, base=0):
    return pl.ds(pl.multiple_of(base + c * width, 128), width)


def wave_tables(is_long, short, span_long, freqs):
    i = jnp.arange(freqs, dtype=jnp.int32)[:, None]
    t = jnp.arange(span_long, dtype=jnp.int32)[None, :]
    blocks, half = span_long // short, short // 2 + 1
    f_short, b_short = i % half, i // half
    phase = jnp.where(
        is_long, (i * t) % span_long, ((f_short * (t % short)) % short) * blocks
    )
    kept = jnp.where(is_long, i <= span_long // 2, (b_short < blocks) & (t // short == b_short))
    angle = phase.astype(F32) * (2.0 * math.pi / span_long)
    kept_f = kept.astype(F32)
    table = jnp.concatenate([jnp.cos(angle) * kept_f, jnp.sin(angle) * kept_f], axis=0)
    once = jnp.where(
        is_long, (i == 0) | (i == span_long // 2), (f_short == 0) | (f_short == short // 2)
    )
    used = jnp.where(is_long, i <= span_long // 2, b_short < blocks)
    mult = jnp.where(used, jnp.where(once, 1.0, 2.0), 0.0).astype(F32)
    table = table.astype(BF)
    return table, table.T, jnp.broadcast_to(mult, (freqs, 128))


def reshard_in_kernel(tok_ref, cot_ref, xs_ref, cs_ref, local_sem, send_sem, recv_sem):
    dp, me = lax.axis_index("dp"), lax.axis_index("seq")
    n = lax.axis_size("seq")
    rows = tok_ref.shape[1]
    barrier = pltpu.get_barrier_semaphore()
    for k in range(1, n):
        pl.semaphore_signal(
            barrier, inc=1, device_id=(dp, lax.rem(me + k, n)), device_id_type=MESH
        )
    pl.semaphore_wait(barrier, n - 1)
    at = pl.ds(pl.multiple_of(me * rows, rows), rows)
    half_at = pl.ds(pl.multiple_of(n * rows + lax.rem(me, 2) * rows, rows), rows)

    def copies(k, peer):
        moves = [
            (tok_ref.at[peer], xs_ref.at[0, at]),
            (tok_ref.at[n + peer // 2], xs_ref.at[1, at]),
            (cot_ref.at[peer], cs_ref.at[at]),
            (cot_ref.at[n + peer // 2], cs_ref.at[half_at]),
        ]
        if k == 0:
            return [
                pltpu.make_async_copy(s, d, local_sem.at[j]) for j, (s, d) in enumerate(moves)
            ]
        return [
            pltpu.make_async_remote_copy(
                src_ref=s,
                dst_ref=d,
                send_sem=send_sem.at[j, k],
                recv_sem=recv_sem.at[j, k],
                device_id=(dp, peer),
                device_id_type=MESH,
            )
            for j, (s, d) in enumerate(moves)
        ]

    peers = [lax.rem(me + k, n) for k in range(n)]
    sources = [lax.rem(me + n - k, n) for k in range(n)]
    sends_half = [lax.rem(p, 2) == me // 2 for p in peers]
    gets_half = [lax.rem(me, 2) == s // 2 for s in sources]
    all_copies = [copies(k, peers[k]) for k in range(n)]
    for j in range(3):
        for k in range(n):
            all_copies[k][j].start()
    for k in range(n):
        pl.when(sends_half[k])(all_copies[k][3].start)
    for j in range(3):
        for k in range(n):
            all_copies[k][j].wait()
    pl.when(sends_half[0])(all_copies[0][3].wait)
    for k in range(1, n):
        pl.when(sends_half[k])(all_copies[k][3].wait_send)
        pl.when(gets_half[k])(all_copies[k][3].wait_recv)


def reshard_in(tok, cot):
    slots, rows, d = tok.shape
    n = lax.axis_size("seq")
    any_spec = pl.BlockSpec(memory_space=pl.ANY)
    return pl.pallas_call(
        reshard_in_kernel,
        name="reshard_in",
        out_shape=(
            jax.ShapeDtypeStruct((2, n * rows, d), BF),
            jax.ShapeDtypeStruct((n * rows + n * rows // 2, d), BF),
        ),
        in_specs=[any_spec] * 2,
        out_specs=(any_spec, any_spec),
        scratch_shapes=[
            pltpu.SemaphoreType.DMA((4,)),
            pltpu.SemaphoreType.DMA((4, n)),
            pltpu.SemaphoreType.DMA((4, n)),
        ],
        compiler_params=pltpu.CompilerParams(collective_id=0, has_side_effects=True),
    )(tok, cot)


def fwd_kernel(
    isp_ref, x_ref, g1_ref, win_ref, st_ref, ct_ref, wc_ref, cb_ref, w_ref, wt_ref,
    m1_ref, m2_ref, mult_ref,
    proj_ref, mixed_ref, filt_ref, xs_ref, xc_ref, th_ref, feat_ref,
    n1_s, q_s,
):
    t, d = n1_s.shape
    f = th_ref.shape[1]
    isp = isp_ref[0]

    @pl.loop(0, t // 128)
    def _(r):
        rows = pl.ds(pl.multiple_of(r * 128, 128), 128)
        u, _ = unit_rows(x_ref[0, rows, :].astype(F32))
        n1_s[rows, :] = (u * g1_ref[...]).astype(BF)

    @pl.loop(0, d // CB)
    def _(c):
        m1, m2 = lanes(m1_ref, CB), lanes(m2_ref, CB)
        own = cols_at(c, CB)

        def part(k):
            cols = cols_at(c, CB, k * d)
            p = mm(n1_s[...], win_ref[:, cols]).astype(BF)
            proj_ref[0, :, cols] = p
            return conv(p.astype(F32), st_ref[:, cols], m1, m2)

        q_s[:, own] = part(0)
        key = part(1)
        value = part(2).astype(BF)
        value_f = value.astype(F32)
        signal = (key * value_f).astype(BF)
        xs_ref[0, :, own] = mm(w_ref[...], signal).astype(BF)
        cond = conv(value_f, ct_ref[:, own], m1, m2).astype(BF)
        xc = mm(w_ref[...], cond)
        xc_ref[0, :, own] = xc.astype(BF)
        power = (xc[:f] * xc[:f] + xc[f:] * xc[f:]) * isp
        feat_ref[0, :, own] = jnp.log1p(power).astype(BF)

    @pl.loop(0, d // CB)
    def _(c):
        own = cols_at(c, CB)
        th = jnp.tanh(mm(feat_ref[0], wc_ref[:, own]) + cb_ref[:, own])
        th_ref[0, :, own] = th
        g = (1.0 + th) * (lanes(mult_ref, CB) * isp)
        xs = xs_ref[0, :, own].astype(F32)
        y = jnp.concatenate([(g * xs[:f]).astype(BF), (g * xs[f:]).astype(BF)], axis=0)
        filt = mm(wt_ref[...], y)
        filt_ref[0, :, own] = filt.astype(BF)
        mixed_ref[0, :, own] = (q_s[:, own] * filt).astype(BF)


def whole(shape):
    return pl.BlockSpec(shape, lambda *_: (0,) * len(shape), pipeline_mode=pl.Buffered(1))


def per_slot(shape):
    return pl.BlockSpec((1,) + shape, lambda s, *_: (s,) + (0,) * len(shape))


def mix_forward(isp, xs, g1, w_in, st, ct, w_cond, cb, table, table_t, m1, m2, mult):
    _, t, d = xs.shape
    f2 = table.shape[0]
    f = f2 // 2
    return pl.pallas_call(
        fwd_kernel,
        name="mix_forward",
        grid=(2,),
        out_shape=(
            jax.ShapeDtypeStruct((2, t, 3 * d), BF),
            jax.ShapeDtypeStruct((2, t, d), BF),
            jax.ShapeDtypeStruct((2, t, d), BF),
            jax.ShapeDtypeStruct((2, f2, d), BF),
            jax.ShapeDtypeStruct((2, f2, d), BF),
            jax.ShapeDtypeStruct((2, f, d), F32),
            jax.ShapeDtypeStruct((2, f, d), BF),
        ),
        in_specs=[
            pl.BlockSpec(memory_space=pltpu.SMEM),
            per_slot((t, d)),
            whole((1, d)),
            whole((d, 3 * d)),
            whole((3, 3 * d)),
            whole((3, d)),
            whole((d, d)),
            whole((1, d)),
            whole((f2, t)),
            whole((t, f2)),
            whole((t, 128)),
            whole((t, 128)),
            whole((f, 128)),
        ],
        out_specs=(
            per_slot((t, 3 * d)),
            per_slot((t, d)),
            per_slot((t, d)),
            per_slot((f2, d)),
            per_slot((f2, d)),
            per_slot((f, d)),
            per_slot((f, d)),
        ),
        scratch_shapes=[pltpu.VMEM((t, d), BF), pltpu.VMEM((t, d), F32)],
        compiler_params=pltpu.CompilerParams(vmem_limit_bytes=VMEM_LIMIT),
    )(isp, xs, g1, w_in, st, ct, w_cond, cb, table, table_t, m1, m2, mult)


def add_into(dst, src):
    dst[...] = (dst[...].astype(F32) + src[...].astype(F32)).astype(dst.dtype)


def back_kernel(side, *refs):
    (
        isp_ref, isl_ref, mixed_h, xs_h, cot_h, wo_h, g2_ref, wg_h, wu_h, wd_h,
        proj_h, filt_h, ss_h, cs_h, th_h, feat_h,
        st_ref, ct_ref, wc_h, tab_h, tabt_h, mult_ref, g1_ref, win_h,
        lay6_h, gtok6_h, odg_h, odu_h, odd_h, owo_h, owc_h, owi_h, small_out,
        a_s, b_s, u_s, r_s, n2_s, n2t_s, cot_s, mg_s, gmix_s,
        act_s, gg_s, gu_s, w0_s, w1_s, w2_s, wo_s, wc_s, tab_s, tabt_s, m1_ref, m2_ref,
        sbg_s, sbu_s, sbd_s, cg_s, cu_s, cd_s,
        dgg_s, dgu_s, xg_s, xu_s, yg_s, yu_s, zg_s, zu_s, d1_s, d2_s, zd_s,
        proj_s, filt_s, ss_s, cs_s, th_s, feat_s, gpre_s, gprem_s,
        c2_s, raw2_s, r2_s, z2_s, cw_s, sbw_s, rw_s, zw_s, small_s, sgot_s, ssum_s,
        load_sem, w_sem, send_sem, recv_sem, local_sem,
    ) = refs
    n, d = n2_s.shape
    t = filt_s.shape[0]
    f = th_s.shape[0]
    isp = isp_ref[0]
    h = d // 2
    quarter = d // 4
    step48 = d // 16
    dr = h // 4

    dp, me = lax.axis_index("dp"), lax.axis_index("seq")
    core = lax.rem(dp, 2)
    x = lax.rem(lax.rem(dp // 2, side), 2)
    y = lax.rem(dp // (2 * side), 2)
    dp_x = dp + 2 - 4 * x
    dp_y = dp + 2 * side - 4 * side * y
    at_core, at_x, at_y = (dp + 1 - 2 * core, me), (dp_x, me), (dp_y, me)
    at_xy = (dp_x + dp_y - dp, me)
    peers = [lax.rem(me + k, 4) for k in range(4)]
    at_z = [(dp, peers[k]) for k in range(4)]
    half = lax.rem(me, 2)
    at_pair = (dp, me + 1 - 2 * half)
    half_at = pl.ds(pl.multiple_of(half * RB, RB), RB)
    xy = 2 * x + y
    diag, by_x, by_y = 3 - xy, 2 * (1 - x) + y, 2 * x + 1 - y

    def owner(s):
        if isinstance(s, int):
            return (diag, by_x, by_y, xy)[s]
        return 2 * jnp.where(s < 2, 1 - x, x) + jnp.where(lax.rem(s, 2) == 0, 1 - y, y)

    def rows_at(i, size, base=0):
        return pl.ds(pl.multiple_of(base + i * size, math.gcd(size, base) if base else size), size)

    def each(copies, what):
        for c in copies:
            getattr(c, what)()

    row_moves = lambda src, dst: [
        (src.at[0], dst.at[pl.ds(0, t)]),
        (src.at[1, half_at], dst.at[pl.ds(t, RB)]),
    ]
    moves = (
        row_moves(mixed_h, mg_s)
        + row_moves(xs_h, gmix_s)
        + [(wo_h, wo_s), (cot_h, cot_s)]
        + [(tab_h, tab_s), (tabt_h, tabt_s), (wc_h, wc_s), (proj_h, proj_s)]
    )
    loads = [pltpu.make_async_copy(s, e, load_sem.at[j]) for j, (s, e) in enumerate(moves)]
    slot_moves = [(filt_h, filt_s), (ss_h, ss_s), (th_h, th_s), (cs_h, cs_s), (feat_h, feat_s)]
    slot_load = lambda slot, j: pltpu.make_async_copy(
        slot_moves[j][0].at[slot], slot_moves[j][1], load_sem.at[10 + j]
    )
    x_loads = [
        pltpu.make_async_copy(a, b, load_sem.at[15 + j])
        for j, (a, b) in enumerate(row_moves(xs_h, cot_s))
    ]

    def weights(s):
        cols = cols_at(owner(s), d)
        return [
            pltpu.make_async_copy(wg_h.at[:, cols], w0_s, w_sem.at[0]),
            pltpu.make_async_copy(wu_h.at[:, cols], w1_s, w_sem.at[1]),
            pltpu.make_async_copy(wd_h.at[cols, :], w2_s, w_sem.at[2]),
        ]

    win_loads = [
        pltpu.make_async_copy(win_h.at[:, k * d : (k + 1) * d], w, w_sem.at[3 + k])
        for k, w in enumerate((w0_s, w1_s, w2_s))
    ]

    each(loads[:6], "start")
    each(weights(0), "start")
    each(loads[6:], "start")
    for j in range(5):
        slot_load(0, j).start()

    barrier = pltpu.get_barrier_semaphore()
    everyone = [at_core, at_x, at_y, at_xy] + at_z[1:]
    for peer in everyone:
        pl.semaphore_signal(barrier, inc=1, device_id=peer, device_id_type=MESH)
    pl.semaphore_wait(barrier, len(everyone))

    place = lax.broadcasted_iota(jnp.int32, m1_ref.shape, 0)
    short = place & (t // 4 - 1)
    place = short + isl_ref[0] * (place - short)
    m1_ref[...] = (place >= 1).astype(F32)
    m2_ref[...] = (place >= 2).astype(F32)

    def remote(src, dst, peer, j):
        return pltpu.make_async_remote_copy(
            src_ref=src,
            dst_ref=dst,
            send_sem=send_sem.at[j],
            recv_sem=recv_sem.at[j],
            device_id=peer,
            device_id_type=MESH,
        )

    C, DG, XS, YS, ZD, ZG, GA, GC, DX, DY = 0, 12, 20, 22, 24, 27, 36, 45, 130, 138
    C2, D2, XS2, YS2, Z2, GA2, GC2 = 57, 59, 67, 69, 71, 77, 83
    CW, DW, XW, YW, ZW, GW, GCW = 91, 95, 99, 100, 101, 104, 107
    LAY, GT0, GT1, PAIR, SMALL = 111, 117, 120, 123, 124

    each(loads[:6], "wait")

    @pl.loop(0, n // RB)
    def _(i):
        rows = rows_at(i, RB)
        hid = gmix_s[rows, :].astype(F32) + mm(mg_s[rows, :], wo_s[...])
        a_s[rows, :] = hid
        b_s[rows, :] = jnp.zeros_like(hid)
        u, r = unit_rows(hid)
        u_s[rows, :] = u
        r_s[rows, :] = jnp.broadcast_to(r, (RB, 128))
        n2 = u * g2_ref[...]
        n2_s[rows, :] = n2.astype(BF)
        n2t_s[:, rows] = n2.T.astype(BF)

    pairs = ((sbg_s, cg_s, dgg_s, xg_s, yg_s, zg_s), (sbu_s, cu_s, dgu_s, xu_s, yu_s, zu_s))
    rank_rows = lambda q: pl.ds(q * quarter, quarter)

    def core_copies(s):
        bufs = ((sbg_s, cg_s.at[s]), (sbu_s, cu_s.at[s]), (sbd_s, cd_s.at[owner(s)]))
        return [remote(a, b, at_core, C + 4 * j + s) for j, (a, b) in enumerate(bufs)]

    def diag_copies(odd):
        return [
            remote(p[1].at[0, rank_rows(q)], p[2].at[rank_rows(q)], at_y if odd else at_x, DG + 4 * j + q)
            for j, p in enumerate(pairs)
            for q in ((1, 3) if odd else (0, 2))
        ]

    x_copies = lambda: [remote(p[1].at[1], p[3], at_x, XS + j) for j, p in enumerate(pairs)]
    y_copies = lambda: [remote(p[1].at[2], p[4], at_y, YS + j) for j, p in enumerate(pairs)]

    def add_ranks(s, first):
        for p in pairs:
            for q in (first, first + 2):
                add_into(p[1].at[s, rank_rows(q)], p[2].at[rank_rows(q)])

    def down_first(q, peer, k, e):
        return remote(cd_s.at[q, rows_at(k, dr)], d1_s.at[q, e], peer, DX + 2 * q + e)

    def step_sums(s):
        q = owner(s)

        @pl.when(lax.rem(q, 2) == 0)
        def _():
            down_first(q, at_x, diag, 0).start()
            down_first(q, at_x, by_x, 1).start()

        @pl.when(lax.rem(q, 2) == 1)
        def _():
            down_first(q, at_y, diag, 0).start()
            down_first(q, at_y, by_y, 1).start()

        @pl.when(s == 0)
        def _():
            each(diag_copies(False), "start")
            each(diag_copies(True), "start")

        @pl.when(s == 1)
        def _():
            each(diag_copies(True), "wait_recv")
            add_ranks(1, 1)
            each(x_copies(), "start")

        @pl.when(s == 2)
        def _():
            each(diag_copies(False), "wait_recv")
            add_ranks(2, 0)
            each(y_copies(), "start")

    @pl.loop(0, 4)
    def _(s):
        each(weights(s), "wait")

        @pl.loop(0, n // RB)
        def _(i):
            rows = rows_at(i, RB)
            n2 = n2_s[rows, :]
            pre = mm(n2, w0_s[...])
            lin = mm(n2, w1_s[...])
            g_act = mm_nt(cot_s[rows, :], w2_s[...])
            sg = 1.0 / (1.0 + jnp.exp(-pre))
            silu = pre * sg
            act = (silu * lin).astype(BF)
            act_s[rows, :] = act
            g_up = (g_act * silu).astype(BF)
            gu_s[rows, :] = g_up
            g_gate = (g_act * lin * sg * (1.0 + pre * (1.0 - sg))).astype(BF)
            gg_s[rows, :] = g_gate
            a_s[rows, :] += mm(act, w2_s[...])
            b_s[rows, :] += mm_nt(g_gate, w0_s[...]) + mm_nt(g_up, w1_s[...])

        @pl.when(s < 3)
        def _():
            each(weights(s + 1), "start")

        @pl.when(s > 0)
        def _():
            each(core_copies(s - 1), "wait_send")

        def product(which, j, put):
            cols = cols_at(which, h)

            @pl.loop(0, d // RB)
            def _(i):
                rows, out = rows_at(i, RB), cols_at(i, RB)
                if j == 2:
                    put(slice(None), out, mm_tn(act_s[:, cols], cot_s[:, out]))
                else:
                    put(rows, slice(None), mm(n2t_s[rows, :], (gg_s, gu_s)[j][:, cols]))

        for j, buf in enumerate((sbg_s, sbu_s, sbd_s)):

            def put(rows, cols, value, buf=buf):
                buf[rows, cols] = value.astype(BF)

            product(1 - core, j, put)
            core_copies(s)[j].start()
        for j, (buf, at) in enumerate(((cg_s, s), (cu_s, s), (cd_s, owner(s)))):
            core_copies(s)[j].wait_recv()

            def put(rows, cols, value, buf=buf, at=at):
                buf[at, rows, cols] = (buf[at, rows, cols].astype(F32) + value).astype(BF)

            product(core, j, put)
        step_sums(s)

    each(win_loads, "start")
    small_s[...] = jnp.zeros_like(small_s)

    @pl.loop(0, n // RB)
    def _(i):
        rows = rows_at(i, RB)
        n2_s[rows, :] = a_s[rows, :].astype(BF)
        g, u = b_s[rows, :], u_s[rows, :]
        small_s[14:15, :] += jnp.sum(g * u, axis=0, keepdims=True)
        gh = cot_s[rows, :].astype(F32) + unit_back(g, u, r_s[rows, 0:1], g2_ref[...])
        gmix_s[rows, :] = gh.astype(BF)

    each(x_loads, "start")
    pair_at = rows_at(half, RB, n)
    mg_s[pair_at, :] = mm_nt(gmix_s[t:, :], wo_s[...]).astype(BF)
    pair_copy = remote(mg_s.at[pair_at], mg_s.at[pair_at], at_pair, PAIR)
    pair_copy.start()

    each(core_copies(3), "wait_send")

    def out_half(which, dst):
        cols = cols_at(which, h)

        @pl.loop(0, d // RB)
        def _(i):
            dst[rows_at(i, RB), :] = mm_tn(mg_s[0:n, cols_at(i, RB)], gmix_s[:, cols]).astype(BF)

    second = lambda c, buf: remote(buf, c2_s.at[c], at_core, C2 + c)
    out_half(1 - core, sbg_s)
    second(0, sbg_s).start()
    out_half(core, raw2_s.at[0])

    each(x_copies(), "wait_recv")
    for p in pairs:

        @pl.loop(0, 4)
        def _(q, p=p):
            add_into(p[1].at[3, rows_at(q, quarter)], p[3].at[rows_at(q, quarter)])

    @pl.loop(0, t // RB)
    def _(i):
        rows = rows_at(i, RB)
        mg_s[rows, :] = mm_nt(gmix_s[rows, :], wo_s[...]).astype(BF)

    each(y_copies(), "wait_recv")
    for p in pairs:

        @pl.loop(0, 4)
        def _(q, p=p):
            add_into(p[1].at[3, rows_at(q, quarter)], p[4].at[rows_at(q, quarter)])

    z_copies = [
        remote(p[1].at[3, rows_at(peers[k], quarter)], p[5].at[k - 1], at_z[k], ZG + 3 * j + k - 1)
        for j, p in enumerate(pairs)
        for k in range(1, 4)
    ]
    each(z_copies, "start")

    rows128 = lay6_h.shape[1]
    sources = [lax.rem(me + 4 - k, 4) for k in range(4)]
    sends_half = [half == p // 2 for p in peers]
    gets_half = [lax.rem(s, 2) == me // 2 for s in sources]

    def home(buf, out, part, base, k):
        if part == 0:
            src, dst = buf.at[rows_at(peers[k], rows128)], out.at[me]
        else:
            src, dst = buf.at[rows_at(lax.rem(peers[k], 2), rows128, t)], out.at[4 + me // 2]
        if k == 0:
            return pltpu.make_async_copy(src, dst, local_sem.at[base])
        return remote(src, dst, at_z[k], base + k - 1)

    def home_start(buf, out, part, base, local):
        for k in range(4):
            copy = home(buf, out, part, base if k else local, k)
            if part == 0:
                copy.start()
            else:
                pl.when(sends_half[k])(copy.start)

    def home_wait(buf, out, part, base, local):
        for k in range(4):
            copy = home(buf, out, part, base if k else local, k)
            if part == 0:
                copy.wait()
            elif k == 0:
                pl.when(sends_half[0])(copy.wait)
            else:
                pl.when(sends_half[k])(copy.wait_send)
                pl.when(gets_half[k])(copy.wait_recv)

    for q in range(4):
        for e in range(2):
            remote(d1_s.at[q, e], d1_s.at[q, e], at_x, DX + 2 * q + e).wait()
        add_into(d1_s.at[q, 0], cd_s.at[q, rows_at(by_x if q % 2 else by_y, dr)])
        add_into(d1_s.at[q, 1], cd_s.at[q, rows_at(xy, dr)])
    down_second = [
        remote(d1_s.at[q, 0], d2_s.at[q], at_x if q % 2 else at_y, DY + q) for q in range(4)
    ]
    each(down_second, "start")
    down_z = [
        remote(d1_s.at[peers[k], 1], zd_s.at[k - 1], at_z[k], ZD + k - 1) for k in range(1, 4)
    ]

    def gather(src, view, base, first_local):
        return [
            remote(src, view(xy, core), peer, base + k)
            for k, peer in enumerate((at_x, at_y, at_xy))
        ], pltpu.make_async_copy(src, view(xy, core), local_sem.at[first_local])

    def gather_core(view, base):
        return [remote(view(k, core), view(k, core), at_core, base + k) for k in range(4)]

    view_dg = lambda k, c: odg_h.at[:, cols_at(2 * k + c, h)]
    view_du = lambda k, c: odu_h.at[:, cols_at(2 * k + c, h)]
    view_dd = lambda k, c: odd_h.at[rows_at(4 * c + k, dr)]
    view_wo = lambda k, c: owo_h.at[rows_at(k, step48), cols_at(c, h)]
    view_wc = lambda k, c: owc_h.at[rows_at(k, step48), cols_at(c, h)]
    view_wi = lambda k, c: owi_h.at[rows_at(k, step48), cols_at(c, 3 * h)]
    gathers = [
        gather(cg_s.at[3, rows_at(me, quarter)], view_dg, GA, 4),
        gather(cu_s.at[3, rows_at(me, quarter)], view_du, GA + 3, 5),
        gather(d1_s.at[me, 1], view_dd, GA + 6, 6),
    ]
    core_gathers = (
        gather_core(view_dg, GC) + gather_core(view_du, GC + 4) + gather_core(view_dd, GC + 8)
    )

    each(loads[6:], "wait")
    each(x_loads, "wait")

    @pl.loop(0, 2)
    def _(slot):
        share = jnp.where(slot == 0, 1.0, 0.5)
        for j in range(3):
            slot_load(slot, j).wait()
        pl.when(slot == 1)(pair_copy.wait)
        gm_at = pl.ds(pl.multiple_of(slot * n, RB), t)

        @pl.loop(0, d // CB)
        def _(c):
            m1, m2 = lanes(m1_ref, CB), lanes(m2_ref, CB)
            mult = lanes(mult_ref, CB)
            cols = cols_at(c, CB)
            query = conv(proj_s[slot, :, cols].astype(F32), st_ref[:, cols], m1, m2)
            gm = mg_s[gm_at, cols].astype(F32)
            a_s[0:t, cols] = gm * filt_s[:, cols].astype(F32)
            spec = mm(tab_s[...], (gm * query).astype(BF)) * isp
            ss = ss_s[:, cols].astype(F32)
            th = th_s[:, cols]
            g_gain = spec[:f] * ss[:f] + spec[f:] * ss[f:]
            g_pre = (g_gain * (1.0 - th * th)).astype(BF)
            gpre_s[:, cols] = g_pre
            weighted = g_pre.astype(F32) * mult
            gprem_s[:, cols] = weighted.astype(BF)
            small_s[13:14, cols] += share * jnp.sum(weighted, axis=0, keepdims=True)
            g = (1.0 + th) * mult
            yy = jnp.concatenate(
                [(g * spec[:f]).astype(BF), (g * spec[f:]).astype(BF)], axis=0
            )
            b_s[0:t, cols] = mm(tabt_s[...], yy)

        @pl.when(slot == 0)
        def _():
            for j in range(3):
                slot_load(1, j).start()
            each(down_second, "wait")
            for q in range(4):
                add_into(d1_s.at[q, 1], d2_s.at[q])
            each(down_z, "start")
            home_start(n2_s, lay6_h, 0, LAY, 0)
            home_start(n2_s, lay6_h, 1, LAY + 3, 1)

        @pl.when(slot == 1)
        def _():
            each(z_copies, "wait")
            for p in pairs:
                rows = rows_at(me, quarter)
                total = p[1][3, rows, :].astype(F32)
                for k in range(3):
                    total += p[5][k].astype(F32)
                p[1][3, rows, :] = total.astype(BF)
            each(down_z, "wait")
            total = d1_s[me, 1].astype(F32)
            for k in range(3):
                total += zd_s[k].astype(F32)
            d1_s[me, 1] = total.astype(BF)
            for copies, local in gathers:
                each(copies, "start")
                local.start()

        for j in range(3, 5):
            slot_load(slot, j).wait()

        @pl.loop(0, d // CB)
        def _(c):
            m1, m2 = lanes(m1_ref, CB), lanes(m2_ref, CB)
            cols = cols_at(c, CB)
            g_feat = mm_nt(gpre_s[...], wc_s[cols, :])
            xc = cs_s[:, cols].astype(F32)
            power = (xc[:f] * xc[:f] + xc[f:] * xc[f:]) * isp
            g_pow = g_feat / (1.0 + power) * (lanes(mult_ref, CB) * (2.0 * isp))
            yy = jnp.concatenate(
                [(g_pow * xc[:f]).astype(BF), (g_pow * xc[f:]).astype(BF)], axis=0
            )
            g_cond = mm(tabt_s[...], yy)
            dwc = share * mm_tn(feat_s[:, cols], gprem_s[...])

            @pl.when(slot == 0)
            def _():
                u_s[cols, :] = dwc

            @pl.when(slot == 1)
            def _():
                u_s[cols, :] += dwc

            def finish(part, g_conv, p):
                at = cols_at(c, CB, part * d)
                sums = share * tap_sums(g_conv, p, m1, m2)
                for j in range(3):
                    row = 1 + 3 * j + part
                    small_s[row : row + 1, cols] += sums[j : j + 1]
                proj_s[slot, :, at] = conv_back(g_conv, st_ref[:, at], m1, m2).astype(BF)

            finish(0, a_s[0:t, cols], proj_s[slot, :, cols].astype(F32))
            key_cols, value_cols = cols_at(c, CB, d), cols_at(c, CB, 2 * d)
            p_value = proj_s[slot, :, value_cols].astype(F32)
            value = conv(p_value, st_ref[:, value_cols], m1, m2).astype(BF).astype(F32)
            g_sig = b_s[0:t, cols]
            p_key = proj_s[slot, :, key_cols].astype(F32)
            key = conv(p_key, st_ref[:, key_cols], m1, m2)
            finish(1, g_sig * value, p_key)
            sums = share * tap_sums(g_cond, value, m1, m2)
            for j in range(3):
                small_s[10 + j : 11 + j, cols] += sums[j : j + 1]
            finish(2, g_sig * key + conv_back(g_cond, ct_ref[:, cols], m1, m2), p_value)

        @pl.when(slot == 0)
        def _():
            for j in range(3, 5):
                slot_load(1, j).start()
            each(win_loads, "wait")

        first = jnp.where(slot == 0, 0, half)

        @pl.loop(0, 2 - slot)
        def _(i):
            rows = pl.ds(pl.multiple_of((2 * slot + i) * RB, RB), RB)
            at = pl.ds(pl.multiple_of((first + i) * RB, RB), RB)
            g = mm_nt(proj_s[slot, at, 0:d], w0_s[...])
            g += mm_nt(proj_s[slot, at, d : 2 * d], w1_s[...])
            g += mm_nt(proj_s[slot, at, 2 * d : 3 * d], w2_s[...])
            u, r = unit_rows(cot_s[rows, :].astype(F32))
            n1t = (u * g1_ref[...]).T.astype(BF)
            for q in range(4):
                for p in range(4):
                    to, fr = (4 * p + q) * step48, (4 * q + p) * step48
                    n2t_s[to : to + step48, rows] = n1t[fr : fr + step48]
            small_s[0:1, :] += jnp.sum(g * u, axis=0, keepdims=True)
            gmix_s[rows, :] = (
                gmix_s[rows, :].astype(F32) + unit_back(g, u, r, g1_ref[...])
            ).astype(BF)

        @pl.when(slot == 0)
        def _():
            home_start(gmix_s, gtok6_h, 0, GT0, 2)

        @pl.when(slot == 1)
        def _():
            home_start(gmix_s, gtok6_h, 1, GT1, 3)

    def cond_half(which, dst):
        cols = cols_at(which, h)

        @pl.loop(0, d // RB)
        def _(i):
            dst[rows_at(i, RB), :] = u_s[rows_at(i, RB), cols].astype(BF)

    cond_half(1 - core, sbu_s)
    second(1, sbu_s).start()
    cond_half(core, raw2_s.at[1])

    def win_product(s, which, add):
        rows = rows_at(owner(s), quarter)
        for c in range(3):
            cols = cols_at(3 * which + c, h)
            dw = mm(n2t_s[rows, 0:RB], proj_s[0, 0:RB, cols])
            dw += mm(n2t_s[rows, RB : 2 * RB], proj_s[0, RB : 2 * RB, cols])
            dw += mm(n2t_s[rows, 2 * RB : 3 * RB], proj_s[1, half_at, cols])
            add(slice(c * h, (c + 1) * h), dw)

    win_core = lambda s: remote(sbw_s.at[s % 2], cw_s.at[s], at_core, CW + s)
    for s in range(4):
        if s > 1:
            win_core(s - 2).wait_send()

        def put(cols, dw, s=s):
            sbw_s[s % 2, :, cols] = dw.astype(BF)

        win_product(s, 1 - core, put)
        win_core(s).start()

    def second_rows(q, k):
        return rows_at(4 * q + k, step48)

    for c in range(2):
        remote(c2_s.at[c], c2_s.at[c], at_core, C2 + c).wait_recv()

        @pl.loop(0, 4)
        def _(q, c=c):
            add_into(c2_s.at[c, rows_at(q, quarter)], raw2_s.at[c, rows_at(q, quarter)])

    d2_copies = [
        remote(
            c2_s.at[c, second_rows(q, diag)],
            r2_s.at[0, c, pl.ds(q * step48, step48)],
            at_y if q % 2 else at_x,
            D2 + 4 * c + q,
        )
        for c in range(2)
        for q in range(4)
    ]
    each(d2_copies, "start")

    def own_put(s):
        def put(cols, dw):
            cw_s[s, :, cols] = (cw_s[s, :, cols].astype(F32) + dw).astype(BF)

        return put

    def wait_core(s):
        remote(cw_s.at[s], cw_s.at[s], at_core, CW + s).wait_recv()

    q48 = lambda q: pl.ds(q * step48, step48)
    win_diag = [
        remote(cw_s.at[0, q48(q)], rw_s.at[0, q48(q)], at_y if q % 2 else at_x, DW + q)
        for q in range(4)
    ]
    wait_core(0)
    win_product(0, core, own_put(0))
    each(win_diag, "start")
    wait_core(1)
    win_product(1, core, own_put(1))
    wait_core(2)
    win_product(2, core, own_put(2))

    each(d2_copies, "wait")
    for c in range(2):
        for q in range(4):
            to = by_x if q % 2 else by_y
            add_into(c2_s.at[c, second_rows(q, to)], r2_s.at[0, c, q48(q)])

    def pack_second(k, dst):
        for c in range(2):
            for q in range(4):
                dst[c, q48(q), :] = c2_s[c, second_rows(q, k), :]

    pack_second(by_x, raw2_s.at[:, pl.ds(0, quarter)])
    pack_second(by_y, raw2_s.at[:, pl.ds(quarter, quarter)])
    x2_copy = remote(raw2_s.at[:, pl.ds(0, quarter)], r2_s.at[1], at_x, XS2)
    y2_copy = remote(raw2_s.at[:, pl.ds(quarter, quarter)], r2_s.at[2], at_y, YS2)
    x2_copy.start()
    y2_copy.start()

    win_x = remote(cw_s.at[1], rw_s.at[1], at_x, XW)
    win_y = remote(cw_s.at[2], rw_s.at[2], at_y, YW)
    each(win_diag, "wait")
    for q in range(4):
        add_into(cw_s.at[1 if q % 2 else 2, q48(q)], rw_s.at[0, q48(q)])
    win_x.start()
    win_y.start()
    small_c = remote(small_s, sgot_s.at[0], at_core, SMALL)
    small_c.start()
    wait_core(3)
    win_product(3, core, own_put(3))

    each([c for copies, _ in gathers for c in copies], "wait")
    each([local for _, local in gathers], "wait")
    each(core_gathers, "start")

    x2_copy.wait()
    y2_copy.wait()
    fin2 = raw2_s.at[:, pl.ds(2 * quarter, quarter)]
    pack_second(xy, fin2)
    for c in range(2):
        add_into(fin2.at[c], r2_s.at[1, c])
        add_into(fin2.at[c], r2_s.at[2, c])
    z2_copies = [
        remote(
            raw2_s.at[:, rows_at(peers[k], step48, 2 * quarter)],
            z2_s.at[k - 1],
            at_z[k],
            Z2 + k - 1,
        )
        for k in range(1, 4)
    ]
    each(z2_copies, "start")
    small_c.wait()
    ssum_s[0] = small_s[...] + sgot_s[0]
    small_x = remote(ssum_s.at[0], sgot_s.at[1], at_x, SMALL + 1)
    small_x.start()

    win_x.wait()
    win_y.wait()
    for q in range(4):
        add_into(cw_s.at[3, q48(q)], rw_s.at[1, q48(q)])
        add_into(cw_s.at[3, q48(q)], rw_s.at[2, q48(q)])
    zw_copies = [
        remote(cw_s.at[3, rows_at(peers[k], step48)], zw_s.at[k - 1], at_z[k], ZW + k - 1)
        for k in range(1, 4)
    ]
    each(zw_copies, "start")
    small_x.wait()
    ssum_s[1] = ssum_s[0] + sgot_s[1]
    small_y = remote(ssum_s.at[1], sgot_s.at[2], at_y, SMALL + 2)
    small_y.start()

    def rank_total(ref, got):
        total = ref[...].astype(F32)
        for k in range(3):
            total += got(k).astype(F32)
        ref[...] = total.astype(BF)

    each(z2_copies, "wait")
    mine2 = rows_at(me, step48, 2 * quarter)
    views2 = (view_wo, view_wc)
    gathers2 = []
    for c in range(2):
        rank_total(raw2_s.at[c, mine2], lambda k, c=c: z2_s[k, c])
        gathers2.append(gather(raw2_s.at[c, mine2], views2[c], GA2 + 3 * c, 7 + c))
    for copies, local in gathers2:
        each(copies, "start")
        local.start()
    small_y.wait()
    ssum_s[2] = ssum_s[1] + sgot_s[2]
    small_z = [
        remote(ssum_s.at[2], sgot_s.at[2 + k], at_z[k], SMALL + 2 + k) for k in range(1, 4)
    ]
    each(small_z, "start")
    for copies, local in gathers2:
        each(copies, "wait")
        local.wait()
    core_gathers2 = gather_core(view_wo, GC2) + gather_core(view_wc, GC2 + 4)
    each(core_gathers2, "start")

    each(zw_copies, "wait")
    minew = rows_at(me, step48)
    rank_total(cw_s.at[3, minew], lambda k: zw_s[k])
    copies, local = gather(cw_s.at[3, minew], view_wi, GW, 9)
    each(copies, "start")
    local.start()
    each(small_z, "wait")
    small_out[...] = ssum_s[2] + sgot_s[3] + sgot_s[4] + sgot_s[5]
    each(copies, "wait")
    local.wait()
    core_gathers3 = gather_core(view_wi, GCW)
    each(core_gathers3, "start")

    each(diag_copies(False) + diag_copies(True) + x_copies() + y_copies(), "wait_send")
    second(0, sbg_s).wait_send()
    second(1, sbu_s).wait_send()
    win_core(2).wait_send()
    win_core(3).wait_send()
    each(core_gathers + core_gathers2, "wait")
    home_wait(n2_s, lay6_h, 0, LAY, 0)
    home_wait(n2_s, lay6_h, 1, LAY + 3, 1)
    home_wait(gmix_s, gtok6_h, 0, GT0, 2)
    home_wait(gmix_s, gtok6_h, 1, GT1, 3)
    each(core_gathers3, "wait")


def back(
    side, slots, isp, isl, mixed, xs, cot, w_out, g2, w_gate, w_up, w_down,
    proj, filt, ss, cs, th, feat, st, ct, w_cond, table, table_t, mult, g1, w_in,
):
    n, d = cot.shape
    t = xs.shape[1]
    f2 = table.shape[0]
    f = f2 // 2
    h, q4, dr, s48 = d // 2, d // 4, d // 8, d // 16
    hbm = pl.BlockSpec(memory_space=pl.ANY)
    vm = pl.BlockSpec(memory_space=pltpu.VMEM)
    smem = pl.BlockSpec(memory_space=pltpu.SMEM)
    b = lambda *s: pltpu.VMEM(s, BF)
    g = lambda *s: pltpu.VMEM(s, F32)
    return pl.pallas_call(
        functools.partial(back_kernel, side),
        name="back",
        out_shape=tuple(
            jax.ShapeDtypeStruct(s, BF)
            for s in (
                (slots, t // 4, d), (slots, t // 4, d), (q4, 4 * d), (q4, 4 * d), (d, d),
                (q4, d), (q4, d), (q4, 3 * d),
            )
        )
        + (jax.ShapeDtypeStruct((16, d), F32),),
        in_specs=[smem, smem] + [hbm] * 4 + [vm] + [hbm] * 9 + [vm, vm, hbm, hbm, hbm]
        + [vm, vm, hbm],
        out_specs=(hbm,) * 8 + (vm,),
        scratch_shapes=[
            g(n, d), g(n, d), g(n, d), g(n, 128),
            b(n, d), b(d, n), b(n, d), b(n + t, d), b(n, d),
            b(n, d), b(n, d), b(n, d), b(d, d), b(d, d), b(d, d), b(d, d), b(d, d),
            b(f2, t), b(t, f2), g(t, 128), g(t, 128),
            b(d, h), b(d, h), b(h, d),
            b(4, d, h), b(4, d, h), b(4, h, d),
            b(d, h), b(d, h), b(d, h), b(d, h), b(d, h), b(d, h),
            b(3, q4, h), b(3, q4, h), b(4, 2, dr, d), b(4, dr, d), b(3, dr, d),
            b(2, t, 3 * d), b(t, d), b(f2, d), b(f2, d), g(f, d), b(f, d), b(f, d), b(f, d),
            b(2, d, h), b(2, d, h), b(3, 2, q4, h), b(3, 2, s48, h),
            b(4, q4, 3 * h), b(2, q4, 3 * h), b(3, q4, 3 * h), b(3, s48, 3 * h),
            g(16, d), g(6, 16, d), g(3, 16, d),
            pltpu.SemaphoreType.DMA((17,)),
            pltpu.SemaphoreType.DMA((6,)),
            pltpu.SemaphoreType.DMA((142,)),
            pltpu.SemaphoreType.DMA((142,)),
            pltpu.SemaphoreType.DMA((10,)),
        ],
        compiler_params=pltpu.CompilerParams(
            collective_id=1, has_side_effects=True, vmem_limit_bytes=65400 * 1024
        ),
    )(
        isp, isl, mixed, xs, cot, w_out, g2, w_gate, w_up, w_down, proj, filt, ss, cs, th, feat,
        st, ct, w_cond, table, table_t, mult, g1, w_in,
    )


def on_device(
    tokens, kind, ln1_gain, w_in, short_taps, cond_taps, w_cond, cond_bias, w_out, ln2_gain,
    w_gate, w_up, w_down, cotangent,
):
    _, rows, slots, d = tokens.shape
    n = lax.axis_size("seq")
    dp_count = lax.axis_size("dp")
    rank = lax.axis_index("seq")
    span_long = rows * n
    is_long = kind[0] == 1

    freqs = -(-max(span_long // 2 + 1, n * (rows // 2 + 1)) // 16) * 16
    table, table_t, mult = wave_tables(is_long, rows, span_long, freqs)
    isp = jnp.where(is_long, 1.0 / span_long, 1.0 / rows).astype(F32).reshape(1)
    place = jnp.arange(span_long, dtype=jnp.int32)
    offset = jnp.where(is_long, place, place % rows)[:, None]
    m1 = jnp.broadcast_to((offset >= 1).astype(F32), (span_long, 128))
    m2 = jnp.broadcast_to((offset >= 2).astype(F32), (span_long, 128))

    tok6 = jnp.transpose(tokens[0], (1, 0, 2))
    cot6 = jnp.transpose(cotangent[0], (1, 0, 2))
    xs, cot = reshard_in(tok6, cot6)

    g1, g2 = ln1_gain.reshape(1, d), ln2_gain.reshape(1, d)
    proj, mixed, filt, sig_spec, cond_spec, th, feat = mix_forward(
        isp, xs, g1, w_in, short_taps, cond_taps, w_cond, cond_bias.reshape(1, d),
        table, table_t, m1, m2, mult,
    )
    side = math.isqrt(dp_count // 2)
    lay6, gtok6, *sums, small = back(
        side, slots, isp, is_long.astype(jnp.int32).reshape(1), mixed, xs, cot, w_out, g2,
        w_gate, w_up, w_down, proj, filt, sig_spec, cond_spec, th, feat, short_taps, cond_taps,
        w_cond, table, table_t, mult, g1, w_in,
    )
    layer_out = jnp.transpose(lay6, (1, 0, 2))[None]
    grad_tokens = jnp.transpose(gtok6, (1, 0, 2))[None]

    sums = [a.astype(F32) for a in sums]
    if dp_count > 8:
        groups = [
            [
                (y * side + x) * 2 + core
                for y in range(y0, side, 2)
                for x in range(x0, side, 2)
            ]
            for y0 in range(2)
            for x0 in range(2)
            for core in range(2)
        ]
        sums = [lax.psum(a, "dp", axis_index_groups=groups) for a in sums]
        small = lax.psum(small, "dp", axis_index_groups=groups)
    grad_gate, grad_up, grad_down, grad_w_out, grad_w_cond, grad_w_in = sums
    part = lambda a, width: lax.dynamic_slice_in_dim(a, rank * width, width, a.ndim - 1)
    return (
        layer_out,
        grad_tokens,
        part(small[0], d // n),
        grad_w_in,
        part(small[1:10].reshape(3, 3 * d), 3 * d // n),
        part(small[10:13], d // n),
        grad_w_cond,
        part(small[13], d // n),
        grad_w_out,
        part(small[14], d // n),
        grad_gate,
        grad_up,
        grad_down,
    )


def solution(mesh):
    rows = P("dp", "seq", None, None)
    return jax.shard_map(
        on_device,
        mesh=mesh,
        in_specs=(rows, P("dp")) + (P(),) * 11 + (rows,),
        out_specs=(
            rows,
            rows,
            P("seq"),
            P("seq", None),
            P(None, "seq"),
            P(None, "seq"),
            P("seq", None),
            P("seq"),
            P("seq", None),
            P("seq"),
            P("seq", None),
            P("seq", None),
            P("seq", None),
        ),
        check_vma=False,
    )
```

```python
import functools
import math

import jax
import jax.numpy as jnp
from jax import lax
from jax.experimental import pallas as pl
from jax.experimental.pallas import tpu as pltpu
from jax.sharding import PartitionSpec as P

BF = jnp.bfloat16
F32 = jnp.float32
MESH = pl.DeviceIdType.MESH
EPS = 1e-05
CB = 256
FC = 384
RB = 256
VMEM_LIMIT = 60 * 2**20


def mm(a, b):
    return jnp.dot(a, b, preferred_element_type=F32)


def mm_nt(a, b):
    return lax.dot_general(a, b, (((1,), (1,)), ((), ())), preferred_element_type=F32)


def mm_tn(a, b):
    return lax.dot_general(a, b, (((0,), (0,)), ((), ())), preferred_element_type=F32)


def unit_rows(x):
    mean = jnp.mean(x, axis=-1, keepdims=True)
    centered = x - mean
    r = lax.rsqrt(jnp.mean(centered * centered, axis=-1, keepdims=True) + EPS)
    return centered * r, r


def unit_back(g, u, r, gain):
    e = g * gain
    return r * (
        e - jnp.mean(e, axis=-1, keepdims=True) - u * jnp.mean(e * u, axis=-1, keepdims=True)
    )


def lanes(ref, width):
    m = ref[...]
    return jnp.concatenate([m] * (width // m.shape[1]), axis=1)


def down(a, j):
    return pltpu.roll(a, j, axis=0)


def up(a, j):
    return pltpu.roll(a, a.shape[0] - j, axis=0)


def conv(a, taps, m1, m2):
    return taps[0:1] * a + taps[1:2] * (down(a, 1) * m1) + taps[2:3] * (down(a, 2) * m2)


def conv_back(g, taps, m1, m2):
    return taps[0:1] * g + taps[1:2] * up(g * m1, 1) + taps[2:3] * up(g * m2, 2)


def tap_sums(g, a, m1, m2):
    return jnp.concatenate(
        [
            jnp.sum(g * a, axis=0, keepdims=True),
            jnp.sum(g * (down(a, 1) * m1), axis=0, keepdims=True),
            jnp.sum(g * (down(a, 2) * m2), axis=0, keepdims=True),
        ],
        axis=0,
    )


def cols_at(c, width, base=0):
    return pl.ds(pl.multiple_of(base + c * width, 128), width)


def short_rows(i, t):
    half = t // 8 + 1
    block = jnp.zeros_like(i)
    for k in range(1, 5):
        block += (i >= k * half).astype(jnp.int32)
    return block, i - half * block


def wave_table(ref, axis, isl, t):
    freqs = ref.shape[axis] // 2
    j = lax.broadcasted_iota(jnp.int32, ref.shape, axis)
    pos = lax.broadcasted_iota(jnp.int32, ref.shape, 1 - axis)
    sin = (j >= freqs).astype(jnp.int32)
    i = j - freqs * sin
    block, f = short_rows(i, t)
    short = t // 4
    phase = isl * (i * pos) + (1 - isl) * (4 * f * (pos & (short - 1)))
    kept_long = (i <= t // 2).astype(jnp.int32)
    kept_short = ((pos >= block * short) & (pos < (block + 1) * short)).astype(jnp.int32)
    kept = isl * kept_long + (1 - isl) * kept_short
    phase = (phase - (t // 4) * sin) & (t - 1)
    angle = (phase - t // 2).astype(F32) * (2.0 * math.pi / t)
    z = angle * angle
    value = jnp.full_like(z, -1.0 / math.factorial(14))
    for k in range(6, -1, -1):
        value = value * z + (-1.0) ** k / math.factorial(2 * k)
    ref[...] = (-value * kept.astype(F32)).astype(ref.dtype)


def multiplicity(shape, isl, t):
    i = lax.broadcasted_iota(jnp.int32, shape, 0)
    block, f = short_rows(i, t)
    once_long = ((i == 0) | (i == t // 2)).astype(jnp.int32)
    once_short = ((f == 0) | (f == t // 8)).astype(jnp.int32)
    long = (2 - once_long) * (i <= t // 2).astype(jnp.int32)
    short = (2 - once_short) * (block < 4).astype(jnp.int32)
    return (isl * long + (1 - isl) * short).astype(F32)


def causal_masks(m1_ref, m2_ref, isl):
    t = m1_ref.shape[0]
    place = lax.broadcasted_iota(jnp.int32, m1_ref.shape, 0)
    short = place & (t // 4 - 1)
    place = short + isl * (place - short)
    m1_ref[...] = (place >= 1).astype(F32)
    m2_ref[...] = (place >= 2).astype(F32)


def inverse_span(isl, t):
    long = isl.astype(F32)
    return long * (1.0 / t) + (1.0 - long) * (4.0 / t)


def front_kernel(
    kind_ref, tok_h, cot_h, g1_ref, win_h, st_ref, ct_ref, wc_h, cb_ref,
    xs_h, cs_h, proj_h, mixed_h, filt_h, ss_h, sc_h, th_h, feat_h, tab_h, tabt_h,
    x_s, win_s, wc_s, tab_s, tabt_s, m1_ref, m2_ref, ms_s, n1_s, q_s,
    proj_s, mixed_s, filt_s, ss_s, sc_s, th_s, feat_s,
    load_sem, out_sem, send_sem, recv_sem,
):
    t, d = n1_s.shape
    f = ms_s.shape[0]
    n = 4
    blk = t // n
    dp, me = lax.axis_index("dp"), lax.axis_index("seq")
    peers = [lax.rem(me + k, n) for k in range(n)]
    sources = [lax.rem(me + n - k, n) for k in range(n)]
    half = lax.rem(me, 2)
    pair = me + 1 - 2 * half
    isl = kind_ref[0]
    isp = inverse_span(isl, t)

    block = lambda i: pl.ds(pl.multiple_of(i * blk, blk), blk)
    half_block = pl.ds(pl.multiple_of(t + half * blk, blk), blk)
    loads = [
        pltpu.make_async_copy(win_h, win_s, load_sem.at[0]),
        pltpu.make_async_copy(wc_h, wc_s, load_sem.at[1]),
        pltpu.make_async_copy(tok_h.at[me], x_s.at[0, block(me)], load_sem.at[2]),
        pltpu.make_async_copy(tok_h.at[n + me // 2], x_s.at[1, block(me)], load_sem.at[3]),
        pltpu.make_async_copy(cot_h.at[me], cs_h.at[block(me)], load_sem.at[4]),
    ]
    half_load = pltpu.make_async_copy(cot_h.at[n + me // 2], cs_h.at[half_block], load_sem.at[5])

    barrier = pltpu.get_barrier_semaphore()
    for k in range(1, n):
        pl.semaphore_signal(barrier, inc=1, device_id=(dp, peers[k]), device_id_type=MESH)
    pl.semaphore_wait(barrier, n - 1)

    def remote(src, dst, peer, j):
        return pltpu.make_async_remote_copy(
            src_ref=src,
            dst_ref=dst,
            send_sem=send_sem.at[j],
            recv_sem=recv_sem.at[j],
            device_id=(dp, peer),
            device_id_type=MESH,
        )

    whole_slot = [
        remote(tok_h.at[peers[k]], x_s.at[0, block(me)], peers[k], k - 1) for k in range(1, n)
    ]
    to_pair = remote(tok_h.at[n + me // 2], x_s.at[1, block(me)], pair, 3)
    across = remote(tok_h.at[n + peers[2] // 2], x_s.at[1, block(me)], peers[2], 4)
    handed = remote(x_s.at[1, block(peers[2])], x_s.at[1, block(peers[2])], pair, 5)
    cots = [remote(cot_h.at[peers[k]], cs_h.at[block(me)], peers[k], 5 + k) for k in range(1, n)]
    halves = [
        remote(cot_h.at[n + peers[k] // 2], cs_h.at[half_block], peers[k], 8 + k)
        for k in range(1, n)
    ]
    sends_half = [lax.rem(p, 2) == me // 2 for p in peers]
    gets_half = [half == s // 2 for s in sources]
    for c in whole_slot + [across, to_pair] + cots:
        c.start()
    for k in range(1, n):
        pl.when(sends_half[k])(halves[k - 1].start)
    for c in loads:
        c.start()
    pl.when(sends_half[0])(half_load.start)

    wave_table(tab_s, 0, isl, t)
    wave_table(tabt_s, 1, isl, t)
    causal_masks(m1_ref, m2_ref, isl)
    ms_s[...] = multiplicity(ms_s.shape, isl, t) * isp

    for c in loads[:4]:
        c.wait()
    for c in whole_slot:
        c.wait()

    outs = [
        (x_s, xs_h), (proj_s, proj_h), (ss_s, ss_h), (sc_s, sc_h), (feat_s, feat_h),
        (mixed_s, mixed_h), (filt_s, filt_h), (th_s, th_h),
    ]

    def out_copy(slot, j):
        return pltpu.make_async_copy(outs[j][0].at[slot], outs[j][1].at[slot], out_sem.at[slot, j])

    tables = [
        pltpu.make_async_copy(tab_s, tab_h, load_sem.at[6]),
        pltpu.make_async_copy(tabt_s, tabt_h, load_sem.at[7]),
    ]
    for c in tables:
        c.start()

    @pl.loop(0, 2)
    def _(slot):
        @pl.when(slot == 1)
        def _():
            to_pair.wait()
            handed.wait()

        @pl.loop(0, t // 128)
        def _(r):
            rows = pl.ds(pl.multiple_of(r * 128, 128), 128)
            u, _ = unit_rows(x_s[slot, rows, :].astype(F32))
            n1_s[rows, :] = (u * g1_ref[...]).astype(BF)

        @pl.loop(0, d // CB)
        def _(c):
            m1, m2 = lanes(m1_ref, CB), lanes(m2_ref, CB)
            own = cols_at(c, CB)

            def part(k):
                cols = cols_at(c, CB, k * d)
                p = mm(n1_s[...], win_s[:, cols]).astype(BF)
                proj_s[slot, :, cols] = p
                return conv(p.astype(F32), st_ref[:, cols], m1, m2)

            q_s[:, own] = part(0)
            key = part(1)
            value = part(2).astype(BF)
            value_f = value.astype(F32)
            signal = (key * value_f).astype(BF)
            ss_s[slot, :, own] = mm(tab_s[...], signal).astype(BF)
            cond = conv(value_f, ct_ref[:, own], m1, m2).astype(BF)
            xc = mm(tab_s[...], cond)
            sc_s[slot, :, own] = xc.astype(BF)
            power = (xc[:f] * xc[:f] + xc[f:] * xc[f:]) * isp
            feat_s[slot, :, own] = jnp.log1p(power).astype(BF)

        for j in range(5):
            out_copy(slot, j).start()

        @pl.when(slot == 0)
        def _():
            across.wait()
            handed.start()

        @pl.loop(0, d // CB)
        def _(c):
            own = cols_at(c, CB)
            th = jnp.tanh(mm(feat_s[slot], wc_s[:, own]) + cb_ref[:, own])
            th_s[slot, :, own] = th
            g = (1.0 + th) * lanes(ms_s, CB)
            xs = ss_s[slot, :, own].astype(F32)
            y = jnp.concatenate([(g * xs[:f]).astype(BF), (g * xs[f:]).astype(BF)], axis=0)
            filt = mm(tabt_s[...], y)
            filt_s[slot, :, own] = filt.astype(BF)
            mixed_s[slot, :, own] = (q_s[:, own] * filt).astype(BF)

        for j in range(5, 8):
            out_copy(slot, j).start()

    for slot in range(2):
        for j in range(8):
            out_copy(slot, j).wait()
    for c in tables + loads[4:] + cots:
        c.wait()
    pl.when(sends_half[0])(half_load.wait)
    for k in range(1, n):
        pl.when(sends_half[k])(halves[k - 1].wait_send)
        pl.when(gets_half[k])(halves[k - 1].wait_recv)


def front(kind, tok, cot, g1, w_in, st, ct, w_cond, cb):
    slots, blk, d = tok.shape
    t = 4 * blk
    f = -(-max(t // 2 + 1, 4 * (blk // 2 + 1)) // 16) * 16
    hbm = pl.BlockSpec(memory_space=pl.ANY)
    vm = pl.BlockSpec(memory_space=pltpu.VMEM)
    smem = pl.BlockSpec(memory_space=pltpu.SMEM)
    per_slot = [
        ((2, t, d), BF), ((2, t, 3 * d), BF), ((2, t, d), BF), ((2, t, d), BF),
        ((2, 2 * f, d), BF), ((2, 2 * f, d), BF), ((2, f, d), F32), ((2, f, d), BF),
    ]
    xs, *rest = [jax.ShapeDtypeStruct(*s) for s in per_slot]
    tables = [((2 * f, t), BF), ((t, 2 * f), BF)]
    return pl.pallas_call(
        front_kernel,
        name="front",
        out_shape=(xs, jax.ShapeDtypeStruct((t + t // 2, d), BF), *rest)
        + tuple(jax.ShapeDtypeStruct(*s) for s in tables),
        in_specs=[smem, hbm, hbm, vm, hbm, vm, vm, hbm, vm],
        out_specs=(hbm,) * 11,
        scratch_shapes=[
            pltpu.VMEM((2, t, d), BF), pltpu.VMEM((d, 3 * d), BF), pltpu.VMEM((d, d), BF),
            pltpu.VMEM(*tables[0]), pltpu.VMEM(*tables[1]),
            pltpu.VMEM((t, 128), F32), pltpu.VMEM((t, 128), F32), pltpu.VMEM((f, 128), F32),
            pltpu.VMEM((t, d), BF), pltpu.VMEM((t, d), F32),
        ]
        + [pltpu.VMEM(*s) for s in per_slot[1:]]
        + [
            pltpu.SemaphoreType.DMA((8,)),
            pltpu.SemaphoreType.DMA((2, 8)),
            pltpu.SemaphoreType.DMA((12,)),
            pltpu.SemaphoreType.DMA((12,)),
        ],
        compiler_params=pltpu.CompilerParams(
            collective_id=0, has_side_effects=True, vmem_limit_bytes=VMEM_LIMIT
        ),
    )(kind, tok, cot, g1, w_in, st, ct, w_cond, cb)


def add_into(dst, src):
    dst[...] = (dst[...].astype(F32) + src[...].astype(F32)).astype(dst.dtype)


def back_kernel(side, *refs):
    (
        kind_ref, mixed_h, xs_h, cot_h, wo_h, g2_ref, wg_h, wu_h, wd_h,
        proj_h, filt_h, ss_h, cs_h, th_h, feat_h,
        st_ref, ct_ref, wc_h, tab_h, tabt_h, g1_ref, win_h,
        lay6_h, gtok6_h, odg_h, odu_h, odd_h, owo_h, owc_h, owi_h, small_out,
        a_s, b_s, u_s, r_s, n2_s, n2t_s, cot_s, mg_s, gmix_s,
        act_s, gg_s, gu_s, w0_s, w1_s, w2_s, wo_s, wc_s, tab_s, tabt_s, m1_ref, m2_ref, mult_ref,
        sbg_s, sbu_s, sbd_s, cg_s, cu_s, cd_s,
        dgg_s, dgu_s, xg_s, xu_s, yg_s, yu_s, zg_s, zu_s, d1_s, d2_s, zd_s,
        proj_s, filt_s, ss_s, cs_s, th_s, feat_s, gpre_s, gprem_s,
        c2_s, raw2_s, r2_s, z2_s, cw_s, sbw_s, rw_s, zw_s, small_s, sgot_s, ssum_s,
        load_sem, w_sem, send_sem, recv_sem, local_sem,
    ) = refs
    n, d = n2_s.shape
    t = filt_s.shape[0]
    f = th_s.shape[0]
    isl = kind_ref[0]
    isp = inverse_span(isl, t)
    h = d // 2
    quarter = d // 4
    step48 = d // 16
    dr = h // 4

    dp, me = lax.axis_index("dp"), lax.axis_index("seq")
    core = lax.rem(dp, 2)
    x = lax.rem(lax.rem(dp // 2, side), 2)
    y = lax.rem(dp // (2 * side), 2)
    dp_x = dp + 2 - 4 * x
    dp_y = dp + 2 * side - 4 * side * y
    at_core, at_x, at_y = (dp + 1 - 2 * core, me), (dp_x, me), (dp_y, me)
    at_xy = (dp_x + dp_y - dp, me)
    peers = [lax.rem(me + k, 4) for k in range(4)]
    at_z = [(dp, peers[k]) for k in range(4)]
    half = lax.rem(me, 2)
    at_pair = (dp, me + 1 - 2 * half)
    half_at = pl.ds(pl.multiple_of(half * RB, RB), RB)
    xy = 2 * x + y
    diag, by_x, by_y = 3 - xy, 2 * (1 - x) + y, 2 * x + 1 - y

    def owner(s):
        if isinstance(s, int):
            return (diag, by_x, by_y, xy)[s]
        return 2 * jnp.where(s < 2, 1 - x, x) + jnp.where(lax.rem(s, 2) == 0, 1 - y, y)

    def rows_at(i, size, base=0):
        return pl.ds(pl.multiple_of(base + i * size, math.gcd(size, base) if base else size), size)

    def each(copies, what):
        for c in copies:
            getattr(c, what)()

    row_moves = lambda src, dst: [
        (src.at[0], dst.at[pl.ds(0, t)]),
        (src.at[1, half_at], dst.at[pl.ds(t, RB)]),
    ]
    moves = (
        row_moves(mixed_h, mg_s)
        + row_moves(xs_h, gmix_s)
        + [(wo_h, wo_s), (cot_h, cot_s)]
        + [(tab_h, tab_s), (tabt_h, tabt_s), (wc_h, wc_s), (proj_h, proj_s)]
    )
    loads = [pltpu.make_async_copy(s, e, load_sem.at[j]) for j, (s, e) in enumerate(moves)]
    slot_moves = [(filt_h, filt_s), (ss_h, ss_s), (th_h, th_s), (cs_h, cs_s), (feat_h, feat_s)]
    slot_load = lambda slot, j: pltpu.make_async_copy(
        slot_moves[j][0].at[slot], slot_moves[j][1], load_sem.at[10 + j]
    )
    x_loads = [
        pltpu.make_async_copy(a, b, load_sem.at[15 + j])
        for j, (a, b) in enumerate(row_moves(xs_h, cot_s))
    ]

    def weights(s):
        cols = cols_at(owner(s), d)
        return [
            pltpu.make_async_copy(wg_h.at[:, cols], w0_s, w_sem.at[0]),
            pltpu.make_async_copy(wu_h.at[:, cols], w1_s, w_sem.at[1]),
            pltpu.make_async_copy(wd_h.at[cols, :], w2_s, w_sem.at[2]),
        ]

    win_loads = [
        pltpu.make_async_copy(win_h.at[:, k * d : (k + 1) * d], w, w_sem.at[3 + k])
        for k, w in enumerate((w0_s, w1_s, w2_s))
    ]

    each(loads[:6], "start")
    each(weights(0), "start")
    each(loads[6:], "start")
    for j in range(5):
        slot_load(0, j).start()

    barrier = pltpu.get_barrier_semaphore()
    everyone = [at_core, at_x, at_y, at_xy] + at_z[1:]
    for peer in everyone:
        pl.semaphore_signal(barrier, inc=1, device_id=peer, device_id_type=MESH)
    pl.semaphore_wait(barrier, len(everyone))

    causal_masks(m1_ref, m2_ref, isl)
    mult_ref[...] = multiplicity(mult_ref.shape, isl, t)

    def remote(src, dst, peer, j):
        return pltpu.make_async_remote_copy(
            src_ref=src,
            dst_ref=dst,
            send_sem=send_sem.at[j],
            recv_sem=recv_sem.at[j],
            device_id=peer,
            device_id_type=MESH,
        )

    C, DG, XS, YS, ZD, ZG, GA, GC, DX, DY = 0, 12, 20, 22, 24, 27, 36, 45, 130, 138
    C2, D2, XS2, YS2, Z2, GA2, GC2 = 57, 59, 67, 69, 71, 77, 83
    CW, DW, XW, YW, ZW, GW, GCW = 91, 95, 99, 100, 101, 104, 107
    LAY, GT0, GT1, PAIR, SMALL = 111, 117, 120, 123, 124

    each(loads[:6], "wait")

    @pl.loop(0, n // RB)
    def _(i):
        rows = rows_at(i, RB)
        hid = gmix_s[rows, :].astype(F32) + mm(mg_s[rows, :], wo_s[...])
        a_s[rows, :] = hid
        b_s[rows, :] = jnp.zeros_like(hid)
        u, r = unit_rows(hid)
        u_s[rows, :] = u
        r_s[rows, :] = jnp.broadcast_to(r, (RB, 128))
        n2 = u * g2_ref[...]
        n2_s[rows, :] = n2.astype(BF)
        n2t_s[:, rows] = n2.T.astype(BF)

    pairs = ((sbg_s, cg_s, dgg_s, xg_s, yg_s, zg_s), (sbu_s, cu_s, dgu_s, xu_s, yu_s, zu_s))
    rank_rows = lambda q: pl.ds(q * quarter, quarter)

    def core_copies(s):
        bufs = ((sbg_s, cg_s.at[s]), (sbu_s, cu_s.at[s]), (sbd_s, cd_s.at[owner(s)]))
        return [remote(a, b, at_core, C + 4 * j + s) for j, (a, b) in enumerate(bufs)]

    def diag_copies(odd):
        return [
            remote(p[1].at[0, rank_rows(q)], p[2].at[rank_rows(q)], at_y if odd else at_x, DG + 4 * j + q)
            for j, p in enumerate(pairs)
            for q in ((1, 3) if odd else (0, 2))
        ]

    x_copies = lambda: [remote(p[1].at[1], p[3], at_x, XS + j) for j, p in enumerate(pairs)]
    y_copies = lambda: [remote(p[1].at[2], p[4], at_y, YS + j) for j, p in enumerate(pairs)]

    def add_ranks(s, first):
        for p in pairs:
            for q in (first, first + 2):
                add_into(p[1].at[s, rank_rows(q)], p[2].at[rank_rows(q)])

    def down_first(q, peer, k, e):
        return remote(cd_s.at[q, rows_at(k, dr)], d1_s.at[q, e], peer, DX + 2 * q + e)

    def step_sums(s):
        q = owner(s)

        @pl.when(lax.rem(q, 2) == 0)
        def _():
            down_first(q, at_x, diag, 0).start()
            down_first(q, at_x, by_x, 1).start()

        @pl.when(lax.rem(q, 2) == 1)
        def _():
            down_first(q, at_y, diag, 0).start()
            down_first(q, at_y, by_y, 1).start()

        @pl.when(s == 0)
        def _():
            each(diag_copies(False), "start")
            each(diag_copies(True), "start")

        @pl.when(s == 1)
        def _():
            each(diag_copies(True), "wait_recv")
            add_ranks(1, 1)
            each(x_copies(), "start")

        @pl.when(s == 2)
        def _():
            each(diag_copies(False), "wait_recv")
            add_ranks(2, 0)
            each(y_copies(), "start")

    @pl.loop(0, 4)
    def _(s):
        each(weights(s), "wait")

        @pl.loop(0, n // RB)
        def _(i):
            rows = rows_at(i, RB)
            n2 = n2_s[rows, :]
            pre = mm(n2, w0_s[...])
            lin = mm(n2, w1_s[...])
            g_act = mm_nt(cot_s[rows, :], w2_s[...])
            sg = 1.0 / (1.0 + jnp.exp(-pre))
            silu = pre * sg
            act = (silu * lin).astype(BF)
            act_s[rows, :] = act
            g_up = (g_act * silu).astype(BF)
            gu_s[rows, :] = g_up
            g_gate = (g_act * lin * sg * (1.0 + pre * (1.0 - sg))).astype(BF)
            gg_s[rows, :] = g_gate
            a_s[rows, :] += mm(act, w2_s[...])
            b_s[rows, :] += mm_nt(g_gate, w0_s[...]) + mm_nt(g_up, w1_s[...])

        @pl.when(s < 3)
        def _():
            each(weights(s + 1), "start")

        @pl.when(s > 0)
        def _():
            each(core_copies(s - 1), "wait_send")

        def product(which, j, put):
            cols = cols_at(which, h)

            @pl.loop(0, d // RB)
            def _(i):
                rows, out = rows_at(i, RB), cols_at(i, RB)
                if j == 2:
                    put(slice(None), out, mm_tn(act_s[:, cols], cot_s[:, out]))
                else:
                    put(rows, slice(None), mm(n2t_s[rows, :], (gg_s, gu_s)[j][:, cols]))

        for j, buf in enumerate((sbg_s, sbu_s, sbd_s)):

            def put(rows, cols, value, buf=buf):
                buf[rows, cols] = value.astype(BF)

            product(1 - core, j, put)
            core_copies(s)[j].start()
        for j, (buf, at) in enumerate(((cg_s, s), (cu_s, s), (cd_s, owner(s)))):
            core_copies(s)[j].wait_recv()

            def put(rows, cols, value, buf=buf, at=at):
                buf[at, rows, cols] = (buf[at, rows, cols].astype(F32) + value).astype(BF)

            product(core, j, put)
        step_sums(s)

    each(win_loads, "start")
    small_s[...] = jnp.zeros_like(small_s)

    @pl.loop(0, n // RB)
    def _(i):
        rows = rows_at(i, RB)
        n2_s[rows, :] = a_s[rows, :].astype(BF)
        g, u = b_s[rows, :], u_s[rows, :]
        small_s[14:15, :] += jnp.sum(g * u, axis=0, keepdims=True)
        gh = cot_s[rows, :].astype(F32) + unit_back(g, u, r_s[rows, 0:1], g2_ref[...])
        gmix_s[rows, :] = gh.astype(BF)

    each(x_loads, "start")
    pair_at = rows_at(half, RB, n)
    mg_s[pair_at, :] = mm_nt(gmix_s[t:, :], wo_s[...]).astype(BF)
    pair_copy = remote(mg_s.at[pair_at], mg_s.at[pair_at], at_pair, PAIR)
    pair_copy.start()

    each(core_copies(3), "wait_send")

    def out_half(which, dst):
        cols = cols_at(which, h)

        @pl.loop(0, d // RB)
        def _(i):
            dst[rows_at(i, RB), :] = mm_tn(mg_s[0:n, cols_at(i, RB)], gmix_s[:, cols]).astype(BF)

    second = lambda c, buf: remote(buf, c2_s.at[c], at_core, C2 + c)
    out_half(1 - core, sbg_s)
    second(0, sbg_s).start()
    out_half(core, raw2_s.at[0])

    each(x_copies(), "wait_recv")
    for p in pairs:

        @pl.loop(0, 4)
        def _(q, p=p):
            add_into(p[1].at[3, rows_at(q, quarter)], p[3].at[rows_at(q, quarter)])

    @pl.loop(0, t // RB)
    def _(i):
        rows = rows_at(i, RB)
        mg_s[rows, :] = mm_nt(gmix_s[rows, :], wo_s[...]).astype(BF)

    each(y_copies(), "wait_recv")
    for p in pairs:

        @pl.loop(0, 4)
        def _(q, p=p):
            add_into(p[1].at[3, rows_at(q, quarter)], p[4].at[rows_at(q, quarter)])

    z_copies = [
        remote(p[1].at[3, rows_at(peers[k], quarter)], p[5].at[k - 1], at_z[k], ZG + 3 * j + k - 1)
        for j, p in enumerate(pairs)
        for k in range(1, 4)
    ]
    each(z_copies, "start")

    rows128 = lay6_h.shape[1]
    sources = [lax.rem(me + 4 - k, 4) for k in range(4)]
    sends_half = [half == p // 2 for p in peers]
    gets_half = [lax.rem(s, 2) == me // 2 for s in sources]

    def home(buf, out, part, base, k):
        if part == 0:
            src, dst = buf.at[rows_at(peers[k], rows128)], out.at[me]
        else:
            src, dst = buf.at[rows_at(lax.rem(peers[k], 2), rows128, t)], out.at[4 + me // 2]
        if k == 0:
            return pltpu.make_async_copy(src, dst, local_sem.at[base])
        return remote(src, dst, at_z[k], base + k - 1)

    def home_start(buf, out, part, base, local):
        for k in range(4):
            copy = home(buf, out, part, base if k else local, k)
            if part == 0:
                copy.start()
            else:
                pl.when(sends_half[k])(copy.start)

    def home_wait(buf, out, part, base, local):
        for k in range(4):
            copy = home(buf, out, part, base if k else local, k)
            if part == 0:
                copy.wait()
            elif k == 0:
                pl.when(sends_half[0])(copy.wait)
            else:
                pl.when(sends_half[k])(copy.wait_send)
                pl.when(gets_half[k])(copy.wait_recv)

    for q in range(4):
        for e in range(2):
            remote(d1_s.at[q, e], d1_s.at[q, e], at_x, DX + 2 * q + e).wait()
        add_into(d1_s.at[q, 0], cd_s.at[q, rows_at(by_x if q % 2 else by_y, dr)])
        add_into(d1_s.at[q, 1], cd_s.at[q, rows_at(xy, dr)])
    down_second = [
        remote(d1_s.at[q, 0], d2_s.at[q], at_x if q % 2 else at_y, DY + q) for q in range(4)
    ]
    each(down_second, "start")
    down_z = [
        remote(d1_s.at[peers[k], 1], zd_s.at[k - 1], at_z[k], ZD + k - 1) for k in range(1, 4)
    ]

    def gather(src, view, base, first_local):
        return [
            remote(src, view(xy, core), peer, base + k)
            for k, peer in enumerate((at_x, at_y, at_xy))
        ], pltpu.make_async_copy(src, view(xy, core), local_sem.at[first_local])

    def gather_core(view, base):
        return [remote(view(k, core), view(k, core), at_core, base + k) for k in range(4)]

    view_dg = lambda k, c: odg_h.at[:, cols_at(2 * k + c, h)]
    view_du = lambda k, c: odu_h.at[:, cols_at(2 * k + c, h)]
    view_dd = lambda k, c: odd_h.at[rows_at(4 * c + k, dr)]
    view_wo = lambda k, c: owo_h.at[rows_at(k, step48), cols_at(c, h)]
    view_wc = lambda k, c: owc_h.at[rows_at(k, step48), cols_at(c, h)]
    view_wi = lambda k, c: owi_h.at[rows_at(k, step48), cols_at(c, 3 * h)]
    gathers = [
        gather(cg_s.at[3, rows_at(me, quarter)], view_dg, GA, 4),
        gather(cu_s.at[3, rows_at(me, quarter)], view_du, GA + 3, 5),
        gather(d1_s.at[me, 1], view_dd, GA + 6, 6),
    ]
    core_gathers = (
        gather_core(view_dg, GC) + gather_core(view_du, GC + 4) + gather_core(view_dd, GC + 8)
    )

    each(loads[6:], "wait")
    each(x_loads, "wait")

    @pl.loop(0, 2)
    def _(slot):
        share = jnp.where(slot == 0, 1.0, 0.5)
        for j in range(3):
            slot_load(slot, j).wait()
        pl.when(slot == 1)(pair_copy.wait)
        gm_at = pl.ds(pl.multiple_of(slot * n, RB), t)

        @pl.loop(0, d // CB)
        def _(c):
            m1, m2 = lanes(m1_ref, CB), lanes(m2_ref, CB)
            mult = lanes(mult_ref, CB)
            cols = cols_at(c, CB)
            query = conv(proj_s[slot, :, cols].astype(F32), st_ref[:, cols], m1, m2)
            gm = mg_s[gm_at, cols].astype(F32)
            a_s[0:t, cols] = gm * filt_s[:, cols].astype(F32)
            spec = mm(tab_s[...], (gm * query).astype(BF)) * isp
            ss = ss_s[:, cols].astype(F32)
            th = th_s[:, cols]
            g_gain = spec[:f] * ss[:f] + spec[f:] * ss[f:]
            g_pre = (g_gain * (1.0 - th * th)).astype(BF)
            gpre_s[:, cols] = g_pre
            weighted = g_pre.astype(F32) * mult
            gprem_s[:, cols] = weighted.astype(BF)
            small_s[13:14, cols] += share * jnp.sum(weighted, axis=0, keepdims=True)
            g = (1.0 + th) * mult
            yy = jnp.concatenate(
                [(g * spec[:f]).astype(BF), (g * spec[f:]).astype(BF)], axis=0
            )
            b_s[0:t, cols] = mm(tabt_s[...], yy)

        @pl.when(slot == 0)
        def _():
            for j in range(3):
                slot_load(1, j).start()
            each(down_second, "wait")
            for q in range(4):
                add_into(d1_s.at[q, 1], d2_s.at[q])
            each(down_z, "start")
            home_start(n2_s, lay6_h, 0, LAY, 0)
            home_start(n2_s, lay6_h, 1, LAY + 3, 1)

        @pl.when(slot == 1)
        def _():
            each(z_copies, "wait")
            for p in pairs:
                rows = rows_at(me, quarter)
                total = p[1][3, rows, :].astype(F32)
                for k in range(3):
                    total += p[5][k].astype(F32)
                p[1][3, rows, :] = total.astype(BF)
            each(down_z, "wait")
            total = d1_s[me, 1].astype(F32)
            for k in range(3):
                total += zd_s[k].astype(F32)
            d1_s[me, 1] = total.astype(BF)
            for copies, local in gathers:
                each(copies, "start")
                local.start()

        for j in range(3, 5):
            slot_load(slot, j).wait()

        @pl.loop(0, d // CB)
        def _(c):
            m1, m2 = lanes(m1_ref, CB), lanes(m2_ref, CB)
            cols = cols_at(c, CB)
            g_feat = mm_nt(gpre_s[...], wc_s[cols, :])
            xc = cs_s[:, cols].astype(F32)
            power = (xc[:f] * xc[:f] + xc[f:] * xc[f:]) * isp
            g_pow = g_feat / (1.0 + power) * (lanes(mult_ref, CB) * (2.0 * isp))
            yy = jnp.concatenate(
                [(g_pow * xc[:f]).astype(BF), (g_pow * xc[f:]).astype(BF)], axis=0
            )
            g_cond = mm(tabt_s[...], yy)
            dwc = share * mm_tn(feat_s[:, cols], gprem_s[...])

            @pl.when(slot == 0)
            def _():
                u_s[cols, :] = dwc

            @pl.when(slot == 1)
            def _():
                u_s[cols, :] += dwc

            def finish(part, g_conv, p):
                at = cols_at(c, CB, part * d)
                sums = share * tap_sums(g_conv, p, m1, m2)
                for j in range(3):
                    row = 1 + 3 * j + part
                    small_s[row : row + 1, cols] += sums[j : j + 1]
                proj_s[slot, :, at] = conv_back(g_conv, st_ref[:, at], m1, m2).astype(BF)

            finish(0, a_s[0:t, cols], proj_s[slot, :, cols].astype(F32))
            key_cols, value_cols = cols_at(c, CB, d), cols_at(c, CB, 2 * d)
            p_value = proj_s[slot, :, value_cols].astype(F32)
            value = conv(p_value, st_ref[:, value_cols], m1, m2).astype(BF).astype(F32)
            g_sig = b_s[0:t, cols]
            p_key = proj_s[slot, :, key_cols].astype(F32)
            key = conv(p_key, st_ref[:, key_cols], m1, m2)
            finish(1, g_sig * value, p_key)
            sums = share * tap_sums(g_cond, value, m1, m2)
            for j in range(3):
                small_s[10 + j : 11 + j, cols] += sums[j : j + 1]
            finish(2, g_sig * key + conv_back(g_cond, ct_ref[:, cols], m1, m2), p_value)

        @pl.when(slot == 0)
        def _():
            for j in range(3, 5):
                slot_load(1, j).start()
            each(win_loads, "wait")

        first = jnp.where(slot == 0, 0, half)

        @pl.loop(0, 2 - slot)
        def _(i):
            rows = pl.ds(pl.multiple_of((2 * slot + i) * RB, RB), RB)
            at = pl.ds(pl.multiple_of((first + i) * RB, RB), RB)
            g = mm_nt(proj_s[slot, at, 0:d], w0_s[...])
            g += mm_nt(proj_s[slot, at, d : 2 * d], w1_s[...])
            g += mm_nt(proj_s[slot, at, 2 * d : 3 * d], w2_s[...])
            u, r = unit_rows(cot_s[rows, :].astype(F32))
            n1t = (u * g1_ref[...]).T.astype(BF)
            for q in range(4):
                for p in range(4):
                    to, fr = (4 * p + q) * step48, (4 * q + p) * step48
                    n2t_s[to : to + step48, rows] = n1t[fr : fr + step48]
            small_s[0:1, :] += jnp.sum(g * u, axis=0, keepdims=True)
            gmix_s[rows, :] = (
                gmix_s[rows, :].astype(F32) + unit_back(g, u, r, g1_ref[...])
            ).astype(BF)

        @pl.when(slot == 0)
        def _():
            home_start(gmix_s, gtok6_h, 0, GT0, 2)

        @pl.when(slot == 1)
        def _():
            home_start(gmix_s, gtok6_h, 1, GT1, 3)

    def cond_half(which, dst):
        cols = cols_at(which, h)

        @pl.loop(0, d // RB)
        def _(i):
            dst[rows_at(i, RB), :] = u_s[rows_at(i, RB), cols].astype(BF)

    cond_half(1 - core, sbu_s)
    second(1, sbu_s).start()
    cond_half(core, raw2_s.at[1])

    def win_product(s, which, add):
        rows = rows_at(owner(s), quarter)
        for c in range(3):
            cols = cols_at(3 * which + c, h)
            dw = mm(n2t_s[rows, 0:RB], proj_s[0, 0:RB, cols])
            dw += mm(n2t_s[rows, RB : 2 * RB], proj_s[0, RB : 2 * RB, cols])
            dw += mm(n2t_s[rows, 2 * RB : 3 * RB], proj_s[1, half_at, cols])
            add(slice(c * h, (c + 1) * h), dw)

    win_core = lambda s: remote(sbw_s.at[s % 2], cw_s.at[s], at_core, CW + s)
    for s in range(4):
        if s > 1:
            win_core(s - 2).wait_send()

        def put(cols, dw, s=s):
            sbw_s[s % 2, :, cols] = dw.astype(BF)

        win_product(s, 1 - core, put)
        win_core(s).start()

    def second_rows(q, k):
        return rows_at(4 * q + k, step48)

    for c in range(2):
        remote(c2_s.at[c], c2_s.at[c], at_core, C2 + c).wait_recv()

        @pl.loop(0, 4)
        def _(q, c=c):
            add_into(c2_s.at[c, rows_at(q, quarter)], raw2_s.at[c, rows_at(q, quarter)])

    d2_copies = [
        remote(
            c2_s.at[c, second_rows(q, diag)],
            r2_s.at[0, c, pl.ds(q * step48, step48)],
            at_y if q % 2 else at_x,
            D2 + 4 * c + q,
        )
        for c in range(2)
        for q in range(4)
    ]
    each(d2_copies, "start")

    def own_put(s):
        def put(cols, dw):
            cw_s[s, :, cols] = (cw_s[s, :, cols].astype(F32) + dw).astype(BF)

        return put

    def wait_core(s):
        remote(cw_s.at[s], cw_s.at[s], at_core, CW + s).wait_recv()

    q48 = lambda q: pl.ds(q * step48, step48)
    win_diag = [
        remote(cw_s.at[0, q48(q)], rw_s.at[0, q48(q)], at_y if q % 2 else at_x, DW + q)
        for q in range(4)
    ]
    wait_core(0)
    win_product(0, core, own_put(0))
    each(win_diag, "start")
    wait_core(1)
    win_product(1, core, own_put(1))
    wait_core(2)
    win_product(2, core, own_put(2))

    each(d2_copies, "wait")
    for c in range(2):
        for q in range(4):
            to = by_x if q % 2 else by_y
            add_into(c2_s.at[c, second_rows(q, to)], r2_s.at[0, c, q48(q)])

    def pack_second(k, dst):
        for c in range(2):
            for q in range(4):
                dst[c, q48(q), :] = c2_s[c, second_rows(q, k), :]

    pack_second(by_x, raw2_s.at[:, pl.ds(0, quarter)])
    pack_second(by_y, raw2_s.at[:, pl.ds(quarter, quarter)])
    x2_copy = remote(raw2_s.at[:, pl.ds(0, quarter)], r2_s.at[1], at_x, XS2)
    y2_copy = remote(raw2_s.at[:, pl.ds(quarter, quarter)], r2_s.at[2], at_y, YS2)
    x2_copy.start()
    y2_copy.start()

    win_x = remote(cw_s.at[1], rw_s.at[1], at_x, XW)
    win_y = remote(cw_s.at[2], rw_s.at[2], at_y, YW)
    each(win_diag, "wait")
    for q in range(4):
        add_into(cw_s.at[1 if q % 2 else 2, q48(q)], rw_s.at[0, q48(q)])
    win_x.start()
    win_y.start()
    small_c = remote(small_s, sgot_s.at[0], at_core, SMALL)
    small_c.start()
    wait_core(3)
    win_product(3, core, own_put(3))

    each([c for copies, _ in gathers for c in copies], "wait")
    each([local for _, local in gathers], "wait")
    each(core_gathers, "start")

    x2_copy.wait()
    y2_copy.wait()
    fin2 = raw2_s.at[:, pl.ds(2 * quarter, quarter)]
    pack_second(xy, fin2)
    for c in range(2):
        add_into(fin2.at[c], r2_s.at[1, c])
        add_into(fin2.at[c], r2_s.at[2, c])
    z2_copies = [
        remote(
            raw2_s.at[:, rows_at(peers[k], step48, 2 * quarter)],
            z2_s.at[k - 1],
            at_z[k],
            Z2 + k - 1,
        )
        for k in range(1, 4)
    ]
    each(z2_copies, "start")
    small_c.wait()
    ssum_s[0] = small_s[...] + sgot_s[0]
    small_x = remote(ssum_s.at[0], sgot_s.at[1], at_x, SMALL + 1)
    small_x.start()

    win_x.wait()
    win_y.wait()
    for q in range(4):
        add_into(cw_s.at[3, q48(q)], rw_s.at[1, q48(q)])
        add_into(cw_s.at[3, q48(q)], rw_s.at[2, q48(q)])
    zw_copies = [
        remote(cw_s.at[3, rows_at(peers[k], step48)], zw_s.at[k - 1], at_z[k], ZW + k - 1)
        for k in range(1, 4)
    ]
    each(zw_copies, "start")
    small_x.wait()
    ssum_s[1] = ssum_s[0] + sgot_s[1]
    small_y = remote(ssum_s.at[1], sgot_s.at[2], at_y, SMALL + 2)
    small_y.start()

    def rank_total(ref, got):
        total = ref[...].astype(F32)
        for k in range(3):
            total += got(k).astype(F32)
        ref[...] = total.astype(BF)

    each(z2_copies, "wait")
    mine2 = rows_at(me, step48, 2 * quarter)
    views2 = (view_wo, view_wc)
    gathers2 = []
    for c in range(2):
        rank_total(raw2_s.at[c, mine2], lambda k, c=c: z2_s[k, c])
        gathers2.append(gather(raw2_s.at[c, mine2], views2[c], GA2 + 3 * c, 7 + c))
    for copies, local in gathers2:
        each(copies, "start")
        local.start()
    small_y.wait()
    ssum_s[2] = ssum_s[1] + sgot_s[2]
    small_z = [
        remote(ssum_s.at[2], sgot_s.at[2 + k], at_z[k], SMALL + 2 + k) for k in range(1, 4)
    ]
    each(small_z, "start")
    for copies, local in gathers2:
        each(copies, "wait")
        local.wait()
    core_gathers2 = gather_core(view_wo, GC2) + gather_core(view_wc, GC2 + 4)
    each(core_gathers2, "start")

    each(zw_copies, "wait")
    minew = rows_at(me, step48)
    rank_total(cw_s.at[3, minew], lambda k: zw_s[k])
    copies, local = gather(cw_s.at[3, minew], view_wi, GW, 9)
    each(copies, "start")
    local.start()
    each(small_z, "wait")
    small_out[...] = ssum_s[2] + sgot_s[3] + sgot_s[4] + sgot_s[5]
    each(copies, "wait")
    local.wait()
    core_gathers3 = gather_core(view_wi, GCW)
    each(core_gathers3, "start")

    each(diag_copies(False) + diag_copies(True) + x_copies() + y_copies(), "wait_send")
    second(0, sbg_s).wait_send()
    second(1, sbu_s).wait_send()
    win_core(2).wait_send()
    win_core(3).wait_send()
    each(core_gathers + core_gathers2, "wait")
    home_wait(n2_s, lay6_h, 0, LAY, 0)
    home_wait(n2_s, lay6_h, 1, LAY + 3, 1)
    home_wait(gmix_s, gtok6_h, 0, GT0, 2)
    home_wait(gmix_s, gtok6_h, 1, GT1, 3)
    each(core_gathers3, "wait")


def back(
    side, slots, kind, mixed, xs, cot, w_out, g2, w_gate, w_up, w_down,
    proj, filt, ss, cs, th, feat, st, ct, w_cond, table, table_t, g1, w_in,
):
    n, d = cot.shape
    t = xs.shape[1]
    f2 = table.shape[0]
    f = f2 // 2
    h, q4, dr, s48 = d // 2, d // 4, d // 8, d // 16
    hbm = pl.BlockSpec(memory_space=pl.ANY)
    vm = pl.BlockSpec(memory_space=pltpu.VMEM)
    smem = pl.BlockSpec(memory_space=pltpu.SMEM)
    b = lambda *s: pltpu.VMEM(s, BF)
    g = lambda *s: pltpu.VMEM(s, F32)
    return pl.pallas_call(
        functools.partial(back_kernel, side),
        name="back",
        out_shape=tuple(
            jax.ShapeDtypeStruct(s, BF)
            for s in (
                (slots, t // 4, d), (slots, t // 4, d), (q4, 4 * d), (q4, 4 * d), (d, d),
                (q4, d), (q4, d), (q4, 3 * d),
            )
        )
        + (jax.ShapeDtypeStruct((16, d), F32),),
        in_specs=[smem] + [hbm] * 4 + [vm] + [hbm] * 9 + [vm, vm, hbm, hbm, hbm, vm, hbm],
        out_specs=(hbm,) * 8 + (vm,),
        scratch_shapes=[
            g(n, d), g(n, d), g(n, d), g(n, 128),
            b(n, d), b(d, n), b(n, d), b(n + t, d), b(n, d),
            b(n, d), b(n, d), b(n, d), b(d, d), b(d, d), b(d, d), b(d, d), b(d, d),
            b(f2, t), b(t, f2), g(t, 128), g(t, 128), g(f, 128),
            b(d, h), b(d, h), b(h, d),
            b(4, d, h), b(4, d, h), b(4, h, d),
            b(d, h), b(d, h), b(d, h), b(d, h), b(d, h), b(d, h),
            b(3, q4, h), b(3, q4, h), b(4, 2, dr, d), b(4, dr, d), b(3, dr, d),
            b(2, t, 3 * d), b(t, d), b(f2, d), b(f2, d), g(f, d), b(f, d), b(f, d), b(f, d),
            b(2, d, h), b(2, d, h), b(3, 2, q4, h), b(3, 2, s48, h),
            b(4, q4, 3 * h), b(2, q4, 3 * h), b(3, q4, 3 * h), b(3, s48, 3 * h),
            g(16, d), g(6, 16, d), g(3, 16, d),
            pltpu.SemaphoreType.DMA((17,)),
            pltpu.SemaphoreType.DMA((6,)),
            pltpu.SemaphoreType.DMA((142,)),
            pltpu.SemaphoreType.DMA((142,)),
            pltpu.SemaphoreType.DMA((10,)),
        ],
        compiler_params=pltpu.CompilerParams(
            collective_id=1, has_side_effects=True, vmem_limit_bytes=65400 * 1024
        ),
    )(
        kind, mixed, xs, cot, w_out, g2, w_gate, w_up, w_down, proj, filt, ss, cs, th, feat,
        st, ct, w_cond, table, table_t, g1, w_in,
    )


def on_device(
    tokens, kind, ln1_gain, w_in, short_taps, cond_taps, w_cond, cond_bias, w_out, ln2_gain,
    w_gate, w_up, w_down, cotangent,
):
    _, rows, slots, d = tokens.shape
    n = lax.axis_size("seq")
    dp_count = lax.axis_size("dp")
    rank = lax.axis_index("seq")
    tok6 = jnp.transpose(tokens[0], (1, 0, 2))
    cot6 = jnp.transpose(cotangent[0], (1, 0, 2))
    g1, g2 = ln1_gain.reshape(1, d), ln2_gain.reshape(1, d)
    xs, cot, proj, mixed, filt, sig_spec, cond_spec, th, feat, table, table_t = front(
        kind, tok6, cot6, g1, w_in, short_taps, cond_taps, w_cond, cond_bias.reshape(1, d)
    )
    side = math.isqrt(dp_count // 2)
    lay6, gtok6, *sums, small = back(
        side, slots, kind, mixed, xs, cot, w_out, g2, w_gate, w_up, w_down,
        proj, filt, sig_spec, cond_spec, th, feat, short_taps, cond_taps, w_cond,
        table, table_t, g1, w_in,
    )
    layer_out = jnp.transpose(lay6, (1, 0, 2))[None]
    grad_tokens = jnp.transpose(gtok6, (1, 0, 2))[None]

    sums = [a.astype(F32) for a in sums]
    if dp_count > 8:
        groups = [
            [
                (y * side + x) * 2 + core
                for y in range(y0, side, 2)
                for x in range(x0, side, 2)
            ]
            for y0 in range(2)
            for x0 in range(2)
            for core in range(2)
        ]
        sums = [lax.psum(a, "dp", axis_index_groups=groups) for a in sums]
        small = lax.psum(small, "dp", axis_index_groups=groups)
    grad_gate, grad_up, grad_down, grad_w_out, grad_w_cond, grad_w_in = sums
    part = lambda a, width: lax.dynamic_slice_in_dim(a, rank * width, width, a.ndim - 1)
    return (
        layer_out,
        grad_tokens,
        part(small[0], d // n),
        grad_w_in,
        part(small[1:10].reshape(3, 3 * d), 3 * d // n),
        part(small[10:13], d // n),
        grad_w_cond,
        part(small[13], d // n),
        grad_w_out,
        part(small[14], d // n),
        grad_gate,
        grad_up,
        grad_down,
    )


def solution(mesh):
    rows = P("dp", "seq", None, None)
    return jax.shard_map(
        on_device,
        mesh=mesh,
        in_specs=(rows, P("dp")) + (P(),) * 11 + (rows,),
        out_specs=(
            rows,
            rows,
            P("seq"),
            P("seq", None),
            P(None, "seq"),
            P(None, "seq"),
            P("seq", None),
            P("seq"),
            P("seq", None),
            P("seq"),
            P("seq", None),
            P("seq", None),
            P("seq", None),
        ),
        check_vma=False,
    )
```

```python
import functools
import math

import jax
import jax.numpy as jnp
from jax import lax
from jax.experimental import pallas as pl
from jax.experimental.pallas import tpu as pltpu
from jax.sharding import PartitionSpec as P

BF = jnp.bfloat16
F32 = jnp.float32
MESH = pl.DeviceIdType.MESH
EPS = 1e-05
CB = 256
FC = 384
RB = 256
VMEM_LIMIT = 60 * 2**20


def mm(a, b):
    return jnp.dot(a, b, preferred_element_type=F32)


def mm_nt(a, b):
    return lax.dot_general(a, b, (((1,), (1,)), ((), ())), preferred_element_type=F32)


def mm_tn(a, b):
    return lax.dot_general(a, b, (((0,), (0,)), ((), ())), preferred_element_type=F32)


def unit_rows(x):
    mean = jnp.mean(x, axis=-1, keepdims=True)
    centered = x - mean
    r = lax.rsqrt(jnp.mean(centered * centered, axis=-1, keepdims=True) + EPS)
    return centered * r, r


def unit_back(g, u, r, gain):
    e = g * gain
    return r * (
        e - jnp.mean(e, axis=-1, keepdims=True) - u * jnp.mean(e * u, axis=-1, keepdims=True)
    )


def lanes(ref, width):
    m = ref[...]
    return jnp.concatenate([m] * (width // m.shape[1]), axis=1)


def down(a, j):
    return pltpu.roll(a, j, axis=0)


def up(a, j):
    return pltpu.roll(a, a.shape[0] - j, axis=0)


def masked(a, m):
    blk = a.shape[0] // 4
    parts = []
    for b in range(4):
        parts.append(a[b * blk : b * blk + 8] * m[8 * b : 8 * b + 8])
        parts.append(a[b * blk + 8 : (b + 1) * blk])
    return jnp.concatenate(parts, axis=0)


def conv(a, taps, m1, m2):
    return taps[0:1] * a + taps[1:2] * masked(down(a, 1), m1) + taps[2:3] * masked(down(a, 2), m2)


def conv_back(g, a, taps, m1, m2):
    g1, g2 = up(masked(g, m1), 1), up(masked(g, m2), 2)
    sums = [jnp.sum(v * a, axis=0, keepdims=True) for v in (g, g1, g2)]
    return taps[0:1] * g + taps[1:2] * g1 + taps[2:3] * g2, sums


def cols_at(c, width, base=0):
    return pl.ds(pl.multiple_of(base + c * width, 128), width)


def short_rows(i, t):
    half = t // 8 + 1
    block = jnp.zeros_like(i)
    for k in range(1, 5):
        block += (i >= k * half).astype(jnp.int32)
    return block, i - half * block


def wave_table(ref, axis, isl, t):
    freqs = ref.shape[axis] // 2
    j = lax.broadcasted_iota(jnp.int32, ref.shape, axis)
    pos = lax.broadcasted_iota(jnp.int32, ref.shape, 1 - axis)
    sin = (j >= freqs).astype(jnp.int32)
    i = j - freqs * sin
    block, f = short_rows(i, t)
    short = t // 4
    phase = isl * (i * pos) + (1 - isl) * (4 * f * (pos & (short - 1)))
    kept_long = (i <= t // 2).astype(jnp.int32)
    kept_short = ((pos >= block * short) & (pos < (block + 1) * short)).astype(jnp.int32)
    kept = isl * kept_long + (1 - isl) * kept_short
    phase = (phase - (t // 4) * sin) & (t - 1)
    angle = (phase - t // 2).astype(F32) * (2.0 * math.pi / t)
    z = angle * angle
    value = jnp.full_like(z, -1.0 / math.factorial(14))
    for k in range(6, -1, -1):
        value = value * z + (-1.0) ** k / math.factorial(2 * k)
    ref[...] = (-value * kept.astype(F32)).astype(ref.dtype)


def multiplicity(shape, isl, t):
    i = lax.broadcasted_iota(jnp.int32, shape, 0)
    block, f = short_rows(i, t)
    once_long = ((i == 0) | (i == t // 2)).astype(jnp.int32)
    once_short = ((f == 0) | (f == t // 8)).astype(jnp.int32)
    long = (2 - once_long) * (i <= t // 2).astype(jnp.int32)
    short = (2 - once_short) * (block < 4).astype(jnp.int32)
    return (isl * long + (1 - isl) * short).astype(F32)


def causal_masks(m1_ref, m2_ref, isl):
    row = lax.broadcasted_iota(jnp.int32, m1_ref.shape, 0)
    place = (row & 7) + isl * (row - (row & 7))
    m1_ref[...] = (place >= 1).astype(F32)
    m2_ref[...] = (place >= 2).astype(F32)


def inverse_span(isl, t):
    long = isl.astype(F32)
    return long * (1.0 / t) + (1.0 - long) * (4.0 / t)


def front_kernel(
    kind_ref, tok_h, g1_ref, win_h, st_ref, ct_ref, wc_h, cb_ref,
    xs_h, proj_h, mixed_h, filt_h, ss_h, sc_h, th_h, feat_h, q_h, k_h, v_h, tab_h, tabt_h,
    x_s, win_s, wc_s, tab_s, tabt_s, m1_ref, m2_ref, ms_s, n1_s, q_s,
    proj_s, mixed_s, filt_s, ss_s, sc_s, th_s, feat_s, qb_s, k_s, v_s,
    load_sem, out_sem, send_sem, recv_sem,
):
    t, d = n1_s.shape
    f = ms_s.shape[0]
    n = 4
    blk = t // n
    dp, me = lax.axis_index("dp"), lax.axis_index("seq")
    peers = [lax.rem(me + k, n) for k in range(n)]
    half = lax.rem(me, 2)
    pair = me + 1 - 2 * half
    isl = kind_ref[0]
    isp = inverse_span(isl, t)

    block = lambda i: pl.ds(pl.multiple_of(i * blk, blk), blk)
    loads = [
        pltpu.make_async_copy(win_h, win_s, load_sem.at[0]),
        pltpu.make_async_copy(wc_h, wc_s, load_sem.at[1]),
        pltpu.make_async_copy(tok_h.at[me], x_s.at[0, block(me)], load_sem.at[2]),
        pltpu.make_async_copy(tok_h.at[n + me // 2], x_s.at[1, block(me)], load_sem.at[3]),
    ]

    barrier = pltpu.get_barrier_semaphore()
    for k in range(1, n):
        pl.semaphore_signal(barrier, inc=1, device_id=(dp, peers[k]), device_id_type=MESH)
    pl.semaphore_wait(barrier, n - 1)

    def remote(src, dst, peer, j):
        return pltpu.make_async_remote_copy(
            src_ref=src,
            dst_ref=dst,
            send_sem=send_sem.at[j],
            recv_sem=recv_sem.at[j],
            device_id=(dp, peer),
            device_id_type=MESH,
        )

    whole_slot = [
        remote(tok_h.at[peers[k]], x_s.at[0, block(me)], peers[k], k - 1) for k in range(1, n)
    ]
    to_pair = remote(tok_h.at[n + me // 2], x_s.at[1, block(me)], pair, 3)
    across = remote(tok_h.at[n + peers[2] // 2], x_s.at[1, block(me)], peers[2], 4)
    handed = remote(x_s.at[1, block(peers[2])], x_s.at[1, block(peers[2])], pair, 5)
    for c in whole_slot + [across, to_pair]:
        c.start()
    for c in loads:
        c.start()

    wave_table(tab_s, 0, isl, t)
    wave_table(tabt_s, 1, isl, t)
    causal_masks(m1_ref, m2_ref, isl)
    ms_s[...] = multiplicity(ms_s.shape, isl, t) * isp

    for c in loads[:4]:
        c.wait()
    for c in whole_slot:
        c.wait()

    outs = [
        (x_s, xs_h), (proj_s, proj_h), (ss_s, ss_h), (sc_s, sc_h), (feat_s, feat_h),
        (qb_s, q_h), (k_s, k_h), (v_s, v_h),
        (mixed_s, mixed_h), (filt_s, filt_h), (th_s, th_h),
    ]

    def out_copy(slot, j):
        return pltpu.make_async_copy(outs[j][0].at[slot], outs[j][1].at[slot], out_sem.at[slot, j])

    tables = [
        pltpu.make_async_copy(tab_s, tab_h, load_sem.at[4]),
        pltpu.make_async_copy(tabt_s, tabt_h, load_sem.at[5]),
    ]
    for c in tables:
        c.start()

    @pl.loop(0, 2)
    def _(slot):
        @pl.when(slot == 1)
        def _():
            to_pair.wait()
            handed.wait()

        @pl.loop(0, t // 128)
        def _(r):
            rows = pl.ds(pl.multiple_of(r * 128, 128), 128)
            u, _ = unit_rows(x_s[slot, rows, :].astype(F32))
            n1_s[rows, :] = (u * g1_ref[...]).astype(BF)

        @pl.loop(0, d // CB)
        def _(c):
            m1, m2 = lanes(m1_ref, CB), lanes(m2_ref, CB)
            own = cols_at(c, CB)

            def part(k):
                cols = cols_at(c, CB, k * d)
                p = mm(n1_s[...], win_s[:, cols]).astype(BF)
                proj_s[slot, :, cols] = p
                return conv(p.astype(F32), st_ref[:, cols], m1, m2)

            query = part(0)
            q_s[:, own] = query
            qb_s[slot, :, own] = query.astype(BF)
            key = part(1)
            k_s[slot, :, own] = key.astype(BF)
            value = part(2).astype(BF)
            v_s[slot, :, own] = value
            value_f = value.astype(F32)
            signal = (key * value_f).astype(BF)
            ss_s[slot, :, own] = mm(tab_s[...], signal).astype(BF)
            cond = conv(value_f, ct_ref[:, own], m1, m2).astype(BF)
            xc = mm(tab_s[...], cond)
            sc_s[slot, :, own] = xc.astype(BF)
            power = (xc[:f] * xc[:f] + xc[f:] * xc[f:]) * isp
            feat_s[slot, :, own] = jnp.log1p(power).astype(BF)

        for j in range(8):
            out_copy(slot, j).start()

        @pl.when(slot == 0)
        def _():
            across.wait()
            handed.start()

        @pl.loop(0, d // CB)
        def _(c):
            own = cols_at(c, CB)
            th = jnp.tanh(mm(feat_s[slot], wc_s[:, own]) + cb_ref[:, own])
            th_s[slot, :, own] = th
            g = (1.0 + th) * lanes(ms_s, CB)
            xs = ss_s[slot, :, own].astype(F32)
            y = jnp.concatenate([(g * xs[:f]).astype(BF), (g * xs[f:]).astype(BF)], axis=0)
            filt = mm(tabt_s[...], y)
            filt_s[slot, :, own] = filt.astype(BF)
            mixed_s[slot, :, own] = (q_s[:, own] * filt).astype(BF)

        for j in range(8, 11):
            out_copy(slot, j).start()

    for slot in range(2):
        for j in range(11):
            out_copy(slot, j).wait()
    for c in tables:
        c.wait()


def front(kind, tok, g1, w_in, st, ct, w_cond, cb):
    slots, blk, d = tok.shape
    t = 4 * blk
    f = -(-max(t // 2 + 1, 4 * (blk // 2 + 1)) // 16) * 16
    hbm = pl.BlockSpec(memory_space=pl.ANY)
    vm = pl.BlockSpec(memory_space=pltpu.VMEM)
    smem = pl.BlockSpec(memory_space=pltpu.SMEM)
    per_slot = [
        ((2, t, d), BF), ((2, t, 3 * d), BF), ((2, t, d), BF), ((2, t, d), BF),
        ((2, 2 * f, d), BF), ((2, 2 * f, d), BF), ((2, f, d), F32), ((2, f, d), BF),
        ((2, t, d), BF), ((2, t, d), BF), ((2, t, d), BF),
    ]
    xs, *rest = [jax.ShapeDtypeStruct(*s) for s in per_slot]
    tables = [((2 * f, t), BF), ((t, 2 * f), BF)]
    return pl.pallas_call(
        front_kernel,
        name="front",
        out_shape=(xs, *rest)
        + tuple(jax.ShapeDtypeStruct(*s) for s in tables),
        in_specs=[smem, hbm, vm, hbm, vm, vm, hbm, vm],
        out_specs=(hbm,) * 13,
        scratch_shapes=[
            pltpu.VMEM((2, t, d), BF), pltpu.VMEM((d, 3 * d), BF), pltpu.VMEM((d, d), BF),
            pltpu.VMEM(*tables[0]), pltpu.VMEM(*tables[1]),
            pltpu.VMEM((32, 128), F32), pltpu.VMEM((32, 128), F32), pltpu.VMEM((f, 128), F32),
            pltpu.VMEM((t, d), BF), pltpu.VMEM((t, d), F32),
        ]
        + [pltpu.VMEM(*s) for s in per_slot[1:]]
        + [
            pltpu.SemaphoreType.DMA((6,)),
            pltpu.SemaphoreType.DMA((2, 11)),
            pltpu.SemaphoreType.DMA((6,)),
            pltpu.SemaphoreType.DMA((6,)),
        ],
        compiler_params=pltpu.CompilerParams(
            collective_id=0, has_side_effects=True, vmem_limit_bytes=VMEM_LIMIT
        ),
    )(kind, tok, g1, w_in, st, ct, w_cond, cb)


def add_into(dst, src):
    dst[...] = (dst[...].astype(F32) + src[...].astype(F32)).astype(dst.dtype)


def back_kernel(side, *refs):
    (
        kind_ref, mixed_h, xs_h, cot_h, wo_h, g2_ref, wg_h, wu_h, wd_h,
        proj_h, filt_h, ss_h, cs_h, th_h, feat_h, q_h, k_h, v_h,
        st_ref, ct_ref, wc_h, tab_h, tabt_h, g1_ref, win_h,
        lay6_h, gtok6_h, odg_h, odu_h, odd_h, owo_h, owc_h, owi_h, spool_h, small_out,
        a_s, b_s, u_s, r_s, n2_s, n2t_s, cot_s, mg_s, gmix_s,
        act_s, gg_s, gu_s, w0_s, w1_s, w2_s, wo_s, wc_s, tab_s, tabt_s, m1_ref, m2_ref, mult_ref,
        sbg_s, sbu_s, sbd_s, cg_s, cu_s, cd_s,
        dgg_s, dgu_s, xg_s, xu_s, yg_s, yu_s, zg_s, zu_s, d1_s, d2_s, zd_s,
        proj_s, filt_s, ss_s, cs_s, th_s, feat_s, q_s, k_s, v_s, gpre_s,
        c2_s, raw2_s, rd_s, rx_s, ry_s, z2_s, small_s, sgot_s, ssum_s,
        load_sem, w_sem, spool_sem, back_sem, send_sem, recv_sem, local_sem,
    ) = refs
    n, d = n2_s.shape
    t = filt_s.shape[0]
    f = th_s.shape[0]
    isl = kind_ref[0]
    isp = inverse_span(isl, t)
    h = d // 2
    quarter = d // 4
    step48 = d // 16
    dr = h // 4

    dp, me = lax.axis_index("dp"), lax.axis_index("seq")
    core = lax.rem(dp, 2)
    x = lax.rem(lax.rem(dp // 2, side), 2)
    y = lax.rem(dp // (2 * side), 2)
    dp_x = dp + 2 - 4 * x
    dp_y = dp + 2 * side - 4 * side * y
    at_core, at_x, at_y = (dp + 1 - 2 * core, me), (dp_x, me), (dp_y, me)
    at_xy = (dp_x + dp_y - dp, me)
    peers = [lax.rem(me + k, 4) for k in range(4)]
    at_z = [(dp, peers[k]) for k in range(4)]
    half = lax.rem(me, 2)
    at_pair = (dp, me + 1 - 2 * half)
    half_at = pl.ds(pl.multiple_of(half * RB, RB), RB)
    xy = 2 * x + y
    diag, by_x, by_y = 3 - xy, 2 * (1 - x) + y, 2 * x + 1 - y

    def owner(s):
        if isinstance(s, int):
            return (diag, by_x, by_y, xy)[s]
        return 2 * jnp.where(s < 2, 1 - x, x) + jnp.where(lax.rem(s, 2) == 0, 1 - y, y)

    def rows_at(i, size, base=0):
        return pl.ds(pl.multiple_of(base + i * size, math.gcd(size, base) if base else size), size)

    def each(copies, what):
        for c in copies:
            getattr(c, what)()

    row_moves = lambda src, dst: [
        (src.at[0], dst.at[pl.ds(0, t)]),
        (src.at[1, half_at], dst.at[pl.ds(t, RB)]),
    ]
    moves = (
        row_moves(mixed_h, mg_s)
        + row_moves(xs_h, gmix_s)
        + [(wo_h, wo_s)]
        + [(tab_h, tab_s), (tabt_h, tabt_s), (wc_h, wc_s), (proj_h, proj_s)]
    )
    loads = [pltpu.make_async_copy(s, e, load_sem.at[j]) for j, (s, e) in enumerate(moves)]
    slot_moves = [
        (filt_h, filt_s), (ss_h, ss_s), (th_h, th_s), (q_h, q_s),
        (cs_h, cs_s), (feat_h, feat_s), (k_h, k_s), (v_h, v_s),
    ]
    slot_load = lambda slot, j: pltpu.make_async_copy(
        slot_moves[j][0].at[slot], slot_moves[j][1], load_sem.at[11 + j]
    )
    x_loads = [
        pltpu.make_async_copy(a, b, load_sem.at[19 + j])
        for j, (a, b) in enumerate(row_moves(xs_h, cot_s))
    ]

    def weights(s):
        cols = cols_at(owner(s), d)
        return [
            pltpu.make_async_copy(wg_h.at[:, cols], w0_s, w_sem.at[0]),
            pltpu.make_async_copy(wu_h.at[:, cols], w1_s, w_sem.at[1]),
            pltpu.make_async_copy(wd_h.at[cols, :], w2_s, w_sem.at[2]),
        ]

    win_loads = [
        pltpu.make_async_copy(win_h.at[:, k * d : (k + 1) * d], w, w_sem.at[3 + k])
        for k, w in enumerate((w0_s, w1_s, w2_s))
    ]

    each(loads[:5], "start")
    each(weights(3), "start")
    each(loads[5:], "start")
    for j in range(8):
        slot_load(0, j).start()

    barrier = pltpu.get_barrier_semaphore()
    everyone = [at_core, at_x, at_y, at_xy] + at_z[1:]
    for peer in everyone:
        pl.semaphore_signal(barrier, inc=1, device_id=peer, device_id_type=MESH)
    pl.semaphore_wait(barrier, len(everyone))

    causal_masks(m1_ref, m2_ref, isl)
    mult_ref[...] = multiplicity(mult_ref.shape, isl, t)

    def remote(src, dst, peer, j):
        return pltpu.make_async_remote_copy(
            src_ref=src,
            dst_ref=dst,
            send_sem=send_sem.at[j],
            recv_sem=recv_sem.at[j],
            device_id=peer,
            device_id_type=MESH,
        )

    C, DG, XS, YS, ZD, ZG, GA, GC = 0, 12, 20, 22, 24, 27, 36, 45
    LAY, GT0, GT1, PAIR, SMALL, COT, DX, DY, UNIT = 57, 63, 66, 69, 70, 76, 82, 90, 94

    rows128 = lay6_h.shape[1]
    sources = [lax.rem(me + 4 - k, 4) for k in range(4)]
    sends_part = [lax.rem(p, 2) == me // 2 for p in peers]
    gets_part = [half == s // 2 for s in sources]

    def cot_copies(k):
        moves = (
            (cot_h.at[peers[k]], cot_s.at[rows_at(me, rows128)]),
            (cot_h.at[4 + peers[k] // 2], cot_s.at[rows_at(half, rows128, t)]),
        )
        if k == 0:
            return [
                pltpu.make_async_copy(a, b, load_sem.at[9 + j]) for j, (a, b) in enumerate(moves)
            ]
        return [remote(a, b, at_z[k], COT + 2 * (k - 1) + j) for j, (a, b) in enumerate(moves)]

    for k in (1, 2, 3, 0):
        full, part = cot_copies(k)
        full.start()
        pl.when(sends_part[k])(part.start)

    each(loads[:5], "wait")

    @pl.loop(0, n // RB)
    def _(i):
        rows = rows_at(i, RB)
        hid = gmix_s[rows, :].astype(F32) + mm(mg_s[rows, :], wo_s[...])
        a_s[rows, :] = hid
        b_s[rows, :] = jnp.zeros_like(hid)
        u, r = unit_rows(hid)
        u_s[rows, :] = u
        r_s[rows, :] = jnp.broadcast_to(r, (RB, 128))
        n2 = u * g2_ref[...]
        n2_s[rows, :] = n2.astype(BF)
        n2t_s[:, rows] = n2.T.astype(BF)

    pairs = ((sbg_s, cg_s, dgg_s, xg_s, yg_s, zg_s), (sbu_s, cu_s, dgu_s, xu_s, yu_s, zu_s))
    rank_rows = lambda q: pl.ds(q * quarter, quarter)

    def core_copies(s):
        bufs = ((sbg_s, cg_s.at[s]), (sbu_s, cu_s.at[s]), (sbd_s, cd_s.at[owner(s)]))
        return [remote(a, b, at_core, C + 4 * j + s) for j, (a, b) in enumerate(bufs)]

    def diag_copies(odd):
        return [
            remote(p[1].at[0, rank_rows(q)], p[2].at[rank_rows(q)], at_y if odd else at_x, DG + 4 * j + q)
            for j, p in enumerate(pairs)
            for q in ((1, 3) if odd else (0, 2))
        ]

    x_copies = lambda: [remote(p[1].at[1], p[3], at_x, XS + j) for j, p in enumerate(pairs)]
    y_copies = lambda: [remote(p[1].at[2], p[4], at_y, YS + j) for j, p in enumerate(pairs)]

    def down_first(q, peer, k, e):
        return remote(cd_s.at[q, rows_at(k, dr)], d1_s.at[q, e], peer, DX + 2 * q + e)

    def step_sums(s, j):
        p = pairs[j]

        def add_ranks(first):
            for q in (first, first + 2):
                add_into(p[1].at[s, rank_rows(q)], p[2].at[rank_rows(q)])

        @pl.when(s == 0)
        def _():
            each(diag_copies(False)[2 * j : 2 * j + 2], "start")
            each(diag_copies(True)[2 * j : 2 * j + 2], "start")

        @pl.when(s == 1)
        def _():
            each(diag_copies(True)[2 * j : 2 * j + 2], "wait_recv")
            add_ranks(1)
            x_copies()[j].start()

        @pl.when(s == 2)
        def _():
            each(diag_copies(False)[2 * j : 2 * j + 2], "wait_recv")
            add_ranks(0)
            y_copies()[j].start()

    saved = (act_s, gu_s, gg_s)

    def spool(s, i, j):
        rows = rows_at(i, RB)
        return pltpu.make_async_copy(
            saved[j].at[rows], spool_h.at[j, s, rows], spool_sem.at[i, j]
        )

    @pl.loop(0, 4)
    def _(p):
        s = 3 - p
        each(weights(s), "wait")

        @pl.loop(0, n // RB)
        def _(i):
            rows = rows_at(i, RB)

            @pl.when(p > 0)
            def _():
                for j in range(3):
                    spool(s, i, j).wait()

            n2 = n2_s[rows, :]
            pre = mm(n2, w0_s[...])
            lin = mm(n2, w1_s[...])
            sg = 1.0 / (1.0 + jnp.exp(-pre))
            silu = pre * sg
            act = (silu * lin).astype(BF)
            act_s[rows, :] = act
            gu_s[rows, :] = silu.astype(BF)
            gg_s[rows, :] = (lin * sg * (1.0 + pre * (1.0 - sg))).astype(BF)
            a_s[rows, :] += mm(act, w2_s[...])

            @pl.when(p < 3)
            def _():
                for j in range(3):
                    spool(s, i, j).start()

        @pl.when(p < 3)
        def _():
            each(weights(s - 1), "start")

    @pl.loop(0, n // RB)
    def _(i):
        rows = rows_at(i, RB)
        n2_s[rows, :] = a_s[rows, :].astype(BF)

    sends_half = [half == p // 2 for p in peers]
    gets_half = [lax.rem(s, 2) == me // 2 for s in sources]

    def home(buf, out, part, base, k):
        if part == 0:
            src, dst = buf.at[rows_at(peers[k], rows128)], out.at[me]
        else:
            src, dst = buf.at[rows_at(lax.rem(peers[k], 2), rows128, t)], out.at[4 + me // 2]
        if k == 0:
            return pltpu.make_async_copy(src, dst, local_sem.at[base])
        return remote(src, dst, at_z[k], base + k - 1)

    def home_start(buf, out, part, base, local):
        for k in range(4):
            copy = home(buf, out, part, base if k else local, k)
            if part == 0:
                copy.start()
            else:
                pl.when(sends_half[k])(copy.start)

    def home_wait(buf, out, part, base, local):
        for k in range(4):
            copy = home(buf, out, part, base if k else local, k)
            if part == 0:
                copy.wait()
            elif k == 0:
                pl.when(sends_half[0])(copy.wait)
            else:
                pl.when(sends_half[k])(copy.wait_send)
                pl.when(gets_half[k])(copy.wait_recv)

    home_start(n2_s, lay6_h, 0, LAY, 0)
    home_start(n2_s, lay6_h, 1, LAY + 3, 1)

    for k in range(4):
        full, part = cot_copies(k)
        full.wait()
        if k == 0:
            pl.when(sends_part[0])(part.wait)
        else:
            pl.when(sends_part[k])(part.wait_send)
            pl.when(gets_part[k])(part.wait_recv)

    def unspool(s, j):
        return pltpu.make_async_copy(spool_h.at[j, s], saved[j], back_sem.at[j])

    @pl.loop(0, 4)
    def _(s):
        @pl.when(s > 0)
        def _():
            each(weights(s), "wait")
            unspool(s, 1).wait()
            unspool(s, 2).wait()

        @pl.loop(0, n // RB)
        def _(i):
            rows = rows_at(i, RB)
            g_act = mm_nt(cot_s[rows, :], w2_s[...])
            g_up = (g_act * gu_s[rows, :].astype(F32)).astype(BF)
            gu_s[rows, :] = g_up
            g_gate = (g_act * gg_s[rows, :].astype(F32)).astype(BF)
            gg_s[rows, :] = g_gate
            b_s[rows, :] += mm_nt(g_gate, w0_s[...]) + mm_nt(g_up, w1_s[...])

        @pl.when(s < 3)
        def _():
            each(weights(s + 1), "start")

        @pl.when(s > 0)
        def _():
            each(core_copies(s - 1), "wait_send")

        def product(which, j, put):
            cols = cols_at(which, h)

            @pl.loop(0, d // RB)
            def _(i):
                rows, out = rows_at(i, RB), cols_at(i, RB)
                if j == 2:
                    put(slice(None), out, mm_tn(act_s[:, cols], cot_s[:, out]))
                else:
                    put(rows, slice(None), mm(n2t_s[rows, :], (gg_s, gu_s)[j][:, cols]))

        for j, buf in enumerate((sbg_s, sbu_s, sbd_s)):

            def put(rows, cols, value, buf=buf):
                buf[rows, cols] = value.astype(BF)

            if j == 2:
                pl.when(s > 0)(unspool(s, 0).wait)
            product(1 - core, j, put)
            core_copies(s)[j].start()
        for j, (buf, at) in enumerate(((cg_s, s), (cu_s, s), (cd_s, owner(s)))):
            core_copies(s)[j].wait_recv()

            def put(rows, cols, value, buf=buf, at=at):
                buf[at, rows, cols] = (buf[at, rows, cols].astype(F32) + value).astype(BF)

            product(core, j, put)
            pl.when(s < 3)(unspool(s + 1, (2, 1, 0)[j]).start)
            if j < 2:
                step_sums(s, j)

    for q in range(4):
        peer, near = (at_y, by_y) if q % 2 else (at_x, by_x)
        down_first(q, peer, diag, 0).start()
        down_first(q, peer, near, 1).start()

    each(win_loads, "start")
    small_s[...] = jnp.zeros_like(small_s)

    @pl.loop(0, n // RB)
    def _(i):
        rows = rows_at(i, RB)
        g, u = b_s[rows, :], u_s[rows, :]
        small_s[14:15, :] += jnp.sum(g * u, axis=0, keepdims=True)
        gh = cot_s[rows, :].astype(F32) + unit_back(g, u, r_s[rows, 0:1], g2_ref[...])
        gmix_s[rows, :] = gh.astype(BF)

    each(x_loads, "start")
    pair_at = rows_at(half, RB, n)
    mg_s[pair_at, :] = mm_nt(gmix_s[t:, :], wo_s[...]).astype(BF)
    pair_copy = remote(mg_s.at[pair_at], mg_s.at[pair_at], at_pair, PAIR)
    pair_copy.start()

    each(core_copies(3), "wait_send")

    def pos(q):
        return q // 2 + 2 * (q % 2 if isinstance(q, int) else lax.rem(q, 2))

    def reorder(dst, src, which):
        cols = cols_at(which, h)
        for q in range(4):
            for k in range(4):
                to, fr = (4 * k + pos(q)) * step48, (4 * q + k) * step48
                dst[to : to + step48, :] = src[fr : fr + step48, cols].astype(BF)

    def unit_core(u):
        return remote((sbg_s, sbu_s)[u % 2], c2_s.at[u], at_core, UNIT + 15 * u)

    raw_of = lambda u: raw2_s.at[2 if u == 4 else u % 2]
    two = 2 * step48

    def unit_diag(u):
        return [
            remote(
                c2_s.at[u, rows_at(2 * diag + e, two)],
                rd_s.at[u, pl.ds(e * two, two)],
                (at_x, at_y)[e],
                UNIT + 15 * u + 1 + e,
            )
            for e in range(2)
        ]

    def unit_near(u):
        return [
            remote(c2_s.at[u, rows_at(by_x, quarter)], rx_s.at[u], at_x, UNIT + 15 * u + 3),
            remote(c2_s.at[u, rows_at(by_y, quarter)], ry_s.at[u], at_y, UNIT + 15 * u + 4),
        ]

    def unit_rank(q):
        return rows_at(4 * xy + pos(q), step48)

    def unit_z(u):
        return [
            remote(
                c2_s.at[u, unit_rank(peers[k])], z2_s.at[u, k - 1], at_z[k], UNIT + 15 * u + 4 + k
            )
            for k in range(1, 4)
        ]

    def unit_view(u):
        if u in (0, 4):
            out = owc_h if u == 0 else owo_h
            return lambda k, c: out.at[rows_at(k, step48), cols_at(c, h)]
        return lambda k, c: owi_h.at[rows_at(k, step48), cols_at(3 * c + u - 1, h)]

    def unit_gather(u):
        return gather(c2_s.at[u, unit_rank(me)], unit_view(u), UNIT + 15 * u + 8, 5 + u)

    def unit_gather_core(u):
        return gather_core(unit_view(u), UNIT + 15 * u + 11)

    def unit1(u):
        unit_core(u).wait()

        @pl.loop(0, 4)
        def _(k):
            add_into(c2_s.at[u, rows_at(k, quarter)], raw_of(u).at[rows_at(k, quarter)])

        each(unit_diag(u), "start")

    def unit2(u):
        each(unit_diag(u), "wait")
        add_into(c2_s.at[u, rows_at(2 * by_y, two)], rd_s.at[u, 0:two])
        add_into(c2_s.at[u, rows_at(2 * by_x + 1, two)], rd_s.at[u, two : 2 * two])
        each(unit_near(u), "start")

    def unit3(u):
        each(unit_near(u), "wait")
        at = c2_s.at[u, rows_at(xy, quarter)]
        total = at[...].astype(F32) + rx_s[u].astype(F32) + ry_s[u].astype(F32)
        at[...] = total.astype(BF)
        each(unit_z(u), "start")

    def unit4(u):
        each(unit_z(u), "wait")
        at = c2_s.at[u, unit_rank(me)]
        total = at[...].astype(F32)
        for k in range(3):
            total += z2_s[u, k].astype(F32)
        at[...] = total.astype(BF)
        copies, local = unit_gather(u)
        each(copies, "start")
        local.start()

    def unit5(u):
        copies, local = unit_gather(u)
        each(copies, "wait")
        local.wait()
        each(unit_gather_core(u), "start")

    @pl.loop(0, d // RB)
    def _(i):
        a_s[rows_at(i, RB), :] = mm_tn(mg_s[0:n, cols_at(i, RB)], gmix_s[...])

    reorder(sbg_s, a_s, 1 - core)
    unit_core(4).start()
    reorder(raw_of(4), a_s, core)

    each(x_copies(), "wait_recv")
    for p in pairs:

        @pl.loop(0, 4)
        def _(q, p=p):
            add_into(p[1].at[3, rows_at(q, quarter)], p[3].at[rows_at(q, quarter)])

    @pl.loop(0, t // RB)
    def _(i):
        rows = rows_at(i, RB)
        mg_s[rows, :] = mm_nt(gmix_s[rows, :], wo_s[...]).astype(BF)

    def z_copies(j):
        p = pairs[j]
        return [
            remote(p[1].at[3, rows_at(peers[k], quarter)], p[5].at[k - 1], at_z[k], ZG + 3 * j + k - 1)
            for k in range(1, 4)
        ]

    def y_end(j):
        p = pairs[j]
        y_copies()[j].wait_recv()

        @pl.loop(0, 4)
        def _(q):
            add_into(p[1].at[3, rows_at(q, quarter)], p[4].at[rows_at(q, quarter)])

        each(z_copies(j), "start")

    y_end(0)

    down_second = [
        remote(d1_s.at[q, 0], d2_s.at[q], at_x if q % 2 else at_y, DY + q) for q in range(4)
    ]
    down_z = [
        remote(d1_s.at[peers[k], 1], zd_s.at[k - 1], at_z[k], ZD + k - 1) for k in range(1, 4)
    ]

    def down_first_end():
        for q in range(4):
            for e in range(2):
                remote(d1_s.at[q, e], d1_s.at[q, e], at_x, DX + 2 * q + e).wait()
            add_into(d1_s.at[q, 0], cd_s.at[q, rows_at(by_x if q % 2 else by_y, dr)])
            add_into(d1_s.at[q, 1], cd_s.at[q, rows_at(xy, dr)])
        each(down_second, "start")

    def down_second_end():
        each(down_second, "wait")
        for q in range(4):
            add_into(d1_s.at[q, 1], d2_s.at[q])
        each(down_z, "start")

    def gather(src, view, base, first_local):
        return [
            remote(src, view(xy, core), peer, base + k)
            for k, peer in enumerate((at_x, at_y, at_xy))
        ], pltpu.make_async_copy(src, view(xy, core), local_sem.at[first_local])

    def gather_core(view, base):
        return [remote(view(k, core), view(k, core), at_core, base + k) for k in range(4)]

    view_dg = lambda k, c: odg_h.at[:, cols_at(2 * k + c, h)]
    view_du = lambda k, c: odu_h.at[:, cols_at(2 * k + c, h)]
    view_dd = lambda k, c: odd_h.at[rows_at(4 * c + k, dr)]
    gathers = [
        gather(cg_s.at[3, rows_at(me, quarter)], view_dg, GA, 10),
        gather(cu_s.at[3, rows_at(me, quarter)], view_du, GA + 3, 11),
        gather(d1_s.at[me, 1], view_dd, GA + 6, 12),
    ]
    core_gathers = (
        gather_core(view_dg, GC) + gather_core(view_du, GC + 4) + gather_core(view_dd, GC + 8)
    )

    def first_norm(rows):
        u, r = unit_rows(cot_s[rows, :].astype(F32))
        n1t = (u * g1_ref[...]).T.astype(BF)
        for q in range(4):
            for k in range(4):
                to, fr = (4 * k + pos(q)) * step48, (4 * q + k) * step48
                n2t_s[to : to + step48, rows] = n1t[fr : fr + step48]
        return u, r

    def token_rows(slot, rows, at):
        g = mm_nt(proj_s[slot, at, 0:d], w0_s[...])
        g += mm_nt(proj_s[slot, at, d : 2 * d], w1_s[...])
        g += mm_nt(proj_s[slot, at, 2 * d : 3 * d], w2_s[...])
        u, r = first_norm(rows)
        small_s[0:1, :] += jnp.sum(g * u, axis=0, keepdims=True)
        gmix_s[rows, :] = (
            gmix_s[rows, :].astype(F32) + unit_back(g, u, r, g1_ref[...])
        ).astype(BF)

    each(loads[5:], "wait")
    each(x_loads, "wait")

    @pl.loop(0, 2)
    def _(slot):
        share = jnp.where(slot == 0, 1.0, 0.5)
        for j in range(4):
            slot_load(slot, j).wait()
        pl.when(slot == 1)(pair_copy.wait)
        gm_at = pl.ds(pl.multiple_of(slot * n, RB), t)

        @pl.loop(0, d // CB)
        def _(c):
            mult = lanes(mult_ref, CB)
            cols = cols_at(c, CB)
            query = q_s[:, cols].astype(F32)
            gm = mg_s[gm_at, cols].astype(F32)
            a_s[0:t, cols] = gm * filt_s[:, cols].astype(F32)
            spec = mm(tab_s[...], (gm * query).astype(BF)) * isp
            ss = ss_s[:, cols].astype(F32)
            th = th_s[:, cols]
            g_gain = spec[:f] * ss[:f] + spec[f:] * ss[f:]
            g_pre = (g_gain * (1.0 - th * th)).astype(BF)
            gpre_s[:, cols] = g_pre
            weighted = g_pre.astype(F32) * mult
            small_s[13:14, cols] += share * jnp.sum(weighted, axis=0, keepdims=True)
            g = (1.0 + th) * mult
            yy = jnp.concatenate(
                [(g * spec[:f]).astype(BF), (g * spec[f:]).astype(BF)], axis=0
            )
            b_s[0:t, cols] = mm(tabt_s[...], yy)

        @pl.when(slot == 0)
        def _():
            for j in range(4):
                slot_load(1, j).start()
            y_end(1)
            unit1(4)

        @pl.when(slot == 1)
        def _():
            for j, p in enumerate(pairs):
                each(z_copies(j), "wait")
                rows = rows_at(me, quarter)
                total = p[1][3, rows, :].astype(F32)
                for k in range(3):
                    total += p[5][k].astype(F32)
                p[1][3, rows, :] = total.astype(BF)
            for copies, local in gathers[:2]:
                each(copies, "start")
                local.start()
            down_second_end()
            unit3(4)

        for j in range(4, 8):
            slot_load(slot, j).wait()

        @pl.loop(0, d // CB)
        def _(c):
            m1, m2 = lanes(m1_ref, CB), lanes(m2_ref, CB)
            cols = cols_at(c, CB)
            g_feat = mm_nt(gpre_s[...], wc_s[cols, :])
            xc = cs_s[:, cols].astype(F32)
            power = (xc[:f] * xc[:f] + xc[f:] * xc[f:]) * isp
            g_pow = g_feat / (1.0 + power) * (lanes(mult_ref, CB) * (2.0 * isp))
            yy = jnp.concatenate(
                [(g_pow * xc[:f]).astype(BF), (g_pow * xc[f:]).astype(BF)], axis=0
            )
            g_cond = mm(tabt_s[...], yy)
            feat = (feat_s[:, cols].astype(F32) * lanes(mult_ref, CB)).astype(BF)
            dwc = share * mm_tn(feat, gpre_s[...])

            @pl.when(slot == 0)
            def _():
                u_s[cols, :] = dwc

            @pl.when(slot == 1)
            def _():
                u_s[cols, :] += dwc

            def finish(part, g_conv, p):
                at = cols_at(c, CB, part * d)
                back, sums = conv_back(g_conv, p, st_ref[:, at], m1, m2)
                for j in range(3):
                    row = 1 + 3 * j + part
                    small_s[row : row + 1, cols] += share * sums[j]
                proj_s[slot, :, at] = back.astype(BF)

            finish(0, a_s[0:t, cols], proj_s[slot, :, cols].astype(F32))
            key_cols, value_cols = cols_at(c, CB, d), cols_at(c, CB, 2 * d)
            p_value = proj_s[slot, :, value_cols].astype(F32)
            value = v_s[:, cols].astype(F32)
            g_sig = b_s[0:t, cols]
            p_key = proj_s[slot, :, key_cols].astype(F32)
            key = k_s[:, cols].astype(F32)
            finish(1, g_sig * value, p_key)
            back, sums = conv_back(g_cond, value, ct_ref[:, cols], m1, m2)
            for j in range(3):
                small_s[10 + j : 11 + j, cols] += share * sums[j]
            finish(2, g_sig * key + back, p_value)

        @pl.when(slot == 0)
        def _():
            for j in range(4, 8):
                slot_load(1, j).start()
            each(win_loads, "wait")
            down_first_end()
            unit2(4)

            @pl.loop(0, t // RB)
            def _(i):
                token_rows(slot, rows_at(i, RB), rows_at(i, RB))

            home_start(gmix_s, gtok6_h, 0, GT0, 2)

    each(down_z, "wait")
    total = d1_s[me, 1].astype(F32)
    for k in range(3):
        total += zd_s[k].astype(F32)
    d1_s[me, 1] = total.astype(BF)
    each(gathers[2][0], "start")
    gathers[2][1].start()

    def win_product(u, which, dst):
        cols = cols_at(3 * which + u - 1, h)

        @pl.loop(0, d // RB)
        def _(i):
            rows = rows_at(i, RB)
            dw = mm(n2t_s[rows, 0:RB], proj_s[0, 0:RB, cols])
            dw += mm(n2t_s[rows, RB : 2 * RB], proj_s[0, RB : 2 * RB, cols])
            dw += mm(n2t_s[rows, 2 * RB : 3 * RB], proj_s[1, half_at, cols])
            dst[rows, :] = dw.astype(BF)

    reorder(sbg_s, u_s, 1 - core)
    unit_core(0).start()
    reorder(raw_of(0), u_s, core)
    last_rows = slice(t, n)
    first_norm(last_rows)
    unit4(4)
    win_product(1, 1 - core, sbu_s)
    unit_core(1).start()
    win_product(1, core, raw_of(1))
    unit1(0)
    win_product(2, 1 - core, sbg_s)
    unit_core(2).start()
    win_product(2, core, raw_of(2))
    unit1(1)
    unit2(0)
    win_product(3, 1 - core, sbu_s)
    unit_core(3).start()
    win_product(3, core, raw_of(3))
    unit1(2)
    unit2(1)
    unit3(0)
    unit5(4)
    token_rows(1, last_rows, half_at)
    small_c = remote(small_s, sgot_s.at[0], at_core, SMALL)
    small_c.start()
    unit1(3)
    unit2(2)
    unit3(1)
    home_start(gmix_s, gtok6_h, 1, GT1, 3)
    unit4(0)
    small_c.wait()
    ssum_s[0] = small_s[...] + sgot_s[0]
    small_x = remote(ssum_s.at[0], sgot_s.at[1], at_x, SMALL + 1)
    small_x.start()
    unit2(3)
    unit3(2)
    each([c for copies, _ in gathers for c in copies], "wait")
    each([local for _, local in gathers], "wait")
    each(core_gathers, "start")
    unit4(1)
    unit5(0)
    small_x.wait()
    ssum_s[1] = ssum_s[0] + sgot_s[1]
    small_y = remote(ssum_s.at[1], sgot_s.at[2], at_y, SMALL + 2)
    small_y.start()
    unit3(3)
    unit4(2)
    unit5(1)
    small_y.wait()
    ssum_s[2] = ssum_s[1] + sgot_s[2]
    small_z = [
        remote(ssum_s.at[2], sgot_s.at[2 + k], at_z[k], SMALL + 2 + k) for k in range(1, 4)
    ]
    each(small_z, "start")
    unit4(3)
    unit5(2)
    each(small_z, "wait")
    small_out[...] = ssum_s[2] + sgot_s[3] + sgot_s[4] + sgot_s[5]
    unit5(3)

    each(diag_copies(False) + diag_copies(True) + x_copies() + y_copies(), "wait_send")
    each(core_gathers, "wait")
    for u in range(5):
        each(unit_gather_core(u), "wait")
    home_wait(n2_s, lay6_h, 0, LAY, 0)
    home_wait(n2_s, lay6_h, 1, LAY + 3, 1)
    home_wait(gmix_s, gtok6_h, 0, GT0, 2)
    home_wait(gmix_s, gtok6_h, 1, GT1, 3)


def back(
    side, slots, kind, mixed, xs, cot, w_out, g2, w_gate, w_up, w_down,
    proj, filt, ss, cs, th, feat, query, key, value, st, ct, w_cond, table, table_t, g1, w_in,
):
    t, d = xs.shape[1:]
    n = t + t // 2
    f2 = table.shape[0]
    f = f2 // 2
    h, q4, dr, s48 = d // 2, d // 4, d // 8, d // 16
    hbm = pl.BlockSpec(memory_space=pl.ANY)
    vm = pl.BlockSpec(memory_space=pltpu.VMEM)
    smem = pl.BlockSpec(memory_space=pltpu.SMEM)
    b = lambda *s: pltpu.VMEM(s, BF)
    g = lambda *s: pltpu.VMEM(s, F32)
    return pl.pallas_call(
        functools.partial(back_kernel, side),
        name="back",
        out_shape=tuple(
            jax.ShapeDtypeStruct(s, BF)
            for s in (
                (slots, t // 4, d), (slots, t // 4, d), (q4, 4 * d), (q4, 4 * d), (d, d),
                (q4, d), (q4, d), (q4, 3 * d), (3, 4, n, d),
            )
        )
        + (jax.ShapeDtypeStruct((16, d), F32),),
        in_specs=[smem] + [hbm] * 4 + [vm] + [hbm] * 12 + [vm, vm, hbm, hbm, hbm, vm, hbm],
        out_specs=(hbm,) * 9 + (vm,),
        scratch_shapes=[
            g(n, d), g(n, d), g(n, d), g(n, 128),
            b(n, d), b(d, n), b(n, d), b(n + t, d), b(n, d),
            b(n, d), b(n, d), b(n, d), b(d, d), b(d, d), b(d, d), b(d, d), b(d, d),
            b(f2, t), b(t, f2), g(32, 128), g(32, 128), g(f, 128),
            b(d, h), b(d, h), b(h, d),
            b(4, d, h), b(4, d, h), b(4, h, d),
            b(d, h), b(d, h), b(d, h), b(d, h), b(d, h), b(d, h),
            b(3, q4, h), b(3, q4, h), b(4, 2, dr, d), b(4, dr, d), b(3, dr, d),
            b(2, t, 3 * d), b(t, d), b(f2, d), b(f2, d), g(f, d), b(f, d), b(t, d), b(t, d), b(t, d), b(f, d),
            b(5, d, h), b(3, d, h), b(5, q4, h), b(5, q4, h), b(5, q4, h), b(5, 3, s48, h),
            g(16, d), g(6, 16, d), g(3, 16, d),
            pltpu.SemaphoreType.DMA((21,)),
            pltpu.SemaphoreType.DMA((6,)),
            pltpu.SemaphoreType.DMA((3, 3)),
            pltpu.SemaphoreType.DMA((3,)),
            pltpu.SemaphoreType.DMA((169,)),
            pltpu.SemaphoreType.DMA((169,)),
            pltpu.SemaphoreType.DMA((13,)),
        ],
        compiler_params=pltpu.CompilerParams(
            collective_id=1, has_side_effects=True, vmem_limit_bytes=65400 * 1024
        ),
    )(
        kind, mixed, xs, cot, w_out, g2, w_gate, w_up, w_down, proj, filt, ss, cs, th, feat,
        query, key, value, st, ct, w_cond, table, table_t, g1, w_in,
    )


def on_device(
    tokens, kind, ln1_gain, w_in, short_taps, cond_taps, w_cond, cond_bias, w_out, ln2_gain,
    w_gate, w_up, w_down, cotangent,
):
    _, rows, slots, d = tokens.shape
    n = lax.axis_size("seq")
    dp_count = lax.axis_size("dp")
    rank = lax.axis_index("seq")
    tok6 = jnp.transpose(tokens[0], (1, 0, 2))
    cot6 = jnp.transpose(cotangent[0], (1, 0, 2))
    g1, g2 = ln1_gain.reshape(1, d), ln2_gain.reshape(1, d)
    xs, proj, mixed, filt, sig_spec, cond_spec, th, feat, query, key, value, table, table_t = front(
        kind, tok6, g1, w_in, short_taps, cond_taps, w_cond, cond_bias.reshape(1, d)
    )
    side = math.isqrt(dp_count // 2)
    lay6, gtok6, *sums, _, small = back(
        side, slots, kind, mixed, xs, cot6, w_out, g2, w_gate, w_up, w_down,
        proj, filt, sig_spec, cond_spec, th, feat, query, key, value, short_taps, cond_taps, w_cond,
        table, table_t, g1, w_in,
    )
    layer_out = jnp.transpose(lay6, (1, 0, 2))[None]
    grad_tokens = jnp.transpose(gtok6, (1, 0, 2))[None]

    sums = [a.astype(F32) for a in sums]
    if dp_count > 8:
        groups = [
            [
                (y * side + x) * 2 + core
                for y in range(y0, side, 2)
                for x in range(x0, side, 2)
            ]
            for y0 in range(2)
            for x0 in range(2)
            for core in range(2)
        ]
        sums = [lax.psum(a, "dp", axis_index_groups=groups) for a in sums]
        small = lax.psum(small, "dp", axis_index_groups=groups)
    grad_gate, grad_up, grad_down, grad_w_out, grad_w_cond, grad_w_in = sums
    part = lambda a, width: lax.dynamic_slice_in_dim(a, rank * width, width, a.ndim - 1)
    return (
        layer_out,
        grad_tokens,
        part(small[0], d // n),
        grad_w_in,
        part(small[1:10].reshape(3, 3 * d), 3 * d // n),
        part(small[10:13], d // n),
        grad_w_cond,
        part(small[13], d // n),
        grad_w_out,
        part(small[14], d // n),
        grad_gate,
        grad_up,
        grad_down,
    )


def solution(mesh):
    rows = P("dp", "seq", None, None)
    return jax.shard_map(
        on_device,
        mesh=mesh,
        in_specs=(rows, P("dp")) + (P(),) * 11 + (rows,),
        out_specs=(
            rows,
            rows,
            P("seq"),
            P("seq", None),
            P(None, "seq"),
            P(None, "seq"),
            P("seq", None),
            P("seq"),
            P("seq", None),
            P("seq"),
            P("seq", None),
            P("seq", None),
            P("seq", None),
        ),
        check_vma=False,
    )
```

```python
import functools
import math

import jax
import jax.numpy as jnp
from jax import lax
from jax.experimental import pallas as pl
from jax.experimental.pallas import tpu as pltpu
from jax.sharding import PartitionSpec as P

BF = jnp.bfloat16
F32 = jnp.float32
MESH = pl.DeviceIdType.MESH
EPS = 1e-05
CB = 256
FC = 384
RB = 256
VMEM_LIMIT = 60 * 2**20


def mm(a, b):
    return jnp.dot(a, b, preferred_element_type=F32)


def mm_nt(a, b):
    return lax.dot_general(a, b, (((1,), (1,)), ((), ())), preferred_element_type=F32)


def mm_tn(a, b):
    return lax.dot_general(a, b, (((0,), (0,)), ((), ())), preferred_element_type=F32)


def unit_rows(x):
    mean = jnp.mean(x, axis=-1, keepdims=True)
    centered = x - mean
    r = lax.rsqrt(jnp.mean(centered * centered, axis=-1, keepdims=True) + EPS)
    return centered * r, r


def unit_back(g, u, r, gain):
    e = g * gain
    return r * (
        e - jnp.mean(e, axis=-1, keepdims=True) - u * jnp.mean(e * u, axis=-1, keepdims=True)
    )


def lanes(ref, width):
    m = ref[...]
    return jnp.concatenate([m] * (width // m.shape[1]), axis=1)


def down(a, j):
    return pltpu.roll(a, j, axis=0)


def up(a, j):
    return pltpu.roll(a, a.shape[0] - j, axis=0)


def masked(a, m):
    blk = a.shape[0] // 4
    parts = []
    for b in range(4):
        parts.append(a[b * blk : b * blk + 8] * m[8 * b : 8 * b + 8])
        parts.append(a[b * blk + 8 : (b + 1) * blk])
    return jnp.concatenate(parts, axis=0)


def conv(a, taps, m1, m2):
    return taps[0:1] * a + taps[1:2] * masked(down(a, 1), m1) + taps[2:3] * masked(down(a, 2), m2)


def conv_back(g, a, taps, m1, m2):
    g1, g2 = up(masked(g, m1), 1), up(masked(g, m2), 2)
    sums = [jnp.sum(v * a, axis=0, keepdims=True) for v in (g, g1, g2)]
    return taps[0:1] * g + taps[1:2] * g1 + taps[2:3] * g2, sums


def cols_at(c, width, base=0):
    return pl.ds(pl.multiple_of(base + c * width, 128), width)


def short_rows(i, t):
    half = t // 8 + 1
    block = jnp.zeros_like(i)
    for k in range(1, 5):
        block += (i >= k * half).astype(jnp.int32)
    return block, i - half * block


def wave_table(ref, axis, isl, t):
    freqs = ref.shape[axis] // 2
    j = lax.broadcasted_iota(jnp.int32, ref.shape, axis)
    pos = lax.broadcasted_iota(jnp.int32, ref.shape, 1 - axis)
    sin = (j >= freqs).astype(jnp.int32)
    i = j - freqs * sin
    block, f = short_rows(i, t)
    short = t // 4
    phase = isl * (i * pos) + (1 - isl) * (4 * f * (pos & (short - 1)))
    kept_long = (i <= t // 2).astype(jnp.int32)
    kept_short = ((pos >= block * short) & (pos < (block + 1) * short)).astype(jnp.int32)
    kept = isl * kept_long + (1 - isl) * kept_short
    phase = (phase - (t // 4) * sin) & (t - 1)
    angle = (phase - t // 2).astype(F32) * (2.0 * math.pi / t)
    z = angle * angle
    value = jnp.full_like(z, -1.0 / math.factorial(14))
    for k in range(6, -1, -1):
        value = value * z + (-1.0) ** k / math.factorial(2 * k)
    ref[...] = (-value * kept.astype(F32)).astype(ref.dtype)


def multiplicity(shape, isl, t):
    i = lax.broadcasted_iota(jnp.int32, shape, 0)
    block, f = short_rows(i, t)
    once_long = ((i == 0) | (i == t // 2)).astype(jnp.int32)
    once_short = ((f == 0) | (f == t // 8)).astype(jnp.int32)
    long = (2 - once_long) * (i <= t // 2).astype(jnp.int32)
    short = (2 - once_short) * (block < 4).astype(jnp.int32)
    return (isl * long + (1 - isl) * short).astype(F32)


def causal_masks(m1_ref, m2_ref, isl):
    row = lax.broadcasted_iota(jnp.int32, m1_ref.shape, 0)
    place = (row & 7) + isl * (row - (row & 7))
    m1_ref[...] = (place >= 1).astype(F32)
    m2_ref[...] = (place >= 2).astype(F32)


def inverse_span(isl, t):
    long = isl.astype(F32)
    return long * (1.0 / t) + (1.0 - long) * (4.0 / t)


def front_kernel(
    kind_ref, tok_h, g1_ref, win_h, st_ref, ct_ref, wc_h, cb_ref,
    xs_h, proj_h, mixed_h, filt_h, ss_h, sc_h, th_h, feat_h, q_h, k_h, v_h, tab_h, tabt_h,
    x_s, win_s, wc_s, tab_s, tabt_s, m1_ref, m2_ref, ms_s, n1_s, q_s,
    proj_s, mixed_s, filt_s, ss_s, sc_s, th_s, feat_s, qb_s, k_s, v_s,
    load_sem, out_sem, send_sem, recv_sem,
):
    t, d = n1_s.shape
    f = ms_s.shape[0]
    n = 4
    blk = t // n
    dp, me = lax.axis_index("dp"), lax.axis_index("seq")
    peers = [lax.rem(me + k, n) for k in range(n)]
    half = lax.rem(me, 2)
    pair = me + 1 - 2 * half
    isl = kind_ref[0]
    isp = inverse_span(isl, t)

    block = lambda i: pl.ds(pl.multiple_of(i * blk, blk), blk)
    loads = [
        pltpu.make_async_copy(win_h, win_s, load_sem.at[0]),
        pltpu.make_async_copy(wc_h, wc_s, load_sem.at[1]),
        pltpu.make_async_copy(tok_h.at[me], x_s.at[0, block(me)], load_sem.at[2]),
        pltpu.make_async_copy(tok_h.at[n + me // 2], x_s.at[1, block(me)], load_sem.at[3]),
    ]

    barrier = pltpu.get_barrier_semaphore()
    for k in range(1, n):
        pl.semaphore_signal(barrier, inc=1, device_id=(dp, peers[k]), device_id_type=MESH)
    pl.semaphore_wait(barrier, n - 1)

    def remote(src, dst, peer, j):
        return pltpu.make_async_remote_copy(
            src_ref=src,
            dst_ref=dst,
            send_sem=send_sem.at[j],
            recv_sem=recv_sem.at[j],
            device_id=(dp, peer),
            device_id_type=MESH,
        )

    whole_slot = [
        remote(tok_h.at[peers[k]], x_s.at[0, block(me)], peers[k], k - 1) for k in range(1, n)
    ]
    to_pair = remote(tok_h.at[n + me // 2], x_s.at[1, block(me)], pair, 3)
    across = remote(tok_h.at[n + peers[2] // 2], x_s.at[1, block(me)], peers[2], 4)
    handed = remote(x_s.at[1, block(peers[2])], x_s.at[1, block(peers[2])], pair, 5)
    for c in whole_slot + [across, to_pair]:
        c.start()
    for c in loads:
        c.start()

    wave_table(tab_s, 0, isl, t)
    wave_table(tabt_s, 1, isl, t)
    causal_masks(m1_ref, m2_ref, isl)
    ms_s[...] = multiplicity(ms_s.shape, isl, t) * isp

    for c in loads[:4]:
        c.wait()
    for c in whole_slot:
        c.wait()

    outs = [
        (x_s, xs_h), (proj_s, proj_h), (ss_s, ss_h), (sc_s, sc_h), (feat_s, feat_h),
        (qb_s, q_h), (k_s, k_h), (v_s, v_h),
        (mixed_s, mixed_h), (filt_s, filt_h), (th_s, th_h),
    ]

    def out_copy(slot, j):
        return pltpu.make_async_copy(outs[j][0].at[slot], outs[j][1].at[slot], out_sem.at[slot, j])

    tables = [
        pltpu.make_async_copy(tab_s, tab_h, load_sem.at[4]),
        pltpu.make_async_copy(tabt_s, tabt_h, load_sem.at[5]),
    ]
    for c in tables:
        c.start()

    @pl.loop(0, 2)
    def _(slot):
        @pl.when(slot == 1)
        def _():
            to_pair.wait()
            handed.wait()

        @pl.loop(0, t // 128)
        def _(r):
            rows = pl.ds(pl.multiple_of(r * 128, 128), 128)
            u, _ = unit_rows(x_s[slot, rows, :].astype(F32))
            n1_s[rows, :] = (u * g1_ref[...].reshape(1, d)).astype(BF)

        @pl.loop(0, d // d)
        def _(c):
            m1, m2 = lanes(m1_ref, d), lanes(m2_ref, d)
            own = cols_at(c, d)

            def part(k):
                cols = cols_at(c, d, k * d)
                p = mm(n1_s[...], win_s[:, cols]).astype(BF)
                proj_s[slot, k, :, own] = p
                return conv(p.astype(F32), st_ref[:, cols], m1, m2)

            query = part(0)
            q_s[:, own] = query
            qb_s[slot, :, own] = query.astype(BF)
            key = part(1)
            k_s[slot, :, own] = key.astype(BF)
            value = part(2).astype(BF)
            v_s[slot, :, own] = value
            value_f = value.astype(F32)
            signal = (key * value_f).astype(BF)
            ss_s[slot, :, own] = mm(tab_s[...], signal).astype(BF)
            cond = conv(value_f, ct_ref[:, own], m1, m2).astype(BF)
            xc = mm(tab_s[...], cond)
            sc_s[slot, :, own] = xc.astype(BF)
            power = (xc[:f] * xc[:f] + xc[f:] * xc[f:]) * isp
            feat_s[slot, :, own] = jnp.log1p(power).astype(BF)

        for j in range(8):
            out_copy(slot, j).start()

        @pl.when(slot == 0)
        def _():
            across.wait()
            handed.start()

        @pl.loop(0, d // d)
        def _(c):
            own = cols_at(c, d)
            th = jnp.tanh(mm(feat_s[slot], wc_s[:, own]) + cb_ref[...].reshape(1, d))
            th_s[slot, :, own] = th
            g = (1.0 + th) * lanes(ms_s, d)
            xs = ss_s[slot, :, own].astype(F32)
            y = jnp.concatenate([(g * xs[:f]).astype(BF), (g * xs[f:]).astype(BF)], axis=0)
            filt = mm(tabt_s[...], y)
            filt_s[slot, :, own] = filt.astype(BF)
            mixed_s[slot, :, own] = (q_s[:, own] * filt).astype(BF)

        for j in range(8, 11):
            out_copy(slot, j).start()

    for slot in range(2):
        for j in range(11):
            out_copy(slot, j).wait()
    for c in tables:
        c.wait()


def front(kind, tok, g1, w_in, st, ct, w_cond, cb):
    slots, blk, d = tok.shape
    t = 4 * blk
    f = -(-max(t // 2 + 1, 4 * (blk // 2 + 1)) // 16) * 16
    hbm = pl.BlockSpec(memory_space=pl.ANY)
    vm = pl.BlockSpec(memory_space=pltpu.VMEM)
    smem = pl.BlockSpec(memory_space=pltpu.SMEM)
    per_slot = [
        ((2, t, d), BF), ((2, 3, t, d), BF), ((2, t, d), BF), ((2, t, d), BF),
        ((2, 2 * f, d), BF), ((2, 2 * f, d), BF), ((2, f, d), F32), ((2, f, d), BF),
        ((2, t, d), BF), ((2, t, d), BF), ((2, t, d), BF),
    ]
    xs, *rest = [jax.ShapeDtypeStruct(*s) for s in per_slot]
    tables = [((2 * f, t), BF), ((t, 2 * f), BF)]
    return pl.pallas_call(
        front_kernel,
        name="front",
        out_shape=(xs, *rest)
        + tuple(jax.ShapeDtypeStruct(*s) for s in tables),
        in_specs=[smem, hbm, vm, hbm, vm, vm, hbm, vm],
        out_specs=(hbm,) * 13,
        scratch_shapes=[
            pltpu.VMEM((2, t, d), BF), pltpu.VMEM((d, 3 * d), BF), pltpu.VMEM((d, d), BF),
            pltpu.VMEM(*tables[0]), pltpu.VMEM(*tables[1]),
            pltpu.VMEM((32, 128), F32), pltpu.VMEM((32, 128), F32), pltpu.VMEM((f, 128), F32),
            pltpu.VMEM((t, d), BF), pltpu.VMEM((t, d), F32),
        ]
        + [pltpu.VMEM(*s) for s in per_slot[1:]]
        + [
            pltpu.SemaphoreType.DMA((6,)),
            pltpu.SemaphoreType.DMA((2, 11)),
            pltpu.SemaphoreType.DMA((6,)),
            pltpu.SemaphoreType.DMA((6,)),
        ],
        compiler_params=pltpu.CompilerParams(
            collective_id=0, has_side_effects=True, vmem_limit_bytes=VMEM_LIMIT
        ),
    )(kind, tok, g1, w_in, st, ct, w_cond, cb)


def add_into(dst, src):
    dst[...] = (dst[...].astype(F32) + src[...].astype(F32)).astype(dst.dtype)


def back_kernel(side, *refs):
    (
        kind_ref, mixed_h, xs_h, cot_h, wo_h, g2_ref, wg_h, wu_h, wd_h,
        proj_h, filt_h, ss_h, cs_h, th_h, feat_h, q_h, k_h, v_h,
        st_ref, ct_ref, wc_h, tab_h, tabt_h, g1_ref, win_h,
        lay6_h, gtok6_h, odg_h, odu_h, odd_h, owo_h, owc_h, owi_h, spool_h, small_out,
        a_s, b_s, u_s, r_s, n2_s, n2t_s, cot_s, mg_s, gmix_s,
        act_s, gg_s, gu_s, wall_s, wo_s, wc_s, tab_s, tabt_s, m1_ref, m2_ref, mult_ref,
        sbg_s, sbu_s, sbd_s, cg_s, cu_s, cd_s,
        dgg_s, dgu_s, xg_s, xu_s, yg_s, yu_s, zg_s, zu_s, d1_s, d2_s, zd_s,
        filt_s, ss_s, cs_s, th_s, feat_s, q_s, k_s, v_s, gpre_s,
        c2_s, raw2_s, rd_s, rx_s, ry_s, z2_s, small_s, sgot_s, ssum_s,
        load_sem, w_sem, spool_sem, back_sem, send_sem, recv_sem, local_sem,
    ) = refs
    n, d = n2_s.shape
    t = filt_s.shape[0]
    f = th_s.shape[0]
    isl = kind_ref[0]
    isp = inverse_span(isl, t)
    h = d // 2
    quarter = d // 4
    step48 = d // 16
    dr = h // 4

    dp, me = lax.axis_index("dp"), lax.axis_index("seq")
    core = lax.rem(dp, 2)
    x = lax.rem(lax.rem(dp // 2, side), 2)
    y = lax.rem(dp // (2 * side), 2)
    dp_x = dp + 2 - 4 * x
    dp_y = dp + 2 * side - 4 * side * y
    at_core, at_x, at_y = (dp + 1 - 2 * core, me), (dp_x, me), (dp_y, me)
    at_xy = (dp_x + dp_y - dp, me)
    peers = [lax.rem(me + k, 4) for k in range(4)]
    at_z = [(dp, peers[k]) for k in range(4)]
    half = lax.rem(me, 2)
    at_pair = (dp, me + 1 - 2 * half)
    half_at = pl.ds(pl.multiple_of(half * RB, RB), RB)
    xy = 2 * x + y
    diag, by_x, by_y = 3 - xy, 2 * (1 - x) + y, 2 * x + 1 - y

    def owner(s):
        if isinstance(s, int):
            return (diag, by_x, by_y, xy)[s]
        return 2 * jnp.where(s < 2, 1 - x, x) + jnp.where(lax.rem(s, 2) == 0, 1 - y, y)

    def rows_at(i, size, base=0):
        return pl.ds(pl.multiple_of(base + i * size, math.gcd(size, base) if base else size), size)

    def each(copies, what):
        for c in copies:
            getattr(c, what)()

    row_moves = lambda src, dst: [
        (src.at[0], dst.at[pl.ds(0, t)]),
        (src.at[1, half_at], dst.at[pl.ds(t, RB)]),
    ]
    moves = (
        row_moves(mixed_h, mg_s)
        + row_moves(xs_h, gmix_s)
        + [(wo_h, wo_s)]
        + [(tab_h, tab_s), (tabt_h, tabt_s), (wc_h, wc_s)]
        + [(proj_h, wall_s.at[pl.ds(3 * d, 6 * t)])]
    )
    loads = [pltpu.make_async_copy(s, e, load_sem.at[j]) for j, (s, e) in enumerate(moves)]
    slot_moves = [
        (filt_h, filt_s), (ss_h, ss_s), (th_h, th_s), (q_h, q_s),
        (cs_h, cs_s), (feat_h, feat_s), (k_h, k_s), (v_h, v_s),
    ]
    slot_load = lambda slot, j: pltpu.make_async_copy(
        slot_moves[j][0].at[slot], slot_moves[j][1], load_sem.at[11 + j]
    )
    x_loads = [
        pltpu.make_async_copy(a, b, load_sem.at[19 + j])
        for j, (a, b) in enumerate(row_moves(xs_h, cot_s))
    ]

    def weight(k, b):
        return pl.ds(pl.multiple_of((3 * b + k) * d, RB), d)

    def weights(s, b):
        cols = cols_at(owner(s), d)
        return [
            pltpu.make_async_copy(src, wall_s.at[weight(k, b)], w_sem.at[b, k])
            for k, src in enumerate((wg_h.at[:, cols], wu_h.at[:, cols], wd_h.at[cols, :]))
        ]

    win_loads = [
        pltpu.make_async_copy(
            win_h.at[:, k * d : (k + 1) * d], wall_s.at[weight(k, 0)], w_sem.at[2, k]
        )
        for k in range(3)
    ]

    def proj_rows(slot, part, offset, size):
        return pl.ds(pl.multiple_of(3 * d + (3 * slot + part) * t + offset, RB), size)

    each(loads[:5], "start")
    each(weights(3, 0), "start")

    barrier = pltpu.get_barrier_semaphore()
    everyone = [at_core, at_x, at_y, at_xy] + at_z[1:]
    for peer in everyone:
        pl.semaphore_signal(barrier, inc=1, device_id=peer, device_id_type=MESH)
    pl.semaphore_wait(barrier, len(everyone))

    causal_masks(m1_ref, m2_ref, isl)
    mult_ref[...] = multiplicity(mult_ref.shape, isl, t)

    def remote(src, dst, peer, j):
        return pltpu.make_async_remote_copy(
            src_ref=src,
            dst_ref=dst,
            send_sem=send_sem.at[j],
            recv_sem=recv_sem.at[j],
            device_id=peer,
            device_id_type=MESH,
        )

    C, DG, XS, YS, ZD, ZG, GA, GC = 0, 12, 20, 22, 24, 27, 36, 45
    LAY, GT0, GT1, PAIR, SMALL, COT, DX, DY, UNIT = 57, 63, 66, 69, 70, 76, 82, 90, 94

    rows128 = lay6_h.shape[1]
    sources = [lax.rem(me + 4 - k, 4) for k in range(4)]
    sends_part = [lax.rem(p, 2) == me // 2 for p in peers]
    gets_part = [half == s // 2 for s in sources]

    def cot_copies(k):
        moves = (
            (cot_h.at[peers[k]], cot_s.at[rows_at(me, rows128)]),
            (cot_h.at[4 + peers[k] // 2], cot_s.at[rows_at(half, rows128, t)]),
        )
        if k == 0:
            return [
                pltpu.make_async_copy(a, b, load_sem.at[9 + j]) for j, (a, b) in enumerate(moves)
            ]
        return [remote(a, b, at_z[k], COT + 2 * (k - 1) + j) for j, (a, b) in enumerate(moves)]

    for k in (1, 2, 3, 0):
        full, part = cot_copies(k)
        full.start()
        pl.when(sends_part[k])(part.start)

    each(loads[:5], "wait")

    @pl.loop(0, n // RB)
    def _(i):
        rows = rows_at(i, RB)
        hid = gmix_s[rows, :].astype(F32) + mm(mg_s[rows, :], wo_s[...])
        a_s[rows, :] = hid
        b_s[rows, :] = jnp.zeros_like(hid)
        u, r = unit_rows(hid)
        u_s[rows, :] = u
        r_s[rows, :] = jnp.broadcast_to(r, (RB, 128))
        n2 = u * g2_ref[...].reshape(1, d)
        n2_s[rows, :] = n2.astype(BF)
        n2t_s[:, rows] = n2.T.astype(BF)

    each(loads[5:-1], "start")
    for j in range(8):
        slot_load(0, j).start()

    pairs = ((sbg_s, cg_s, dgg_s, xg_s, yg_s, zg_s), (sbu_s, cu_s, dgu_s, xu_s, yu_s, zu_s))
    rank_rows = lambda q: pl.ds(q * quarter, quarter)

    def core_copies(s):
        bufs = ((sbg_s, cg_s.at[s]), (sbu_s, cu_s.at[s]), (sbd_s, cd_s.at[owner(s)]))
        return [remote(a, b, at_core, C + 4 * j + s) for j, (a, b) in enumerate(bufs)]

    def diag_copies(odd):
        return [
            remote(p[1].at[0, rank_rows(q)], p[2].at[rank_rows(q)], at_y if odd else at_x, DG + 4 * j + q)
            for j, p in enumerate(pairs)
            for q in ((1, 3) if odd else (0, 2))
        ]

    x_copies = lambda: [remote(p[1].at[1], p[3], at_x, XS + j) for j, p in enumerate(pairs)]
    y_copies = lambda: [remote(p[1].at[2], p[4], at_y, YS + j) for j, p in enumerate(pairs)]

    def down_first(q, peer, k, e):
        return remote(cd_s.at[q, rows_at(k, dr)], d1_s.at[q, e], peer, DX + 2 * q + e)

    def step_sums(s, j):
        p = pairs[j]

        def add_ranks(first):
            for q in (first, first + 2):
                add_into(p[1].at[s, rank_rows(q)], p[2].at[rank_rows(q)])

        @pl.when(s == 0)
        def _():
            each(diag_copies(False)[2 * j : 2 * j + 2], "start")
            each(diag_copies(True)[2 * j : 2 * j + 2], "start")

        @pl.when(s == 1)
        def _():
            each(diag_copies(True)[2 * j : 2 * j + 2], "wait_recv")
            add_ranks(1)
            x_copies()[j].start()

        @pl.when(s == 2)
        def _():
            each(diag_copies(False)[2 * j : 2 * j + 2], "wait_recv")
            add_ranks(0)
            y_copies()[j].start()

    saved = (act_s, gu_s, gg_s)

    def spool(s, i, j):
        rows = rows_at(i, RB)
        return pltpu.make_async_copy(
            saved[j].at[rows], spool_h.at[j, s, rows], spool_sem.at[i, j]
        )

    @pl.loop(0, 4)
    def _(p):
        s, b = 3 - p, lax.rem(p, 2)
        each(weights(s, b), "wait")

        @pl.when(p < 3)
        def _():
            each(weights(s - 1, 1 - b), "start")

        @pl.loop(0, n // RB)
        def _(i):
            rows = rows_at(i, RB)

            @pl.when(p > 0)
            def _():
                for j in range(3):
                    spool(s, i, j).wait()

            n2 = n2_s[rows, :]
            pre = mm(n2, wall_s[weight(0, b), :])
            lin = mm(n2, wall_s[weight(1, b), :])
            sg = 1.0 / (1.0 + jnp.exp(-pre))
            silu = pre * sg
            act = (silu * lin).astype(BF)
            act_s[rows, :] = act
            gu_s[rows, :] = silu.astype(BF)
            gg_s[rows, :] = (lin * sg * (1.0 + pre * (1.0 - sg))).astype(BF)
            a_s[rows, :] += mm(act, wall_s[weight(2, b), :])

            @pl.when(p < 3)
            def _():
                for j in range(3):
                    spool(s, i, j).start()

    @pl.loop(0, n // RB)
    def _(i):
        rows = rows_at(i, RB)
        n2_s[rows, :] = a_s[rows, :].astype(BF)

    sends_half = [half == p // 2 for p in peers]
    gets_half = [lax.rem(s, 2) == me // 2 for s in sources]

    def home(buf, out, part, base, k):
        if part == 0:
            src, dst = buf.at[rows_at(peers[k], rows128)], out.at[me]
        else:
            src, dst = buf.at[rows_at(lax.rem(peers[k], 2), rows128, t)], out.at[4 + me // 2]
        if k == 0:
            return pltpu.make_async_copy(src, dst, local_sem.at[base])
        return remote(src, dst, at_z[k], base + k - 1)

    def home_start(buf, out, part, base, local):
        for k in range(4):
            copy = home(buf, out, part, base if k else local, k)
            if part == 0:
                copy.start()
            else:
                pl.when(sends_half[k])(copy.start)

    def home_wait(buf, out, part, base, local):
        for k in range(4):
            copy = home(buf, out, part, base if k else local, k)
            if part == 0:
                copy.wait()
            elif k == 0:
                pl.when(sends_half[0])(copy.wait)
            else:
                pl.when(sends_half[k])(copy.wait_send)
                pl.when(gets_half[k])(copy.wait_recv)

    home_start(n2_s, lay6_h, 0, LAY, 0)
    home_start(n2_s, lay6_h, 1, LAY + 3, 1)

    for k in range(4):
        full, part = cot_copies(k)
        full.wait()
        if k == 0:
            pl.when(sends_part[0])(part.wait)
        else:
            pl.when(sends_part[k])(part.wait_send)
            pl.when(gets_part[k])(part.wait_recv)

    def unspool(s, j):
        return pltpu.make_async_copy(spool_h.at[j, s], saved[j], back_sem.at[j])

    @pl.loop(0, 4)
    def _(s):
        b = lax.rem(s + 1, 2)

        @pl.when(s > 0)
        def _():
            each(weights(s, b), "wait")

        @pl.when(s < 3)
        def _():
            each(weights(s + 1, 1 - b), "start")

        pl.when(s == 3)(loads[-1].start)

        @pl.when(s > 0)
        def _():
            unspool(s, 1).wait()
            unspool(s, 2).wait()

        @pl.loop(0, n // RB)
        def _(i):
            rows = rows_at(i, RB)
            g_act = mm_nt(cot_s[rows, :], wall_s[weight(2, b), :])
            g_up = (g_act * gu_s[rows, :].astype(F32)).astype(BF)
            gu_s[rows, :] = g_up
            g_gate = (g_act * gg_s[rows, :].astype(F32)).astype(BF)
            gg_s[rows, :] = g_gate
            b_s[rows, :] += mm_nt(g_gate, wall_s[weight(0, b), :]) + mm_nt(
                g_up, wall_s[weight(1, b), :]
            )

        @pl.when(s > 0)
        def _():
            each(core_copies(s - 1), "wait_send")

        def product(which, j, put):
            cols = cols_at(which, h)

            @pl.loop(0, d // RB)
            def _(i):
                rows, out = rows_at(i, RB), cols_at(i, RB)
                if j == 2:
                    put(slice(None), out, mm_tn(act_s[:, cols], cot_s[:, out]))
                else:
                    put(rows, slice(None), mm(n2t_s[rows, :], (gg_s, gu_s)[j][:, cols]))

        for j, buf in enumerate((sbg_s, sbu_s, sbd_s)):

            def put(rows, cols, value, buf=buf):
                buf[rows, cols] = value.astype(BF)

            if j == 2:
                pl.when(s > 0)(unspool(s, 0).wait)
            product(1 - core, j, put)
            core_copies(s)[j].start()
        for j, (buf, at) in enumerate(((cg_s, s), (cu_s, s), (cd_s, owner(s)))):
            core_copies(s)[j].wait_recv()

            def put(rows, cols, value, buf=buf, at=at):
                buf[at, rows, cols] = (buf[at, rows, cols].astype(F32) + value).astype(BF)

            product(core, j, put)
            pl.when(s < 3)(unspool(s + 1, (2, 1, 0)[j]).start)
            if j < 2:
                step_sums(s, j)

    for q in range(4):
        peer, near = (at_y, by_y) if q % 2 else (at_x, by_x)
        down_first(q, peer, diag, 0).start()
        down_first(q, peer, near, 1).start()

    each(win_loads, "start")
    small_s[...] = jnp.zeros_like(small_s)

    @pl.loop(0, n // RB)
    def _(i):
        rows = rows_at(i, RB)
        g, u = b_s[rows, :], u_s[rows, :]
        small_s[14:15, :] += jnp.sum(g * u, axis=0, keepdims=True)
        gh = cot_s[rows, :].astype(F32) + unit_back(g, u, r_s[rows, 0:1], g2_ref[...].reshape(1, d))
        gmix_s[rows, :] = gh.astype(BF)

    each(x_loads, "start")
    pair_at = rows_at(half, RB, n)
    mg_s[pair_at, :] = mm_nt(gmix_s[t:, :], wo_s[...]).astype(BF)
    pair_copy = remote(mg_s.at[pair_at], mg_s.at[pair_at], at_pair, PAIR)
    pair_copy.start()

    each(core_copies(3), "wait_send")

    def pos(q):
        return q // 2 + 2 * (q % 2 if isinstance(q, int) else lax.rem(q, 2))

    def reorder(dst, src, which):
        cols = cols_at(which, h)
        for q in range(4):
            for k in range(4):
                to, fr = (4 * k + pos(q)) * step48, (4 * q + k) * step48
                dst[to : to + step48, :] = src[fr : fr + step48, cols].astype(BF)

    def unit_core(u):
        return remote((sbg_s, sbu_s)[u % 2], c2_s.at[u], at_core, UNIT + 15 * u)

    raw_of = lambda u: raw2_s.at[2 if u == 4 else u % 2]
    two = 2 * step48

    def unit_diag(u):
        return [
            remote(
                c2_s.at[u, rows_at(2 * diag + e, two)],
                rd_s.at[u, pl.ds(e * two, two)],
                (at_x, at_y)[e],
                UNIT + 15 * u + 1 + e,
            )
            for e in range(2)
        ]

    def unit_near(u):
        return [
            remote(c2_s.at[u, rows_at(by_x, quarter)], rx_s.at[u], at_x, UNIT + 15 * u + 3),
            remote(c2_s.at[u, rows_at(by_y, quarter)], ry_s.at[u], at_y, UNIT + 15 * u + 4),
        ]

    def unit_rank(q):
        return rows_at(4 * xy + pos(q), step48)

    def unit_z(u):
        return [
            remote(
                c2_s.at[u, unit_rank(peers[k])], z2_s.at[u, k - 1], at_z[k], UNIT + 15 * u + 4 + k
            )
            for k in range(1, 4)
        ]

    def unit_view(u):
        if u in (0, 4):
            out = owc_h if u == 0 else owo_h
            return lambda k, c: out.at[rows_at(k, step48), cols_at(c, h)]
        return lambda k, c: owi_h.at[rows_at(k, step48), cols_at(3 * c + u - 1, h)]

    def unit_gather(u):
        return gather(c2_s.at[u, unit_rank(me)], unit_view(u), UNIT + 15 * u + 8, 5 + u)

    def unit_gather_core(u):
        return gather_core(unit_view(u), UNIT + 15 * u + 11)

    def unit1(u):
        unit_core(u).wait()

        @pl.loop(0, 4)
        def _(k):
            add_into(c2_s.at[u, rows_at(k, quarter)], raw_of(u).at[rows_at(k, quarter)])

        each(unit_diag(u), "start")

    def unit2(u):
        each(unit_diag(u), "wait")
        add_into(c2_s.at[u, rows_at(2 * by_y, two)], rd_s.at[u, 0:two])
        add_into(c2_s.at[u, rows_at(2 * by_x + 1, two)], rd_s.at[u, two : 2 * two])
        each(unit_near(u), "start")

    def unit3(u):
        each(unit_near(u), "wait")
        at = c2_s.at[u, rows_at(xy, quarter)]
        total = at[...].astype(F32) + rx_s[u].astype(F32) + ry_s[u].astype(F32)
        at[...] = total.astype(BF)
        each(unit_z(u), "start")

    def unit4(u):
        each(unit_z(u), "wait")
        at = c2_s.at[u, unit_rank(me)]
        total = at[...].astype(F32)
        for k in range(3):
            total += z2_s[u, k].astype(F32)
        at[...] = total.astype(BF)
        copies, local = unit_gather(u)
        each(copies, "start")
        local.start()

    def unit5(u):
        copies, local = unit_gather(u)
        each(copies, "wait")
        local.wait()
        each(unit_gather_core(u), "start")

    @pl.loop(0, d // RB)
    def _(i):
        a_s[rows_at(i, RB), :] = mm_tn(mg_s[0:n, cols_at(i, RB)], gmix_s[...])

    reorder(sbg_s, a_s, 1 - core)
    unit_core(4).start()
    reorder(raw_of(4), a_s, core)

    each(x_copies(), "wait_recv")
    for p in pairs:

        @pl.loop(0, 4)
        def _(q, p=p):
            add_into(p[1].at[3, rows_at(q, quarter)], p[3].at[rows_at(q, quarter)])

    @pl.loop(0, t // RB)
    def _(i):
        rows = rows_at(i, RB)
        mg_s[rows, :] = mm_nt(gmix_s[rows, :], wo_s[...]).astype(BF)

    def z_copies(j):
        p = pairs[j]
        return [
            remote(p[1].at[3, rows_at(peers[k], quarter)], p[5].at[k - 1], at_z[k], ZG + 3 * j + k - 1)
            for k in range(1, 4)
        ]

    def y_end(j):
        p = pairs[j]
        y_copies()[j].wait_recv()

        @pl.loop(0, 4)
        def _(q):
            add_into(p[1].at[3, rows_at(q, quarter)], p[4].at[rows_at(q, quarter)])

        each(z_copies(j), "start")

    y_end(0)

    down_second = [
        remote(d1_s.at[q, 0], d2_s.at[q], at_x if q % 2 else at_y, DY + q) for q in range(4)
    ]
    down_z = [
        remote(d1_s.at[peers[k], 1], zd_s.at[k - 1], at_z[k], ZD + k - 1) for k in range(1, 4)
    ]

    def down_first_end():
        for q in range(4):
            for e in range(2):
                remote(d1_s.at[q, e], d1_s.at[q, e], at_x, DX + 2 * q + e).wait()
            add_into(d1_s.at[q, 0], cd_s.at[q, rows_at(by_x if q % 2 else by_y, dr)])
            add_into(d1_s.at[q, 1], cd_s.at[q, rows_at(xy, dr)])
        each(down_second, "start")

    def down_second_end():
        each(down_second, "wait")
        for q in range(4):
            add_into(d1_s.at[q, 1], d2_s.at[q])
        each(down_z, "start")

    def gather(src, view, base, first_local):
        return [
            remote(src, view(xy, core), peer, base + k)
            for k, peer in enumerate((at_x, at_y, at_xy))
        ], pltpu.make_async_copy(src, view(xy, core), local_sem.at[first_local])

    def gather_core(view, base):
        return [remote(view(k, core), view(k, core), at_core, base + k) for k in range(4)]

    view_dg = lambda k, c: odg_h.at[:, cols_at(2 * k + c, h)]
    view_du = lambda k, c: odu_h.at[:, cols_at(2 * k + c, h)]
    view_dd = lambda k, c: odd_h.at[rows_at(4 * c + k, dr)]
    gathers = [
        gather(cg_s.at[3, rows_at(me, quarter)], view_dg, GA, 10),
        gather(cu_s.at[3, rows_at(me, quarter)], view_du, GA + 3, 11),
        gather(d1_s.at[me, 1], view_dd, GA + 6, 12),
    ]
    core_gathers = (
        gather_core(view_dg, GC) + gather_core(view_du, GC + 4) + gather_core(view_dd, GC + 8)
    )

    def keep_norm(u, rows):
        n1t = (u * g1_ref[...].reshape(1, d)).T.astype(BF)
        for q in range(4):
            for k in range(4):
                to, fr = (4 * k + pos(q)) * step48, (4 * q + k) * step48
                n2t_s[to : to + step48, rows] = n1t[fr : fr + step48]

    def token_rows(slot, rows, offset, u, r):
        g = jnp.zeros((RB, d), F32)
        for part in range(3):
            g += mm_nt(wall_s[proj_rows(slot, part, offset, RB), :], wall_s[weight(part, 0), :])
        small_s[0:1, :] += jnp.sum(g * u, axis=0, keepdims=True)
        gmix_s[rows, :] = (
            gmix_s[rows, :].astype(F32) + unit_back(g, u, r, g1_ref[...].reshape(1, d))
        ).astype(BF)

    each(loads[5:], "wait")
    each(x_loads, "wait")

    @pl.loop(0, 2)
    def _(slot):
        share = jnp.where(slot == 0, 1.0, 0.5)
        for j in range(4):
            slot_load(slot, j).wait()
        pl.when(slot == 1)(pair_copy.wait)
        gm_at = pl.ds(pl.multiple_of(slot * n, RB), t)

        @pl.loop(0, d // CB)
        def _(c):
            mult = lanes(mult_ref, CB)
            cols = cols_at(c, CB)
            query = q_s[:, cols].astype(F32)
            gm = mg_s[gm_at, cols].astype(F32)
            a_s[0:t, cols] = gm * filt_s[:, cols].astype(F32)
            spec = mm(tab_s[...], (gm * query).astype(BF)) * isp
            ss = ss_s[:, cols].astype(F32)
            th = th_s[:, cols]
            g_gain = spec[:f] * ss[:f] + spec[f:] * ss[f:]
            g_pre = (g_gain * (1.0 - th * th)).astype(BF)
            gpre_s[:, cols] = g_pre
            weighted = g_pre.astype(F32) * mult
            small_s[13:14, cols] += share * jnp.sum(weighted, axis=0, keepdims=True)
            g = (1.0 + th) * mult
            yy = jnp.concatenate(
                [(g * spec[:f]).astype(BF), (g * spec[f:]).astype(BF)], axis=0
            )
            b_s[0:t, cols] = mm(tabt_s[...], yy)

        @pl.when(slot == 0)
        def _():
            for j in range(4):
                slot_load(1, j).start()
            y_end(1)
            unit1(4)

        @pl.when(slot == 1)
        def _():
            for j, p in enumerate(pairs):
                each(z_copies(j), "wait")
                rows = rows_at(me, quarter)
                total = p[1][3, rows, :].astype(F32)
                for k in range(3):
                    total += p[5][k].astype(F32)
                p[1][3, rows, :] = total.astype(BF)
            for copies, local in gathers[:2]:
                each(copies, "start")
                local.start()
            down_second_end()
            unit3(4)
            home_start(gmix_s, gtok6_h, 0, GT0, 2)

        for j in range(4, 8):
            slot_load(slot, j).wait()

        @pl.loop(0, d // CB)
        def _(c):
            m1, m2 = lanes(m1_ref, CB), lanes(m2_ref, CB)
            cols = cols_at(c, CB)
            g_feat = mm_nt(gpre_s[...], wc_s[cols, :])
            xc = cs_s[:, cols].astype(F32)
            power = (xc[:f] * xc[:f] + xc[f:] * xc[f:]) * isp
            g_pow = g_feat / (1.0 + power) * (lanes(mult_ref, CB) * (2.0 * isp))
            yy = jnp.concatenate(
                [(g_pow * xc[:f]).astype(BF), (g_pow * xc[f:]).astype(BF)], axis=0
            )
            g_cond = mm(tabt_s[...], yy)
            feat = (feat_s[:, cols].astype(F32) * lanes(mult_ref, CB)).astype(BF)
            dwc = share * mm_tn(feat, gpre_s[...])

            @pl.when(slot == 0)
            def _():
                u_s[cols, :] = dwc

            @pl.when(slot == 1)
            def _():
                u_s[cols, :] += dwc

            def finish(part, g_conv, p):
                at = cols_at(c, CB, part * d)
                back, sums = conv_back(g_conv, p, st_ref[:, at], m1, m2)
                for j in range(3):
                    row = 1 + 3 * j + part
                    small_s[row : row + 1, cols] += share * sums[j]
                wall_s[proj_rows(slot, part, 0, t), cols] = back.astype(BF)

            projected = lambda part: wall_s[proj_rows(slot, part, 0, t), cols].astype(F32)
            finish(0, a_s[0:t, cols], projected(0))
            value = v_s[:, cols].astype(F32)
            g_sig = b_s[0:t, cols]
            key = k_s[:, cols].astype(F32)
            finish(1, g_sig * value, projected(1))
            back, sums = conv_back(g_cond, value, ct_ref[:, cols], m1, m2)
            for j in range(3):
                small_s[10 + j : 11 + j, cols] += share * sums[j]
            finish(2, g_sig * key + back, projected(2))

        @pl.when(slot == 0)
        def _():
            for j in range(4, 8):
                slot_load(1, j).start()
            each(win_loads, "wait")
            down_first_end()
            unit2(4)

            @pl.loop(0, t // RB)
            def _(i):
                rows = rows_at(i, RB)
                u, r = unit_rows(cot_s[rows, :].astype(F32))
                keep_norm(u, rows)
                token_rows(0, rows, i * RB, u, r)

    def win_product(u, which, dst):
        at = 3 * which + u - 1
        part, cols = at // 2, cols_at(lax.rem(at, 2), h)
        blocks = [(0, 0), (0, RB), (1, half * RB)]

        @pl.loop(0, d // RB)
        def _(i):
            rows = rows_at(i, RB)
            dw = jnp.zeros((RB, h), F32)
            for k, (slot, offset) in enumerate(blocks):
                g = wall_s[proj_rows(slot, part, offset, RB), cols]
                dw += mm(n2t_s[rows, k * RB : (k + 1) * RB], g)
            dst[rows, :] = dw.astype(BF)

    reorder(sbg_s, u_s, 1 - core)
    unit_core(0).start()
    reorder(raw_of(0), u_s, core)
    last_rows = slice(t, n)
    u1, r1 = unit_rows(cot_s[last_rows, :].astype(F32))
    keep_norm(u1, last_rows)
    win_product(1, 1 - core, sbu_s)
    unit_core(1).start()
    win_product(1, core, raw_of(1))
    unit1(0)
    win_product(2, 1 - core, sbg_s)
    unit_core(2).start()
    win_product(2, core, raw_of(2))
    unit1(1)
    unit2(0)
    win_product(3, 1 - core, sbu_s)
    unit_core(3).start()
    win_product(3, core, raw_of(3))
    unit1(2)
    unit2(1)
    unit3(0)
    each(down_z, "wait")
    total = d1_s[me, 1].astype(F32)
    for k in range(3):
        total += zd_s[k].astype(F32)
    d1_s[me, 1] = total.astype(BF)
    each(gathers[2][0], "start")
    gathers[2][1].start()
    unit4(4)
    u1, r1 = unit_rows(cot_s[last_rows, :].astype(F32))
    token_rows(1, last_rows, half * RB, u1, r1)
    small_c = remote(small_s, sgot_s.at[0], at_core, SMALL)
    small_c.start()
    unit1(3)
    unit2(2)
    unit3(1)
    home_start(gmix_s, gtok6_h, 1, GT1, 3)
    unit4(0)
    small_c.wait()
    ssum_s[0] = small_s[...] + sgot_s[0]
    small_x = remote(ssum_s.at[0], sgot_s.at[1], at_x, SMALL + 1)
    small_x.start()
    unit2(3)
    unit3(2)
    each([c for copies, _ in gathers for c in copies], "wait")
    each([local for _, local in gathers], "wait")
    each(core_gathers, "start")
    unit4(1)
    unit5(0)
    unit5(4)
    small_x.wait()
    ssum_s[1] = ssum_s[0] + sgot_s[1]
    small_y = remote(ssum_s.at[1], sgot_s.at[2], at_y, SMALL + 2)
    small_y.start()
    unit3(3)
    unit4(2)
    unit5(1)
    small_y.wait()
    ssum_s[2] = ssum_s[1] + sgot_s[2]
    small_z = [
        remote(ssum_s.at[2], sgot_s.at[2 + k], at_z[k], SMALL + 2 + k) for k in range(1, 4)
    ]
    each(small_z, "start")
    unit4(3)
    unit5(2)
    each(small_z, "wait")
    small_out[...] = ssum_s[2] + sgot_s[3] + sgot_s[4] + sgot_s[5]
    unit5(3)

    each(diag_copies(False) + diag_copies(True) + x_copies() + y_copies(), "wait_send")
    each(core_gathers, "wait")
    for u in range(5):
        each(unit_gather_core(u), "wait")
    home_wait(n2_s, lay6_h, 0, LAY, 0)
    home_wait(n2_s, lay6_h, 1, LAY + 3, 1)
    home_wait(gmix_s, gtok6_h, 0, GT0, 2)
    home_wait(gmix_s, gtok6_h, 1, GT1, 3)


def back(
    side, slots, kind, mixed, xs, cot, w_out, g2, w_gate, w_up, w_down,
    proj, filt, ss, cs, th, feat, query, key, value, st, ct, w_cond, table, table_t, g1, w_in,
):
    t, d = xs.shape[1:]
    n = t + t // 2
    f2 = table.shape[0]
    f = f2 // 2
    h, q4, dr, s48 = d // 2, d // 4, d // 8, d // 16
    hbm = pl.BlockSpec(memory_space=pl.ANY)
    vm = pl.BlockSpec(memory_space=pltpu.VMEM)
    smem = pl.BlockSpec(memory_space=pltpu.SMEM)
    b = lambda *s: pltpu.VMEM(s, BF)
    g = lambda *s: pltpu.VMEM(s, F32)
    return pl.pallas_call(
        functools.partial(back_kernel, side),
        name="back",
        out_shape=tuple(
            jax.ShapeDtypeStruct(s, BF)
            for s in (
                (slots, t // 4, d), (slots, t // 4, d), (q4, 4 * d), (q4, 4 * d), (d, d),
                (q4, d), (q4, d), (q4, 3 * d), (3, 4, n, d),
            )
        )
        + (jax.ShapeDtypeStruct((16, d), F32),),
        in_specs=[smem] + [hbm] * 4 + [vm] + [hbm] * 12 + [vm, vm, hbm, hbm, hbm, vm, hbm],
        out_specs=(hbm,) * 9 + (vm,),
        scratch_shapes=[
            g(n, d), g(n, d), g(n, d), g(n, 128),
            b(n, d), b(d, n), b(n, d), b(n + t, d), b(n, d),
            b(n, d), b(n, d), b(n, d), b(3 * d + 6 * t, d), b(d, d), b(d, d),
            b(f2, t), b(t, f2), g(32, 128), g(32, 128), g(f, 128),
            b(d, h), b(d, h), b(h, d),
            b(4, d, h), b(4, d, h), b(4, h, d),
            b(d, h), b(d, h), b(d, h), b(d, h), b(d, h), b(d, h),
            b(3, q4, h), b(3, q4, h), b(4, 2, dr, d), b(4, dr, d), b(3, dr, d),
            b(t, d), b(f2, d), b(f2, d), g(f, d), b(f, d), b(t, d), b(t, d), b(t, d), b(f, d),
            b(5, d, h), b(3, d, h), b(5, q4, h), b(5, q4, h), b(5, q4, h), b(5, 3, s48, h),
            g(16, d), g(6, 16, d), g(3, 16, d),
            pltpu.SemaphoreType.DMA((21,)),
            pltpu.SemaphoreType.DMA((3, 3)),
            pltpu.SemaphoreType.DMA((3, 3)),
            pltpu.SemaphoreType.DMA((3,)),
            pltpu.SemaphoreType.DMA((169,)),
            pltpu.SemaphoreType.DMA((169,)),
            pltpu.SemaphoreType.DMA((13,)),
        ],
        compiler_params=pltpu.CompilerParams(
            collective_id=1, has_side_effects=True, vmem_limit_bytes=65400 * 1024
        ),
    )(
        kind, mixed, xs, cot, w_out, g2, w_gate, w_up, w_down, proj, filt, ss, cs, th, feat,
        query, key, value, st, ct, w_cond, table, table_t, g1, w_in,
    )


def on_device(
    tokens, kind, ln1_gain, w_in, short_taps, cond_taps, w_cond, cond_bias, w_out, ln2_gain,
    w_gate, w_up, w_down, cotangent,
):
    _, rows, slots, d = tokens.shape
    n = lax.axis_size("seq")
    dp_count = lax.axis_size("dp")
    rank = lax.axis_index("seq")
    tok6 = jnp.transpose(tokens[0], (1, 0, 2))
    cot6 = jnp.transpose(cotangent[0], (1, 0, 2))
    xs, proj, mixed, filt, sig_spec, cond_spec, th, feat, query, key, value, table, table_t = front(
        kind, tok6, ln1_gain, w_in, short_taps, cond_taps, w_cond, cond_bias
    )
    side = math.isqrt(dp_count // 2)
    lay6, gtok6, *sums, _, small = back(
        side, slots, kind, mixed, xs, cot6, w_out, ln2_gain, w_gate, w_up, w_down,
        proj.reshape(-1, d), filt, sig_spec, cond_spec, th, feat, query, key, value, short_taps, cond_taps, w_cond,
        table, table_t, ln1_gain, w_in,
    )
    layer_out = jnp.transpose(lay6, (1, 0, 2))[None]
    grad_tokens = jnp.transpose(gtok6, (1, 0, 2))[None]

    sums = [a.astype(F32) for a in sums]
    if dp_count > 8:
        groups = [
            [
                (y * side + x) * 2 + core
                for y in range(y0, side, 2)
                for x in range(x0, side, 2)
            ]
            for y0 in range(2)
            for x0 in range(2)
            for core in range(2)
        ]
        sums = [lax.psum(a, "dp", axis_index_groups=groups) for a in sums]
        small = lax.psum(small, "dp", axis_index_groups=groups)
    grad_gate, grad_up, grad_down, grad_w_out, grad_w_cond, grad_w_in = sums
    part = lambda a, width: lax.dynamic_slice_in_dim(a, rank * width, width, a.ndim - 1)
    return (
        layer_out,
        grad_tokens,
        part(small[0], d // n),
        grad_w_in,
        part(small[1:10].reshape(3, 3 * d), 3 * d // n),
        part(small[10:13], d // n),
        grad_w_cond,
        part(small[13], d // n),
        grad_w_out,
        part(small[14], d // n),
        grad_gate,
        grad_up,
        grad_down,
    )


def solution(mesh):
    rows = P("dp", "seq", None, None)
    return jax.shard_map(
        on_device,
        mesh=mesh,
        in_specs=(rows, P("dp")) + (P(),) * 11 + (rows,),
        out_specs=(
            rows,
            rows,
            P("seq"),
            P("seq", None),
            P(None, "seq"),
            P(None, "seq"),
            P("seq", None),
            P("seq"),
            P("seq", None),
            P("seq"),
            P("seq", None),
            P("seq", None),
            P("seq", None),
        ),
        check_vma=False,
    )
```

```python
import functools
import math

import jax
import jax.numpy as jnp
from jax import lax
from jax.experimental import pallas as pl
from jax.experimental.pallas import tpu as pltpu
from jax.sharding import PartitionSpec as P

BF = jnp.bfloat16
F32 = jnp.float32
MESH = pl.DeviceIdType.MESH
EPS = 1e-05
CB = 256
FC = 384
RB = 256
VMEM_LIMIT = 60 * 2**20


def mm(a, b):
    return jnp.dot(a, b, preferred_element_type=F32)


def mm_nt(a, b):
    return lax.dot_general(a, b, (((1,), (1,)), ((), ())), preferred_element_type=F32)


def mm_tn(a, b):
    return lax.dot_general(a, b, (((0,), (0,)), ((), ())), preferred_element_type=F32)


def unit_rows(x):
    mean = jnp.mean(x, axis=-1, keepdims=True)
    centered = x - mean
    r = lax.rsqrt(jnp.mean(centered * centered, axis=-1, keepdims=True) + EPS)
    return centered * r, r


def unit_back(g, u, r, gain):
    e = g * gain
    return r * (
        e - jnp.mean(e, axis=-1, keepdims=True) - u * jnp.mean(e * u, axis=-1, keepdims=True)
    )


def lanes(ref, width):
    m = ref[...]
    return jnp.concatenate([m] * (width // m.shape[1]), axis=1)


def down(a, j):
    return pltpu.roll(a, j, axis=0)


def up(a, j):
    return pltpu.roll(a, a.shape[0] - j, axis=0)


def masked(a, m):
    blk = a.shape[0] // 4
    parts = []
    for b in range(4):
        parts.append(a[b * blk : b * blk + 8] * m[8 * b : 8 * b + 8])
        parts.append(a[b * blk + 8 : (b + 1) * blk])
    return jnp.concatenate(parts, axis=0)


def conv(a, taps, m1, m2):
    return taps[0:1] * a + taps[1:2] * masked(down(a, 1), m1) + taps[2:3] * masked(down(a, 2), m2)


def conv_back(g, a, taps, m1, m2):
    g1, g2 = up(masked(g, m1), 1), up(masked(g, m2), 2)
    sums = [jnp.sum(v * a, axis=0, keepdims=True) for v in (g, g1, g2)]
    return taps[0:1] * g + taps[1:2] * g1 + taps[2:3] * g2, sums


def cols_at(c, width, base=0):
    return pl.ds(pl.multiple_of(base + c * width, 128), width)


def short_rows(i, t):
    half = t // 8 + 1
    block = jnp.zeros_like(i)
    for k in range(1, 5):
        block += (i >= k * half).astype(jnp.int32)
    return block, i - half * block


def wave_table(ref, axis, isl, t):
    freqs = ref.shape[axis] // 2
    j = lax.broadcasted_iota(jnp.int32, ref.shape, axis)
    pos = lax.broadcasted_iota(jnp.int32, ref.shape, 1 - axis)
    sin = (j >= freqs).astype(jnp.int32)
    i = j - freqs * sin
    block, f = short_rows(i, t)
    short = t // 4
    phase = isl * (i * pos) + (1 - isl) * (4 * f * (pos & (short - 1)))
    kept_long = (i <= t // 2).astype(jnp.int32)
    kept_short = ((pos >= block * short) & (pos < (block + 1) * short)).astype(jnp.int32)
    kept = isl * kept_long + (1 - isl) * kept_short
    phase = (phase - (t // 4) * sin) & (t - 1)
    angle = (phase - t // 2).astype(F32) * (2.0 * math.pi / t)
    z = angle * angle
    value = jnp.full_like(z, -1.0 / math.factorial(14))
    for k in range(6, -1, -1):
        value = value * z + (-1.0) ** k / math.factorial(2 * k)
    ref[...] = (-value * kept.astype(F32)).astype(ref.dtype)


def multiplicity(shape, isl, t):
    i = lax.broadcasted_iota(jnp.int32, shape, 0)
    block, f = short_rows(i, t)
    once_long = ((i == 0) | (i == t // 2)).astype(jnp.int32)
    once_short = ((f == 0) | (f == t // 8)).astype(jnp.int32)
    long = (2 - once_long) * (i <= t // 2).astype(jnp.int32)
    short = (2 - once_short) * (block < 4).astype(jnp.int32)
    return (isl * long + (1 - isl) * short).astype(F32)


def causal_masks(m1_ref, m2_ref, isl):
    row = lax.broadcasted_iota(jnp.int32, m1_ref.shape, 0)
    place = (row & 7) + isl * (row - (row & 7))
    m1_ref[...] = (place >= 1).astype(F32)
    m2_ref[...] = (place >= 2).astype(F32)


def inverse_span(isl, t):
    long = isl.astype(F32)
    return long * (1.0 / t) + (1.0 - long) * (4.0 / t)


def front_kernel(
    kind_ref, tok_h, g1_ref, win_h, st_ref, ct_ref, wc_h, cb_ref,
    xs_h, proj_h, mixed_h, filt_h, ss_h, sc_h, th_h, feat_h, q_h, k_h, v_h, tab_h, tabt_h,
    x_s, win_s, wc_s, tab_s, tabt_s, m1_ref, m2_ref, ms_s, n1_s, q_s,
    proj_s, mixed_s, filt_s, ss_s, sc_s, th_s, feat_s, qb_s, k_s, v_s,
    load_sem, out_sem, send_sem, recv_sem,
):
    t, d = n1_s.shape
    f = ms_s.shape[0]
    n = 4
    blk = t // n
    dp, me = lax.axis_index("dp"), lax.axis_index("seq")
    peers = [lax.rem(me + k, n) for k in range(n)]
    half = lax.rem(me, 2)
    pair = me + 1 - 2 * half
    isl = kind_ref[0]
    isp = inverse_span(isl, t)

    block = lambda i: pl.ds(pl.multiple_of(i * blk, blk), blk)
    loads = [
        pltpu.make_async_copy(win_h, win_s, load_sem.at[0]),
        pltpu.make_async_copy(wc_h, wc_s, load_sem.at[1]),
        pltpu.make_async_copy(tok_h.at[me], x_s.at[0, block(me)], load_sem.at[2]),
        pltpu.make_async_copy(tok_h.at[n + me // 2], x_s.at[1, block(me)], load_sem.at[3]),
    ]

    barrier = pltpu.get_barrier_semaphore()
    for k in range(1, n):
        pl.semaphore_signal(barrier, inc=1, device_id=(dp, peers[k]), device_id_type=MESH)
    pl.semaphore_wait(barrier, n - 1)

    def remote(src, dst, peer, j):
        return pltpu.make_async_remote_copy(
            src_ref=src,
            dst_ref=dst,
            send_sem=send_sem.at[j],
            recv_sem=recv_sem.at[j],
            device_id=(dp, peer),
            device_id_type=MESH,
        )

    whole_slot = [
        remote(tok_h.at[peers[k]], x_s.at[0, block(me)], peers[k], k - 1) for k in range(1, n)
    ]
    to_pair = remote(tok_h.at[n + me // 2], x_s.at[1, block(me)], pair, 3)
    across = remote(tok_h.at[n + peers[2] // 2], x_s.at[1, block(me)], peers[2], 4)
    handed = remote(x_s.at[1, block(peers[2])], x_s.at[1, block(peers[2])], pair, 5)
    for c in whole_slot + [across, to_pair]:
        c.start()
    for c in loads:
        c.start()

    wave_table(tab_s, 0, isl, t)
    wave_table(tabt_s, 1, isl, t)
    causal_masks(m1_ref, m2_ref, isl)
    ms_s[...] = multiplicity(ms_s.shape, isl, t) * isp

    for c in loads[:4]:
        c.wait()
    for c in whole_slot:
        c.wait()

    outs = [
        (x_s, xs_h), (proj_s, proj_h), (ss_s, ss_h), (sc_s, sc_h), (feat_s, feat_h),
        (qb_s, q_h), (k_s, k_h), (v_s, v_h),
        (mixed_s, mixed_h), (filt_s, filt_h), (th_s, th_h),
    ]

    def out_copy(slot, j):
        return pltpu.make_async_copy(outs[j][0].at[slot], outs[j][1].at[slot], out_sem.at[slot, j])

    tables = [
        pltpu.make_async_copy(tab_s, tab_h, load_sem.at[4]),
        pltpu.make_async_copy(tabt_s, tabt_h, load_sem.at[5]),
    ]
    for c in tables:
        c.start()

    @pl.loop(0, 2)
    def _(slot):
        @pl.when(slot == 1)
        def _():
            to_pair.wait()
            handed.wait()

        @pl.loop(0, t // 128)
        def _(r):
            rows = pl.ds(pl.multiple_of(r * 128, 128), 128)
            u, _ = unit_rows(x_s[slot, rows, :].astype(F32))
            n1_s[rows, :] = (u * g1_ref[...].reshape(1, d)).astype(BF)

        @pl.loop(0, d // d)
        def _(c):
            m1, m2 = lanes(m1_ref, d), lanes(m2_ref, d)
            own = cols_at(c, d)

            def part(k):
                cols = cols_at(c, d, k * d)
                p = mm(n1_s[...], win_s[:, cols]).astype(BF)
                proj_s[slot, k, :, own] = p
                return conv(p.astype(F32), st_ref[:, cols], m1, m2)

            query = part(0)
            q_s[:, own] = query
            qb_s[slot, :, own] = query.astype(BF)
            key = part(1)
            k_s[slot, :, own] = key.astype(BF)
            value = part(2).astype(BF)
            v_s[slot, :, own] = value
            value_f = value.astype(F32)
            signal = (key * value_f).astype(BF)
            ss_s[slot, :, own] = mm(tab_s[...], signal).astype(BF)
            cond = conv(value_f, ct_ref[:, own], m1, m2).astype(BF)
            xc = mm(tab_s[...], cond)
            sc_s[slot, :, own] = xc.astype(BF)
            power = (xc[:f] * xc[:f] + xc[f:] * xc[f:]) * isp
            feat_s[slot, :, own] = jnp.log1p(power).astype(BF)

        for j in range(8):
            out_copy(slot, j).start()

        @pl.when(slot == 0)
        def _():
            across.wait()
            handed.start()

        @pl.loop(0, d // d)
        def _(c):
            own = cols_at(c, d)
            th = jnp.tanh(mm(feat_s[slot], wc_s[:, own]) + cb_ref[...].reshape(1, d))
            th_s[slot, :, own] = th
            g = (1.0 + th) * lanes(ms_s, d)
            xs = ss_s[slot, :, own].astype(F32)
            y = jnp.concatenate([(g * xs[:f]).astype(BF), (g * xs[f:]).astype(BF)], axis=0)
            filt = mm(tabt_s[...], y)
            filt_s[slot, :, own] = filt.astype(BF)
            mixed_s[slot, :, own] = (q_s[:, own] * filt).astype(BF)

        for j in range(8, 11):
            out_copy(slot, j).start()

    for slot in range(2):
        for j in range(11):
            out_copy(slot, j).wait()
    for c in tables:
        c.wait()


def front(kind, tok, g1, w_in, st, ct, w_cond, cb):
    slots, blk, d = tok.shape
    t = 4 * blk
    f = -(-max(t // 2 + 1, 4 * (blk // 2 + 1)) // 16) * 16
    hbm = pl.BlockSpec(memory_space=pl.ANY)
    vm = pl.BlockSpec(memory_space=pltpu.VMEM)
    smem = pl.BlockSpec(memory_space=pltpu.SMEM)
    per_slot = [
        ((2, t, d), BF), ((2, 3, t, d), BF), ((2, t, d), BF), ((2, t, d), BF),
        ((2, 2 * f, d), BF), ((2, 2 * f, d), BF), ((2, f, d), F32), ((2, f, d), BF),
        ((2, t, d), BF), ((2, t, d), BF), ((2, t, d), BF),
    ]
    xs, *rest = [jax.ShapeDtypeStruct(*s) for s in per_slot]
    tables = [((2 * f, t), BF), ((t, 2 * f), BF)]
    return pl.pallas_call(
        front_kernel,
        name="front",
        out_shape=(xs, *rest)
        + tuple(jax.ShapeDtypeStruct(*s) for s in tables),
        in_specs=[smem, hbm, vm, hbm, vm, vm, hbm, vm],
        out_specs=(hbm,) * 13,
        scratch_shapes=[
            pltpu.VMEM((2, t, d), BF), pltpu.VMEM((d, 3 * d), BF), pltpu.VMEM((d, d), BF),
            pltpu.VMEM(*tables[0]), pltpu.VMEM(*tables[1]),
            pltpu.VMEM((32, 128), F32), pltpu.VMEM((32, 128), F32), pltpu.VMEM((f, 128), F32),
            pltpu.VMEM((t, d), BF), pltpu.VMEM((t, d), F32),
        ]
        + [pltpu.VMEM(*s) for s in per_slot[1:]]
        + [
            pltpu.SemaphoreType.DMA((6,)),
            pltpu.SemaphoreType.DMA((2, 11)),
            pltpu.SemaphoreType.DMA((6,)),
            pltpu.SemaphoreType.DMA((6,)),
        ],
        compiler_params=pltpu.CompilerParams(
            collective_id=0, has_side_effects=True, vmem_limit_bytes=VMEM_LIMIT
        ),
    )(kind, tok, g1, w_in, st, ct, w_cond, cb)


def add_into(dst, src):
    dst[...] = (dst[...].astype(F32) + src[...].astype(F32)).astype(dst.dtype)


def back_kernel(side, *refs):
    (
        kind_ref, mixed_h, xs_h, cot_h, wo_h, g2_ref, wg_h, wu_h, wd_h,
        proj_h, filt_h, ss_h, cs_h, th_h, feat_h, q_h, k_h, v_h,
        st_ref, ct_ref, wc_h, tab_h, tabt_h, g1_ref, win_h,
        lay6_h, gtok6_h, odg_h, odu_h, odd_h, owo_h, owc_h, owi_h, spool_h, small_out,
        a_s, b_s, u_s, r_s, n2_s, n2t_s, cot_s, mg_s, gmix_s,
        act_s, gg_s, gu_s, wall_s, wo_s, wc_s, tab_s, tabt_s, m1_ref, m2_ref, mult_ref,
        sbg_s, sbu_s, sbd_s, cg_s, cu_s, cd_s,
        dgg_s, dgu_s, xg_s, xu_s, yg_s, yu_s, zg_s, zu_s, d1_s, d2_s, zd_s,
        filt_s, ss_s, cs_s, th_s, feat_s, q_s, k_s, v_s, gpre_s,
        c2_s, raw2_s, rd_s, rx_s, ry_s, z2_s, small_s, sgot_s, ssum_s,
        load_sem, w_sem, spool_sem, back_sem, send_sem, recv_sem, local_sem,
    ) = refs
    n, d = n2_s.shape
    t = filt_s.shape[0]
    f = th_s.shape[0]
    isl = kind_ref[0]
    isp = inverse_span(isl, t)
    h = d // 2
    quarter = d // 4
    step48 = d // 16
    dr = h // 4

    dp, me = lax.axis_index("dp"), lax.axis_index("seq")
    core = lax.rem(dp, 2)
    x = lax.rem(lax.rem(dp // 2, side), 2)
    y = lax.rem(dp // (2 * side), 2)
    dp_x = dp + 2 - 4 * x
    dp_y = dp + 2 * side - 4 * side * y
    at_core, at_x, at_y = (dp + 1 - 2 * core, me), (dp_x, me), (dp_y, me)
    at_xy = (dp_x + dp_y - dp, me)
    peers = [lax.rem(me + k, 4) for k in range(4)]
    at_z = [(dp, peers[k]) for k in range(4)]
    half = lax.rem(me, 2)
    at_pair = (dp, me + 1 - 2 * half)
    half_at = pl.ds(pl.multiple_of(half * RB, RB), RB)
    xy = 2 * x + y
    diag, by_x, by_y = 3 - xy, 2 * (1 - x) + y, 2 * x + 1 - y

    def owner(s):
        if isinstance(s, int):
            return (diag, by_x, by_y, xy)[s]
        return 2 * jnp.where(s < 2, 1 - x, x) + jnp.where(lax.rem(s, 2) == 0, 1 - y, y)

    def rows_at(i, size, base=0):
        return pl.ds(pl.multiple_of(base + i * size, math.gcd(size, base) if base else size), size)

    def each(copies, what):
        for c in copies:
            getattr(c, what)()

    row_moves = lambda src, dst: [
        (src.at[0], dst.at[pl.ds(0, t)]),
        (src.at[1, half_at], dst.at[pl.ds(t, RB)]),
    ]
    moves = (
        row_moves(mixed_h, mg_s)
        + row_moves(xs_h, gmix_s)
        + [(wo_h, wo_s)]
        + [(tab_h, tab_s), (tabt_h, tabt_s), (wc_h, wc_s)]
        + [(proj_h, wall_s.at[pl.ds(3 * d, 6 * t)])]
    )
    loads = [pltpu.make_async_copy(s, e, load_sem.at[j]) for j, (s, e) in enumerate(moves)]
    slot_moves = [
        (filt_h, filt_s), (ss_h, ss_s), (th_h, th_s), (q_h, q_s),
        (cs_h, cs_s), (feat_h, feat_s), (k_h, k_s), (v_h, v_s),
    ]
    slot_load = lambda slot, j: pltpu.make_async_copy(
        slot_moves[j][0].at[slot], slot_moves[j][1], load_sem.at[11 + j]
    )
    x_loads = [
        pltpu.make_async_copy(a, b, load_sem.at[19 + j])
        for j, (a, b) in enumerate(row_moves(xs_h, cot_s))
    ]

    def weight(k, b):
        return pl.ds(pl.multiple_of((3 * b + k) * d, RB), d)

    def weights(s, b):
        cols = cols_at(owner(s), d)
        return [
            pltpu.make_async_copy(src, wall_s.at[weight(k, b)], w_sem.at[b, k])
            for k, src in enumerate((wg_h.at[:, cols], wu_h.at[:, cols], wd_h.at[cols, :]))
        ]

    win_loads = [
        pltpu.make_async_copy(
            win_h.at[:, k * d : (k + 1) * d], wall_s.at[weight(k, 0)], w_sem.at[2, k]
        )
        for k in range(3)
    ]

    def proj_rows(slot, part, offset, size):
        return pl.ds(pl.multiple_of(3 * d + (3 * slot + part) * t + offset, RB), size)

    each(loads[:5], "start")
    each(weights(3, 0), "start")

    barrier = pltpu.get_barrier_semaphore()
    everyone = [at_core, at_x, at_y, at_xy] + at_z[1:]
    for peer in everyone:
        pl.semaphore_signal(barrier, inc=1, device_id=peer, device_id_type=MESH)
    pl.semaphore_wait(barrier, len(everyone))

    causal_masks(m1_ref, m2_ref, isl)
    mult_ref[...] = multiplicity(mult_ref.shape, isl, t)

    def remote(src, dst, peer, j):
        return pltpu.make_async_remote_copy(
            src_ref=src,
            dst_ref=dst,
            send_sem=send_sem.at[j],
            recv_sem=recv_sem.at[j],
            device_id=peer,
            device_id_type=MESH,
        )

    C, DG, XS, YS, ZD, ZG, GA, GC = 0, 12, 20, 22, 24, 27, 36, 45
    LAY, GT0, GT1, PAIR, SMALL, COT, DX, DY, UNIT = 57, 63, 66, 69, 70, 76, 82, 90, 94

    rows128 = lay6_h.shape[1]
    sources = [lax.rem(me + 4 - k, 4) for k in range(4)]
    sends_part = [lax.rem(p, 2) == me // 2 for p in peers]
    gets_part = [half == s // 2 for s in sources]

    def cot_copies(k):
        moves = (
            (cot_h.at[peers[k]], cot_s.at[rows_at(me, rows128)]),
            (cot_h.at[4 + peers[k] // 2], cot_s.at[rows_at(half, rows128, t)]),
        )
        if k == 0:
            return [
                pltpu.make_async_copy(a, b, load_sem.at[9 + j]) for j, (a, b) in enumerate(moves)
            ]
        return [remote(a, b, at_z[k], COT + 2 * (k - 1) + j) for j, (a, b) in enumerate(moves)]

    for k in (1, 2, 3, 0):
        full, part = cot_copies(k)
        full.start()
        pl.when(sends_part[k])(part.start)

    each(loads[:5], "wait")

    @pl.loop(0, n // RB)
    def _(i):
        rows = rows_at(i, RB)
        hid = gmix_s[rows, :].astype(F32) + mm(mg_s[rows, :], wo_s[...])
        a_s[rows, :] = hid
        b_s[rows, :] = jnp.zeros_like(hid)
        u, r = unit_rows(hid)
        u_s[rows, :] = u
        r_s[rows, :] = jnp.broadcast_to(r, (RB, 128))
        n2 = u * g2_ref[...].reshape(1, d)
        n2_s[rows, :] = n2.astype(BF)
        n2t_s[:, rows] = n2.T.astype(BF)

    each(loads[5:-1], "start")
    for j in range(8):
        slot_load(0, j).start()

    pairs = ((sbg_s, cg_s, dgg_s, xg_s, yg_s, zg_s), (sbu_s, cu_s, dgu_s, xu_s, yu_s, zu_s))
    rank_rows = lambda q: pl.ds(q * quarter, quarter)

    def core_copies(s):
        bufs = ((sbg_s, cg_s.at[s]), (sbu_s, cu_s.at[s]), (sbd_s, cd_s.at[owner(s)]))
        return [remote(a, b, at_core, C + 4 * j + s) for j, (a, b) in enumerate(bufs)]

    def diag_copies(odd):
        return [
            remote(p[1].at[0, rank_rows(q)], p[2].at[rank_rows(q)], at_y if odd else at_x, DG + 4 * j + q)
            for j, p in enumerate(pairs)
            for q in ((1, 3) if odd else (0, 2))
        ]

    x_copies = lambda: [remote(p[1].at[1], p[3], at_x, XS + j) for j, p in enumerate(pairs)]
    y_copies = lambda: [remote(p[1].at[2], p[4], at_y, YS + j) for j, p in enumerate(pairs)]

    def down_first(q, peer, k, e):
        return remote(cd_s.at[q, rows_at(k, dr)], d1_s.at[q, e], peer, DX + 2 * q + e)

    def step_sums(s, j):
        p = pairs[j]

        def add_ranks(first):
            for q in (first, first + 2):
                add_into(p[1].at[s, rank_rows(q)], p[2].at[rank_rows(q)])

        @pl.when(s == 0)
        def _():
            each(diag_copies(False)[2 * j : 2 * j + 2], "start")
            each(diag_copies(True)[2 * j : 2 * j + 2], "start")

        @pl.when(s == 1)
        def _():
            each(diag_copies(True)[2 * j : 2 * j + 2], "wait_recv")
            add_ranks(1)
            x_copies()[j].start()

        @pl.when(s == 2)
        def _():
            each(diag_copies(False)[2 * j : 2 * j + 2], "wait_recv")
            add_ranks(0)
            y_copies()[j].start()

    saved = (act_s, gu_s, gg_s)

    def spool(s, i, j):
        rows = rows_at(i, RB)
        return pltpu.make_async_copy(
            saved[j].at[rows], spool_h.at[j, s, rows], spool_sem.at[i, j]
        )

    @pl.loop(0, 4)
    def _(p):
        s, b = 3 - p, lax.rem(p, 2)
        each(weights(s, b), "wait")

        @pl.when(p < 3)
        def _():
            each(weights(s - 1, 1 - b), "start")

        @pl.loop(0, n // RB)
        def _(i):
            rows = rows_at(i, RB)

            @pl.when(p > 0)
            def _():
                for j in range(3):
                    spool(s, i, j).wait()

            n2 = n2_s[rows, :]
            pre = mm(n2, wall_s[weight(0, b), :])
            lin = mm(n2, wall_s[weight(1, b), :])
            sg = 1.0 / (1.0 + jnp.exp(-pre))
            silu = pre * sg
            act = (silu * lin).astype(BF)
            act_s[rows, :] = act
            gu_s[rows, :] = silu.astype(BF)
            gg_s[rows, :] = (lin * sg * (1.0 + pre * (1.0 - sg))).astype(BF)
            a_s[rows, :] += mm(act, wall_s[weight(2, b), :])

            @pl.when(p < 3)
            def _():
                for j in range(3):
                    spool(s, i, j).start()

    @pl.loop(0, n // RB)
    def _(i):
        rows = rows_at(i, RB)
        n2_s[rows, :] = a_s[rows, :].astype(BF)

    sends_half = [half == p // 2 for p in peers]
    gets_half = [lax.rem(s, 2) == me // 2 for s in sources]

    def home(buf, out, part, base, k):
        if part == 0:
            src, dst = buf.at[rows_at(peers[k], rows128)], out.at[me]
        else:
            src, dst = buf.at[rows_at(lax.rem(peers[k], 2), rows128, t)], out.at[4 + me // 2]
        if k == 0:
            return pltpu.make_async_copy(src, dst, local_sem.at[base])
        return remote(src, dst, at_z[k], base + k - 1)

    def home_start(buf, out, part, base, local):
        for k in range(4):
            copy = home(buf, out, part, base if k else local, k)
            if part == 0:
                copy.start()
            else:
                pl.when(sends_half[k])(copy.start)

    def home_wait(buf, out, part, base, local):
        for k in range(4):
            copy = home(buf, out, part, base if k else local, k)
            if part == 0:
                copy.wait()
            elif k == 0:
                pl.when(sends_half[0])(copy.wait)
            else:
                pl.when(sends_half[k])(copy.wait_send)
                pl.when(gets_half[k])(copy.wait_recv)

    for k in range(4):
        full, part = cot_copies(k)
        full.wait()
        if k == 0:
            pl.when(sends_part[0])(part.wait)
        else:
            pl.when(sends_part[k])(part.wait_send)
            pl.when(gets_part[k])(part.wait_recv)

    def unspool(s, j):
        return pltpu.make_async_copy(spool_h.at[j, s], saved[j], back_sem.at[j])

    @pl.loop(0, 4)
    def _(s):
        b = lax.rem(s + 1, 2)

        @pl.when(s > 0)
        def _():
            each(weights(s, b), "wait")

        @pl.when(s < 3)
        def _():
            each(weights(s + 1, 1 - b), "start")

        pl.when(s == 3)(loads[-1].start)

        @pl.when(s == 1)
        def _():
            home_start(n2_s, lay6_h, 0, LAY, 0)
            home_start(n2_s, lay6_h, 1, LAY + 3, 1)

        @pl.when(s > 0)
        def _():
            unspool(s, 1).wait()
            unspool(s, 2).wait()

        @pl.loop(0, n // RB)
        def _(i):
            rows = rows_at(i, RB)
            g_act = mm_nt(cot_s[rows, :], wall_s[weight(2, b), :])
            g_up = (g_act * gu_s[rows, :].astype(F32)).astype(BF)
            gu_s[rows, :] = g_up
            g_gate = (g_act * gg_s[rows, :].astype(F32)).astype(BF)
            gg_s[rows, :] = g_gate
            b_s[rows, :] += mm_nt(g_gate, wall_s[weight(0, b), :]) + mm_nt(
                g_up, wall_s[weight(1, b), :]
            )

        @pl.when(s > 0)
        def _():
            each(core_copies(s - 1), "wait_send")

        def product(which, j, put):
            cols = cols_at(which, h)

            @pl.loop(0, d // RB)
            def _(i):
                rows, out = rows_at(i, RB), cols_at(i, RB)
                if j == 2:
                    put(slice(None), out, mm_tn(act_s[:, cols], cot_s[:, out]))
                else:
                    put(rows, slice(None), mm(n2t_s[rows, :], (gg_s, gu_s)[j][:, cols]))

        for j, buf in enumerate((sbg_s, sbu_s, sbd_s)):

            def put(rows, cols, value, buf=buf):
                buf[rows, cols] = value.astype(BF)

            if j == 2:
                pl.when(s > 0)(unspool(s, 0).wait)
            product(1 - core, j, put)
            core_copies(s)[j].start()
        for j, (buf, at) in enumerate(((cg_s, s), (cu_s, s), (cd_s, owner(s)))):
            core_copies(s)[j].wait_recv()

            def put(rows, cols, value, buf=buf, at=at):
                buf[at, rows, cols] = (buf[at, rows, cols].astype(F32) + value).astype(BF)

            product(core, j, put)
            pl.when(s < 3)(unspool(s + 1, (2, 1, 0)[j]).start)
            if j < 2:
                step_sums(s, j)

    for q in range(4):
        peer, near = (at_y, by_y) if q % 2 else (at_x, by_x)
        down_first(q, peer, diag, 0).start()
        down_first(q, peer, near, 1).start()

    each(win_loads, "start")
    small_s[...] = jnp.zeros_like(small_s)

    @pl.loop(0, n // RB)
    def _(i):
        rows = rows_at(i, RB)
        g, u = b_s[rows, :], u_s[rows, :]
        small_s[14:15, :] += jnp.sum(g * u, axis=0, keepdims=True)
        gh = cot_s[rows, :].astype(F32) + unit_back(g, u, r_s[rows, 0:1], g2_ref[...].reshape(1, d))
        gmix_s[rows, :] = gh.astype(BF)

    each(x_loads, "start")
    pair_at = rows_at(half, RB, n)
    mg_s[pair_at, :] = mm_nt(gmix_s[t:, :], wo_s[...]).astype(BF)
    pair_copy = remote(mg_s.at[pair_at], mg_s.at[pair_at], at_pair, PAIR)
    pair_copy.start()

    each(core_copies(3), "wait_send")

    def pos(q):
        return q // 2 + 2 * (q % 2 if isinstance(q, int) else lax.rem(q, 2))

    def reorder(dst, src, which):
        cols = cols_at(which, h)
        for q in range(4):
            for k in range(4):
                to, fr = (4 * k + pos(q)) * step48, (4 * q + k) * step48
                dst[to : to + step48, :] = src[fr : fr + step48, cols].astype(BF)

    def unit_core(u):
        return remote((sbg_s, sbu_s)[u % 2], c2_s.at[u], at_core, UNIT + 15 * u)

    raw_of = lambda u: raw2_s.at[2 if u == 4 else u % 2]
    two = 2 * step48

    def unit_diag(u):
        return [
            remote(
                c2_s.at[u, rows_at(2 * diag + e, two)],
                rd_s.at[u, pl.ds(e * two, two)],
                (at_x, at_y)[e],
                UNIT + 15 * u + 1 + e,
            )
            for e in range(2)
        ]

    def unit_near(u):
        return [
            remote(c2_s.at[u, rows_at(by_x, quarter)], rx_s.at[u], at_x, UNIT + 15 * u + 3),
            remote(c2_s.at[u, rows_at(by_y, quarter)], ry_s.at[u], at_y, UNIT + 15 * u + 4),
        ]

    def unit_rank(q):
        return rows_at(4 * xy + pos(q), step48)

    def unit_z(u):
        return [
            remote(
                c2_s.at[u, unit_rank(peers[k])], z2_s.at[u, k - 1], at_z[k], UNIT + 15 * u + 4 + k
            )
            for k in range(1, 4)
        ]

    def unit_view(u):
        if u in (0, 4):
            out = owc_h if u == 0 else owo_h
            return lambda k, c: out.at[rows_at(k, step48), cols_at(c, h)]
        return lambda k, c: owi_h.at[rows_at(k, step48), cols_at(3 * c + u - 1, h)]

    def unit_gather(u):
        return gather(c2_s.at[u, unit_rank(me)], unit_view(u), UNIT + 15 * u + 8, 5 + u)

    def unit_gather_core(u):
        return gather_core(unit_view(u), UNIT + 15 * u + 11)

    def unit1(u):
        unit_core(u).wait()

        @pl.loop(0, 4)
        def _(k):
            add_into(c2_s.at[u, rows_at(k, quarter)], raw_of(u).at[rows_at(k, quarter)])

        each(unit_diag(u), "start")

    def unit2(u):
        each(unit_diag(u), "wait")
        add_into(c2_s.at[u, rows_at(2 * by_y, two)], rd_s.at[u, 0:two])
        add_into(c2_s.at[u, rows_at(2 * by_x + 1, two)], rd_s.at[u, two : 2 * two])
        each(unit_near(u), "start")

    def unit3(u):
        each(unit_near(u), "wait")
        at = c2_s.at[u, rows_at(xy, quarter)]
        total = at[...].astype(F32) + rx_s[u].astype(F32) + ry_s[u].astype(F32)
        at[...] = total.astype(BF)
        each(unit_z(u), "start")

    def unit4(u):
        each(unit_z(u), "wait")
        at = c2_s.at[u, unit_rank(me)]
        total = at[...].astype(F32)
        for k in range(3):
            total += z2_s[u, k].astype(F32)
        at[...] = total.astype(BF)
        copies, local = unit_gather(u)
        each(copies, "start")
        local.start()

    def unit5(u):
        copies, local = unit_gather(u)
        each(copies, "wait")
        local.wait()
        each(unit_gather_core(u), "start")

    @pl.loop(0, d // RB)
    def _(i):
        a_s[rows_at(i, RB), :] = mm_tn(mg_s[0:n, cols_at(i, RB)], gmix_s[...])

    reorder(sbg_s, a_s, 1 - core)
    unit_core(4).start()
    reorder(raw_of(4), a_s, core)

    each(x_copies(), "wait_recv")
    for p in pairs:

        @pl.loop(0, 4)
        def _(q, p=p):
            add_into(p[1].at[3, rows_at(q, quarter)], p[3].at[rows_at(q, quarter)])

    @pl.loop(0, t // RB)
    def _(i):
        rows = rows_at(i, RB)
        mg_s[rows, :] = mm_nt(gmix_s[rows, :], wo_s[...]).astype(BF)

    def z_copies(j):
        p = pairs[j]
        return [
            remote(p[1].at[3, rows_at(peers[k], quarter)], p[5].at[k - 1], at_z[k], ZG + 3 * j + k - 1)
            for k in range(1, 4)
        ]

    def y_end(j):
        p = pairs[j]
        y_copies()[j].wait_recv()

        @pl.loop(0, 4)
        def _(q):
            add_into(p[1].at[3, rows_at(q, quarter)], p[4].at[rows_at(q, quarter)])

        each(z_copies(j), "start")

    y_end(0)

    down_second = [
        remote(d1_s.at[q, 0], d2_s.at[q], at_x if q % 2 else at_y, DY + q) for q in range(4)
    ]
    down_z = [
        remote(d1_s.at[peers[k], 1], zd_s.at[k - 1], at_z[k], ZD + k - 1) for k in range(1, 4)
    ]

    def down_first_end():
        for q in range(4):
            for e in range(2):
                remote(d1_s.at[q, e], d1_s.at[q, e], at_x, DX + 2 * q + e).wait()
            add_into(d1_s.at[q, 0], cd_s.at[q, rows_at(by_x if q % 2 else by_y, dr)])
            add_into(d1_s.at[q, 1], cd_s.at[q, rows_at(xy, dr)])
        each(down_second, "start")

    def down_second_end():
        each(down_second, "wait")
        for q in range(4):
            add_into(d1_s.at[q, 1], d2_s.at[q])
        each(down_z, "start")

    def gather(src, view, base, first_local):
        return [
            remote(src, view(xy, core), peer, base + k)
            for k, peer in enumerate((at_x, at_y, at_xy))
        ], pltpu.make_async_copy(src, view(xy, core), local_sem.at[first_local])

    def gather_core(view, base):
        return [remote(view(k, core), view(k, core), at_core, base + k) for k in range(4)]

    view_dg = lambda k, c: odg_h.at[:, cols_at(2 * k + c, h)]
    view_du = lambda k, c: odu_h.at[:, cols_at(2 * k + c, h)]
    view_dd = lambda k, c: odd_h.at[rows_at(4 * c + k, dr)]
    gathers = [
        gather(cg_s.at[3, rows_at(me, quarter)], view_dg, GA, 10),
        gather(cu_s.at[3, rows_at(me, quarter)], view_du, GA + 3, 11),
        gather(d1_s.at[me, 1], view_dd, GA + 6, 12),
    ]
    core_gathers = (
        gather_core(view_dg, GC) + gather_core(view_du, GC + 4) + gather_core(view_dd, GC + 8)
    )

    def keep_norm(u, rows):
        n1t = (u * g1_ref[...].reshape(1, d)).T.astype(BF)
        for q in range(4):
            for k in range(4):
                to, fr = (4 * k + pos(q)) * step48, (4 * q + k) * step48
                n2t_s[to : to + step48, rows] = n1t[fr : fr + step48]

    def token_rows(slot, rows, offset, u, r):
        g = jnp.zeros((RB, d), F32)
        for part in range(3):
            g += mm_nt(wall_s[proj_rows(slot, part, offset, RB), :], wall_s[weight(part, 0), :])
        small_s[0:1, :] += jnp.sum(g * u, axis=0, keepdims=True)
        gmix_s[rows, :] = (
            gmix_s[rows, :].astype(F32) + unit_back(g, u, r, g1_ref[...].reshape(1, d))
        ).astype(BF)

    each(loads[5:], "wait")
    each(x_loads, "wait")

    @pl.loop(0, 2)
    def _(slot):
        share = jnp.where(slot == 0, 1.0, 0.5)
        for j in range(4):
            slot_load(slot, j).wait()
        pl.when(slot == 1)(pair_copy.wait)
        gm_at = pl.ds(pl.multiple_of(slot * n, RB), t)

        @pl.loop(0, d // CB)
        def _(c):
            mult = lanes(mult_ref, CB)
            cols = cols_at(c, CB)
            query = q_s[:, cols].astype(F32)
            gm = mg_s[gm_at, cols].astype(F32)
            a_s[0:t, cols] = gm * filt_s[:, cols].astype(F32)
            spec = mm(tab_s[...], (gm * query).astype(BF)) * isp
            ss = ss_s[:, cols].astype(F32)
            th = th_s[:, cols]
            g_gain = spec[:f] * ss[:f] + spec[f:] * ss[f:]
            g_pre = (g_gain * (1.0 - th * th)).astype(BF)
            gpre_s[:, cols] = g_pre
            weighted = g_pre.astype(F32) * mult
            small_s[13:14, cols] += share * jnp.sum(weighted, axis=0, keepdims=True)
            g = (1.0 + th) * mult
            yy = jnp.concatenate(
                [(g * spec[:f]).astype(BF), (g * spec[f:]).astype(BF)], axis=0
            )
            b_s[0:t, cols] = mm(tabt_s[...], yy)

        @pl.when(slot == 0)
        def _():
            for j in range(4):
                slot_load(1, j).start()
            y_end(1)
            unit1(4)

        @pl.when(slot == 1)
        def _():
            for j, p in enumerate(pairs):
                each(z_copies(j), "wait")
                rows = rows_at(me, quarter)
                total = p[1][3, rows, :].astype(F32)
                for k in range(3):
                    total += p[5][k].astype(F32)
                p[1][3, rows, :] = total.astype(BF)
            for copies, local in gathers[:2]:
                each(copies, "start")
                local.start()
            down_second_end()
            unit3(4)
            home_start(gmix_s, gtok6_h, 0, GT0, 2)

        for j in range(4, 8):
            slot_load(slot, j).wait()

        @pl.loop(0, d // CB)
        def _(c):
            m1, m2 = lanes(m1_ref, CB), lanes(m2_ref, CB)
            cols = cols_at(c, CB)
            g_feat = mm_nt(gpre_s[...], wc_s[cols, :])
            xc = cs_s[:, cols].astype(F32)
            power = (xc[:f] * xc[:f] + xc[f:] * xc[f:]) * isp
            g_pow = g_feat / (1.0 + power) * (lanes(mult_ref, CB) * (2.0 * isp))
            yy = jnp.concatenate(
                [(g_pow * xc[:f]).astype(BF), (g_pow * xc[f:]).astype(BF)], axis=0
            )
            g_cond = mm(tabt_s[...], yy)
            feat = (feat_s[:, cols].astype(F32) * lanes(mult_ref, CB)).astype(BF)
            dwc = share * mm_tn(feat, gpre_s[...])

            @pl.when(slot == 0)
            def _():
                u_s[cols, :] = dwc

            @pl.when(slot == 1)
            def _():
                u_s[cols, :] += dwc

            def finish(part, g_conv, p):
                at = cols_at(c, CB, part * d)
                back, sums = conv_back(g_conv, p, st_ref[:, at], m1, m2)
                for j in range(3):
                    row = 1 + 3 * j + part
                    small_s[row : row + 1, cols] += share * sums[j]
                wall_s[proj_rows(slot, part, 0, t), cols] = back.astype(BF)

            projected = lambda part: wall_s[proj_rows(slot, part, 0, t), cols].astype(F32)
            finish(0, a_s[0:t, cols], projected(0))
            value = v_s[:, cols].astype(F32)
            g_sig = b_s[0:t, cols]
            key = k_s[:, cols].astype(F32)
            finish(1, g_sig * value, projected(1))
            back, sums = conv_back(g_cond, value, ct_ref[:, cols], m1, m2)
            for j in range(3):
                small_s[10 + j : 11 + j, cols] += share * sums[j]
            finish(2, g_sig * key + back, projected(2))

        @pl.when(slot == 0)
        def _():
            for j in range(4, 8):
                slot_load(1, j).start()
            each(win_loads, "wait")
            down_first_end()
            unit2(4)

            @pl.loop(0, t // RB)
            def _(i):
                rows = rows_at(i, RB)
                u, r = unit_rows(cot_s[rows, :].astype(F32))
                keep_norm(u, rows)
                token_rows(0, rows, i * RB, u, r)

    def gathers_end(j):
        each(gathers[j][0], "wait")
        gathers[j][1].wait()
        each(core_gathers[4 * j : 4 * j + 4], "start")

    def win_product(u, which, dst):
        at = 3 * which + u - 1
        part, cols = at // 2, cols_at(lax.rem(at, 2), h)
        blocks = [(0, 0), (0, RB), (1, half * RB)]

        @pl.loop(0, d // RB)
        def _(i):
            rows = rows_at(i, RB)
            dw = jnp.zeros((RB, h), F32)
            for k, (slot, offset) in enumerate(blocks):
                g = wall_s[proj_rows(slot, part, offset, RB), cols]
                dw += mm(n2t_s[rows, k * RB : (k + 1) * RB], g)
            dst[rows, :] = dw.astype(BF)

    reorder(sbg_s, u_s, 1 - core)
    unit_core(0).start()
    reorder(raw_of(0), u_s, core)
    last_rows = slice(t, n)
    u1, r1 = unit_rows(cot_s[last_rows, :].astype(F32))
    keep_norm(u1, last_rows)
    win_product(1, 1 - core, sbu_s)
    unit_core(1).start()
    win_product(1, core, raw_of(1))
    unit1(0)
    win_product(2, 1 - core, sbg_s)
    unit_core(2).start()
    win_product(2, core, raw_of(2))
    unit1(1)
    unit2(0)
    win_product(3, 1 - core, sbu_s)
    unit_core(3).start()
    win_product(3, core, raw_of(3))
    unit1(2)
    unit2(1)
    gathers_end(0)
    gathers_end(1)
    unit3(0)
    each(down_z, "wait")
    total = d1_s[me, 1].astype(F32)
    for k in range(3):
        total += zd_s[k].astype(F32)
    d1_s[me, 1] = total.astype(BF)
    each(gathers[2][0], "start")
    gathers[2][1].start()
    unit4(4)
    u1, r1 = unit_rows(cot_s[last_rows, :].astype(F32))
    token_rows(1, last_rows, half * RB, u1, r1)
    small_c = remote(small_s, sgot_s.at[0], at_core, SMALL)
    small_c.start()
    unit1(3)
    unit2(2)
    unit3(1)
    home_start(gmix_s, gtok6_h, 1, GT1, 3)
    unit4(0)
    small_c.wait()
    ssum_s[0] = small_s[...] + sgot_s[0]
    small_x = remote(ssum_s.at[0], sgot_s.at[1], at_x, SMALL + 1)
    small_x.start()
    unit2(3)
    unit3(2)
    unit4(1)
    unit5(0)
    unit5(4)
    small_x.wait()
    ssum_s[1] = ssum_s[0] + sgot_s[1]
    small_y = remote(ssum_s.at[1], sgot_s.at[2], at_y, SMALL + 2)
    small_y.start()
    unit3(3)
    unit4(2)
    gathers_end(2)
    unit5(1)
    small_y.wait()
    ssum_s[2] = ssum_s[1] + sgot_s[2]
    small_z = [
        remote(ssum_s.at[2], sgot_s.at[2 + k], at_z[k], SMALL + 2 + k) for k in range(1, 4)
    ]
    each(small_z, "start")
    unit4(3)
    unit5(2)
    each(small_z, "wait")
    small_out[...] = ssum_s[2] + sgot_s[3] + sgot_s[4] + sgot_s[5]
    unit5(3)

    each(diag_copies(False) + diag_copies(True) + x_copies() + y_copies(), "wait_send")
    each(core_gathers, "wait")
    for u in range(5):
        each(unit_gather_core(u), "wait")
    home_wait(n2_s, lay6_h, 0, LAY, 0)
    home_wait(n2_s, lay6_h, 1, LAY + 3, 1)
    home_wait(gmix_s, gtok6_h, 0, GT0, 2)
    home_wait(gmix_s, gtok6_h, 1, GT1, 3)


def back(
    side, slots, kind, mixed, xs, cot, w_out, g2, w_gate, w_up, w_down,
    proj, filt, ss, cs, th, feat, query, key, value, st, ct, w_cond, table, table_t, g1, w_in,
):
    t, d = xs.shape[1:]
    n = t + t // 2
    f2 = table.shape[0]
    f = f2 // 2
    h, q4, dr, s48 = d // 2, d // 4, d // 8, d // 16
    hbm = pl.BlockSpec(memory_space=pl.ANY)
    vm = pl.BlockSpec(memory_space=pltpu.VMEM)
    smem = pl.BlockSpec(memory_space=pltpu.SMEM)
    b = lambda *s: pltpu.VMEM(s, BF)
    g = lambda *s: pltpu.VMEM(s, F32)
    return pl.pallas_call(
        functools.partial(back_kernel, side),
        name="back",
        out_shape=tuple(
            jax.ShapeDtypeStruct(s, BF)
            for s in (
                (slots, t // 4, d), (slots, t // 4, d), (q4, 4 * d), (q4, 4 * d), (d, d),
                (q4, d), (q4, d), (q4, 3 * d), (3, 4, n, d),
            )
        )
        + (jax.ShapeDtypeStruct((16, d), F32),),
        in_specs=[smem] + [hbm] * 4 + [vm] + [hbm] * 12 + [vm, vm, hbm, hbm, hbm, vm, hbm],
        out_specs=(hbm,) * 9 + (vm,),
        scratch_shapes=[
            g(n, d), g(n, d), g(n, d), g(n, 128),
            b(n, d), b(d, n), b(n, d), b(n + t, d), b(n, d),
            b(n, d), b(n, d), b(n, d), b(3 * d + 6 * t, d), b(d, d), b(d, d),
            b(f2, t), b(t, f2), g(32, 128), g(32, 128), g(f, 128),
            b(d, h), b(d, h), b(h, d),
            b(4, d, h), b(4, d, h), b(4, h, d),
            b(d, h), b(d, h), b(d, h), b(d, h), b(d, h), b(d, h),
            b(3, q4, h), b(3, q4, h), b(4, 2, dr, d), b(4, dr, d), b(3, dr, d),
            b(t, d), b(f2, d), b(f2, d), g(f, d), b(f, d), b(t, d), b(t, d), b(t, d), b(f, d),
            b(5, d, h), b(3, d, h), b(5, q4, h), b(5, q4, h), b(5, q4, h), b(5, 3, s48, h),
            g(16, d), g(6, 16, d), g(3, 16, d),
            pltpu.SemaphoreType.DMA((21,)),
            pltpu.SemaphoreType.DMA((3, 3)),
            pltpu.SemaphoreType.DMA((3, 3)),
            pltpu.SemaphoreType.DMA((3,)),
            pltpu.SemaphoreType.DMA((169,)),
            pltpu.SemaphoreType.DMA((169,)),
            pltpu.SemaphoreType.DMA((13,)),
        ],
        compiler_params=pltpu.CompilerParams(
            collective_id=1, has_side_effects=True, vmem_limit_bytes=65400 * 1024
        ),
    )(
        kind, mixed, xs, cot, w_out, g2, w_gate, w_up, w_down, proj, filt, ss, cs, th, feat,
        query, key, value, st, ct, w_cond, table, table_t, g1, w_in,
    )


def on_device(
    tokens, kind, ln1_gain, w_in, short_taps, cond_taps, w_cond, cond_bias, w_out, ln2_gain,
    w_gate, w_up, w_down, cotangent,
):
    _, rows, slots, d = tokens.shape
    n = lax.axis_size("seq")
    dp_count = lax.axis_size("dp")
    rank = lax.axis_index("seq")
    tok6 = jnp.transpose(tokens[0], (1, 0, 2))
    cot6 = jnp.transpose(cotangent[0], (1, 0, 2))
    xs, proj, mixed, filt, sig_spec, cond_spec, th, feat, query, key, value, table, table_t = front(
        kind, tok6, ln1_gain, w_in, short_taps, cond_taps, w_cond, cond_bias
    )
    side = math.isqrt(dp_count // 2)
    lay6, gtok6, *sums, _, small = back(
        side, slots, kind, mixed, xs, cot6, w_out, ln2_gain, w_gate, w_up, w_down,
        proj.reshape(-1, d), filt, sig_spec, cond_spec, th, feat, query, key, value, short_taps, cond_taps, w_cond,
        table, table_t, ln1_gain, w_in,
    )
    layer_out = jnp.transpose(lay6, (1, 0, 2))[None]
    grad_tokens = jnp.transpose(gtok6, (1, 0, 2))[None]

    sums = [a.astype(F32) for a in sums]
    if dp_count > 8:
        groups = [
            [
                (y * side + x) * 2 + core
                for y in range(y0, side, 2)
                for x in range(x0, side, 2)
            ]
            for y0 in range(2)
            for x0 in range(2)
            for core in range(2)
        ]
        sums = [lax.psum(a, "dp", axis_index_groups=groups) for a in sums]
        small = lax.psum(small, "dp", axis_index_groups=groups)
    grad_gate, grad_up, grad_down, grad_w_out, grad_w_cond, grad_w_in = sums
    part = lambda a, width: lax.dynamic_slice_in_dim(a, rank * width, width, a.ndim - 1)
    return (
        layer_out,
        grad_tokens,
        part(small[0], d // n),
        grad_w_in,
        part(small[1:10].reshape(3, 3 * d), 3 * d // n),
        part(small[10:13], d // n),
        grad_w_cond,
        part(small[13], d // n),
        grad_w_out,
        part(small[14], d // n),
        grad_gate,
        grad_up,
        grad_down,
    )


def solution(mesh):
    rows = P("dp", "seq", None, None)
    return jax.shard_map(
        on_device,
        mesh=mesh,
        in_specs=(rows, P("dp")) + (P(),) * 11 + (rows,),
        out_specs=(
            rows,
            rows,
            P("seq"),
            P("seq", None),
            P(None, "seq"),
            P(None, "seq"),
            P("seq", None),
            P("seq"),
            P("seq", None),
            P("seq"),
            P("seq", None),
            P("seq", None),
            P("seq", None),
        ),
        check_vma=False,
    )
```

```python
import functools
import math

import jax
import jax.numpy as jnp
from jax import lax
from jax.experimental import pallas as pl
from jax.experimental.pallas import tpu as pltpu
from jax.sharding import PartitionSpec as P

BF = jnp.bfloat16
F32 = jnp.float32
MESH = pl.DeviceIdType.MESH
EPS = 1e-05
CB = 256
FC = 384
RB = 256
VMEM_LIMIT = 60 * 2**20


def mm(a, b):
    return jnp.dot(a, b, preferred_element_type=F32)


def mm_nt(a, b):
    return lax.dot_general(a, b, (((1,), (1,)), ((), ())), preferred_element_type=F32)


def mm_tn(a, b):
    return lax.dot_general(a, b, (((0,), (0,)), ((), ())), preferred_element_type=F32)


def unit_rows(x):
    mean = jnp.mean(x, axis=-1, keepdims=True)
    centered = x - mean
    r = lax.rsqrt(jnp.mean(centered * centered, axis=-1, keepdims=True) + EPS)
    return centered * r, r


def unit_back(g, u, r, gain):
    e = g * gain
    return r * (
        e - jnp.mean(e, axis=-1, keepdims=True) - u * jnp.mean(e * u, axis=-1, keepdims=True)
    )


def lanes(ref, width):
    m = ref[...]
    return jnp.concatenate([m] * (width // m.shape[1]), axis=1)


def down(a, j):
    return pltpu.roll(a, j, axis=0)


def up(a, j):
    return pltpu.roll(a, a.shape[0] - j, axis=0)


def masked(a, m):
    blk = a.shape[0] // 4
    parts = []
    for b in range(4):
        parts.append(a[b * blk : b * blk + 8] * m[8 * b : 8 * b + 8])
        parts.append(a[b * blk + 8 : (b + 1) * blk])
    return jnp.concatenate(parts, axis=0)


def conv(a, taps, m1, m2):
    return taps[0:1] * a + taps[1:2] * masked(down(a, 1), m1) + taps[2:3] * masked(down(a, 2), m2)


def conv_back(g, a, taps, m1, m2):
    g1, g2 = up(masked(g, m1), 1), up(masked(g, m2), 2)
    sums = [jnp.sum(v * a, axis=0, keepdims=True) for v in (g, g1, g2)]
    return taps[0:1] * g + taps[1:2] * g1 + taps[2:3] * g2, sums


def cols_at(c, width, base=0):
    return pl.ds(pl.multiple_of(base + c * width, 128), width)


def short_rows(i, t):
    half = t // 8 + 1
    block = jnp.zeros_like(i)
    for k in range(1, 5):
        block += (i >= k * half).astype(jnp.int32)
    return block, i - half * block


def wave_table(ref, axis, isl, t):
    freqs = ref.shape[axis] // 2
    j = lax.broadcasted_iota(jnp.int32, ref.shape, axis)
    pos = lax.broadcasted_iota(jnp.int32, ref.shape, 1 - axis)
    sin = (j >= freqs).astype(jnp.int32)
    i = j - freqs * sin
    block, f = short_rows(i, t)
    short = t // 4
    phase = isl * (i * pos) + (1 - isl) * (4 * f * (pos & (short - 1)))
    kept_long = (i <= t // 2).astype(jnp.int32)
    kept_short = ((pos >= block * short) & (pos < (block + 1) * short)).astype(jnp.int32)
    kept = isl * kept_long + (1 - isl) * kept_short
    phase = (phase - (t // 4) * sin) & (t - 1)
    angle = (phase - t // 2).astype(F32) * (2.0 * math.pi / t)
    z = angle * angle
    value = jnp.full_like(z, -1.0 / math.factorial(14))
    for k in range(6, -1, -1):
        value = value * z + (-1.0) ** k / math.factorial(2 * k)
    ref[...] = (-value * kept.astype(F32)).astype(ref.dtype)


def multiplicity(shape, isl, t):
    i = lax.broadcasted_iota(jnp.int32, shape, 0)
    block, f = short_rows(i, t)
    once_long = ((i == 0) | (i == t // 2)).astype(jnp.int32)
    once_short = ((f == 0) | (f == t // 8)).astype(jnp.int32)
    long = (2 - once_long) * (i <= t // 2).astype(jnp.int32)
    short = (2 - once_short) * (block < 4).astype(jnp.int32)
    return (isl * long + (1 - isl) * short).astype(F32)


def causal_masks(m1_ref, m2_ref, isl):
    row = lax.broadcasted_iota(jnp.int32, m1_ref.shape, 0)
    place = (row & 7) + isl * (row - (row & 7))
    m1_ref[...] = (place >= 1).astype(F32)
    m2_ref[...] = (place >= 2).astype(F32)


def inverse_span(isl, t):
    long = isl.astype(F32)
    return long * (1.0 / t) + (1.0 - long) * (4.0 / t)


def front_kernel(
    kind_ref, tok_h, g1_ref, win_h, st_ref, ct_ref, wc_h, cb_ref,
    xs_h, proj_h, mixed_h, filt_h, ss_h, sc_h, th_h, feat_h, q_h, k_h, v_h, tab_h, tabt_h,
    x_s, win_s, wc_s, tab_s, tabt_s, m1_ref, m2_ref, ms_s, n1_s, q_s,
    proj_s, mixed_s, filt_s, ss_s, sc_s, th_s, feat_s, qb_s, k_s, v_s,
    load_sem, out_sem, send_sem, recv_sem,
):
    t, d = n1_s.shape
    f = ms_s.shape[0]
    n = 4
    blk = t // n
    dp, me = lax.axis_index("dp"), lax.axis_index("seq")
    peers = [lax.rem(me + k, n) for k in range(n)]
    half = lax.rem(me, 2)
    pair = me + 1 - 2 * half
    isl = kind_ref[0]
    isp = inverse_span(isl, t)

    block = lambda i: pl.ds(pl.multiple_of(i * blk, blk), blk)
    loads = [
        pltpu.make_async_copy(win_h, win_s, load_sem.at[0]),
        pltpu.make_async_copy(wc_h, wc_s, load_sem.at[1]),
        pltpu.make_async_copy(tok_h.at[me], x_s.at[0, block(me)], load_sem.at[2]),
        pltpu.make_async_copy(tok_h.at[n + me // 2], x_s.at[1, block(me)], load_sem.at[3]),
    ]

    barrier = pltpu.get_barrier_semaphore()
    for k in range(1, n):
        pl.semaphore_signal(barrier, inc=1, device_id=(dp, peers[k]), device_id_type=MESH)
    pl.semaphore_wait(barrier, n - 1)

    def remote(src, dst, peer, j):
        return pltpu.make_async_remote_copy(
            src_ref=src,
            dst_ref=dst,
            send_sem=send_sem.at[j],
            recv_sem=recv_sem.at[j],
            device_id=(dp, peer),
            device_id_type=MESH,
        )

    whole_slot = [
        remote(tok_h.at[peers[k]], x_s.at[0, block(me)], peers[k], k - 1) for k in range(1, n)
    ]
    to_pair = remote(tok_h.at[n + me // 2], x_s.at[1, block(me)], pair, 3)
    across = remote(tok_h.at[n + peers[2] // 2], x_s.at[1, block(me)], peers[2], 4)
    handed = remote(x_s.at[1, block(peers[2])], x_s.at[1, block(peers[2])], pair, 5)
    for c in whole_slot + [across, to_pair]:
        c.start()
    for c in loads:
        c.start()

    wave_table(tab_s, 0, isl, t)
    wave_table(tabt_s, 1, isl, t)
    causal_masks(m1_ref, m2_ref, isl)
    ms_s[...] = multiplicity(ms_s.shape, isl, t) * isp

    for c in loads[:4]:
        c.wait()
    for c in whole_slot:
        c.wait()

    outs = [
        (x_s, xs_h), (proj_s, proj_h), (ss_s, ss_h), (sc_s, sc_h), (feat_s, feat_h),
        (qb_s, q_h), (k_s, k_h), (v_s, v_h),
        (mixed_s, mixed_h), (filt_s, filt_h), (th_s, th_h),
    ]

    def out_copy(slot, j):
        return pltpu.make_async_copy(outs[j][0].at[slot], outs[j][1].at[slot], out_sem.at[slot, j])

    tables = [
        pltpu.make_async_copy(tab_s, tab_h, load_sem.at[4]),
        pltpu.make_async_copy(tabt_s, tabt_h, load_sem.at[5]),
    ]
    for c in tables:
        c.start()

    @pl.loop(0, 2)
    def _(slot):
        @pl.when(slot == 1)
        def _():
            to_pair.wait()
            handed.wait()

        @pl.loop(0, t // 128)
        def _(r):
            rows = pl.ds(pl.multiple_of(r * 128, 128), 128)
            u, _ = unit_rows(x_s[slot, rows, :].astype(F32))
            n1_s[rows, :] = (u * g1_ref[...].reshape(1, d)).astype(BF)

        @pl.loop(0, d // d)
        def _(c):
            m1, m2 = lanes(m1_ref, d), lanes(m2_ref, d)
            own = cols_at(c, d)

            def part(k):
                cols = cols_at(c, d, k * d)
                p = mm(n1_s[...], win_s[:, cols]).astype(BF)
                proj_s[slot, k, :, own] = p
                return conv(p.astype(F32), st_ref[:, cols], m1, m2)

            query = part(0)
            q_s[:, own] = query
            qb_s[slot, :, own] = query.astype(BF)
            key = part(1)
            k_s[slot, :, own] = key.astype(BF)
            value = part(2).astype(BF)
            v_s[slot, :, own] = value
            value_f = value.astype(F32)
            signal = (key * value_f).astype(BF)
            ss_s[slot, :, own] = mm(tab_s[...], signal).astype(BF)
            cond = conv(value_f, ct_ref[:, own], m1, m2).astype(BF)
            xc = mm(tab_s[...], cond)
            sc_s[slot, :, own] = xc.astype(BF)
            power = (xc[:f] * xc[:f] + xc[f:] * xc[f:]) * isp
            feat_s[slot, :, own] = jnp.log1p(power).astype(BF)

        for j in range(8):
            out_copy(slot, j).start()

        @pl.when(slot == 0)
        def _():
            across.wait()
            handed.start()

        @pl.loop(0, d // d)
        def _(c):
            own = cols_at(c, d)
            th = jnp.tanh(mm(feat_s[slot], wc_s[:, own]) + cb_ref[...].reshape(1, d))
            th_s[slot, :, own] = th
            g = (1.0 + th) * lanes(ms_s, d)
            xs = ss_s[slot, :, own].astype(F32)
            y = jnp.concatenate([(g * xs[:f]).astype(BF), (g * xs[f:]).astype(BF)], axis=0)
            filt = mm(tabt_s[...], y)
            filt_s[slot, :, own] = filt.astype(BF)
            mixed_s[slot, :, own] = (q_s[:, own] * filt).astype(BF)

        for j in range(8, 11):
            out_copy(slot, j).start()

    for slot in range(2):
        for j in range(11):
            out_copy(slot, j).wait()
    for c in tables:
        c.wait()


def front(kind, tok, g1, w_in, st, ct, w_cond, cb):
    slots, blk, d = tok.shape
    t = 4 * blk
    f = -(-max(t // 2 + 1, 4 * (blk // 2 + 1)) // 16) * 16
    hbm = pl.BlockSpec(memory_space=pl.ANY)
    vm = pl.BlockSpec(memory_space=pltpu.VMEM)
    smem = pl.BlockSpec(memory_space=pltpu.SMEM)
    per_slot = [
        ((2, t, d), BF), ((2, 3, t, d), BF), ((2, t, d), BF), ((2, t, d), BF),
        ((2, 2 * f, d), BF), ((2, 2 * f, d), BF), ((2, f, d), F32), ((2, f, d), BF),
        ((2, t, d), BF), ((2, t, d), BF), ((2, t, d), BF),
    ]
    xs, *rest = [jax.ShapeDtypeStruct(*s) for s in per_slot]
    tables = [((2 * f, t), BF), ((t, 2 * f), BF)]
    return pl.pallas_call(
        front_kernel,
        name="front",
        out_shape=(xs, *rest)
        + tuple(jax.ShapeDtypeStruct(*s) for s in tables),
        in_specs=[smem, hbm, vm, hbm, vm, vm, hbm, vm],
        out_specs=(hbm,) * 13,
        scratch_shapes=[
            pltpu.VMEM((2, t, d), BF), pltpu.VMEM((d, 3 * d), BF), pltpu.VMEM((d, d), BF),
            pltpu.VMEM(*tables[0]), pltpu.VMEM(*tables[1]),
            pltpu.VMEM((32, 128), F32), pltpu.VMEM((32, 128), F32), pltpu.VMEM((f, 128), F32),
            pltpu.VMEM((t, d), BF), pltpu.VMEM((t, d), F32),
        ]
        + [pltpu.VMEM(*s) for s in per_slot[1:]]
        + [
            pltpu.SemaphoreType.DMA((6,)),
            pltpu.SemaphoreType.DMA((2, 11)),
            pltpu.SemaphoreType.DMA((6,)),
            pltpu.SemaphoreType.DMA((6,)),
        ],
        compiler_params=pltpu.CompilerParams(
            collective_id=0, has_side_effects=True, vmem_limit_bytes=VMEM_LIMIT
        ),
    )(kind, tok, g1, w_in, st, ct, w_cond, cb)


def add_into(dst, src):
    dst[...] = (dst[...].astype(F32) + src[...].astype(F32)).astype(dst.dtype)


def back_kernel(side, *refs):
    (
        kind_ref, mixed_h, xs_h, cot_h, wo_h, g2_ref, wg_h, wu_h, wd_h,
        proj_h, filt_h, ss_h, cs_h, th_h, feat_h, q_h, k_h, v_h,
        st_ref, ct_ref, wc_h, tab_h, tabt_h, g1_ref, win_h,
        lay6_h, gtok6_h, odg_h, odu_h, odd_h, owo_h, owc_h, owi_h, spool_h, small_out,
        a_s, b_s, u_s, r_s, n2_s, n2t_s, cot_s, mg_s, gmix_s,
        act_s, gg_s, gu_s, wall_s, wo_s, wc_s, tab_s, tabt_s, m1_ref, m2_ref, mult_ref,
        sbg_s, sbu_s, sbd_s, cg_s, cu_s, cd_s,
        dgg_s, dgu_s, xg_s, xu_s, yg_s, yu_s, zg_s, zu_s, d1_s, d2_s, zd_s,
        filt_s, ss_s, cs_s, th_s, feat_s, q_s, k_s, v_s, gpre_s,
        c2_s, raw2_s, rd_s, rx_s, ry_s, z2_s, small_s, sgot_s, ssum_s,
        load_sem, w_sem, spool_sem, back_sem, send_sem, recv_sem, local_sem,
    ) = refs
    n, d = n2_s.shape
    t = filt_s.shape[0]
    f = th_s.shape[0]
    isl = kind_ref[0]
    isp = inverse_span(isl, t)
    h = d // 2
    quarter = d // 4
    step48 = d // 16
    dr = h // 4

    dp, me = lax.axis_index("dp"), lax.axis_index("seq")
    core = lax.rem(dp, 2)
    x = lax.rem(lax.rem(dp // 2, side), 2)
    y = lax.rem(dp // (2 * side), 2)
    dp_x = dp + 2 - 4 * x
    dp_y = dp + 2 * side - 4 * side * y
    at_core, at_x, at_y = (dp + 1 - 2 * core, me), (dp_x, me), (dp_y, me)
    at_xy = (dp_x + dp_y - dp, me)
    peers = [lax.rem(me + k, 4) for k in range(4)]
    at_z = [(dp, peers[k]) for k in range(4)]
    half = lax.rem(me, 2)
    at_pair = (dp, me + 1 - 2 * half)
    half_at = pl.ds(pl.multiple_of(half * RB, RB), RB)
    xy = 2 * x + y
    diag, by_x, by_y = 3 - xy, 2 * (1 - x) + y, 2 * x + 1 - y

    def owner(s):
        if isinstance(s, int):
            return (diag, by_x, by_y, xy)[s]
        return 2 * jnp.where(s < 2, 1 - x, x) + jnp.where(lax.rem(s, 2) == 0, 1 - y, y)

    def rows_at(i, size, base=0):
        return pl.ds(pl.multiple_of(base + i * size, math.gcd(size, base) if base else size), size)

    def each(copies, what):
        for c in copies:
            getattr(c, what)()

    row_moves = lambda src, dst: [
        (src.at[0], dst.at[pl.ds(0, t)]),
        (src.at[1, half_at], dst.at[pl.ds(t, RB)]),
    ]
    moves = (
        row_moves(mixed_h, mg_s)
        + row_moves(xs_h, gmix_s)
        + [(wo_h, wo_s)]
        + [(tab_h, tab_s), (tabt_h, tabt_s), (wc_h, wc_s)]
        + [(proj_h, wall_s.at[pl.ds(3 * d, 6 * t)])]
    )
    loads = [pltpu.make_async_copy(s, e, load_sem.at[j]) for j, (s, e) in enumerate(moves)]
    slot_moves = [
        (filt_h, filt_s), (ss_h, ss_s), (th_h, th_s), (q_h, q_s),
        (cs_h, cs_s), (feat_h, feat_s), (k_h, k_s), (v_h, v_s),
    ]
    slot_load = lambda slot, j: pltpu.make_async_copy(
        slot_moves[j][0].at[slot], slot_moves[j][1], load_sem.at[11 + j]
    )
    x_loads = [
        pltpu.make_async_copy(a, b, load_sem.at[19 + j])
        for j, (a, b) in enumerate(row_moves(xs_h, cot_s))
    ]

    def weight(k, b):
        return pl.ds(pl.multiple_of((3 * b + k) * d, RB), d)

    def weights(s, b):
        cols = cols_at(owner(s), d)
        return [
            pltpu.make_async_copy(src, wall_s.at[weight(k, b)], w_sem.at[b, k])
            for k, src in enumerate((wg_h.at[:, cols], wu_h.at[:, cols], wd_h.at[cols, :]))
        ]

    win_loads = [
        pltpu.make_async_copy(
            win_h.at[:, k * d : (k + 1) * d], wall_s.at[weight(k, 0)], w_sem.at[2, k]
        )
        for k in range(3)
    ]

    def proj_rows(slot, part, offset, size):
        return pl.ds(pl.multiple_of(3 * d + (3 * slot + part) * t + offset, RB), size)

    each(loads[:5], "start")
    each(weights(3, 0), "start")

    barrier = pltpu.get_barrier_semaphore()
    everyone = [at_core, at_x, at_y, at_xy] + at_z[1:]
    for peer in everyone:
        pl.semaphore_signal(barrier, inc=1, device_id=peer, device_id_type=MESH)
    pl.semaphore_wait(barrier, len(everyone))

    causal_masks(m1_ref, m2_ref, isl)
    mult_ref[...] = multiplicity(mult_ref.shape, isl, t)

    def remote(src, dst, peer, j):
        return pltpu.make_async_remote_copy(
            src_ref=src,
            dst_ref=dst,
            send_sem=send_sem.at[j],
            recv_sem=recv_sem.at[j],
            device_id=peer,
            device_id_type=MESH,
        )

    C, DG, XS, YS, ZD, ZG, GA, GC = 0, 12, 20, 22, 24, 27, 36, 45
    LAY, GT0, GT1, PAIR, SMALL, COT, DX, DY, UNIT = 57, 63, 66, 69, 70, 76, 82, 90, 94

    rows128 = lay6_h.shape[1]
    sources = [lax.rem(me + 4 - k, 4) for k in range(4)]
    sends_part = [lax.rem(p, 2) == me // 2 for p in peers]
    gets_part = [half == s // 2 for s in sources]

    def cot_copies(k):
        moves = (
            (cot_h.at[peers[k]], cot_s.at[rows_at(me, rows128)]),
            (cot_h.at[4 + peers[k] // 2], cot_s.at[rows_at(half, rows128, t)]),
        )
        if k == 0:
            return [
                pltpu.make_async_copy(a, b, load_sem.at[9 + j]) for j, (a, b) in enumerate(moves)
            ]
        return [remote(a, b, at_z[k], COT + 2 * (k - 1) + j) for j, (a, b) in enumerate(moves)]

    for k in (1, 2, 3, 0):
        full, part = cot_copies(k)
        full.start()
        pl.when(sends_part[k])(part.start)

    each(loads[:5], "wait")

    @pl.loop(0, n // RB)
    def _(i):
        rows = rows_at(i, RB)
        hid = gmix_s[rows, :].astype(F32) + mm(mg_s[rows, :], wo_s[...])
        a_s[rows, :] = hid
        b_s[rows, :] = jnp.zeros_like(hid)
        u, r = unit_rows(hid)
        u_s[rows, :] = u
        r_s[rows, :] = jnp.broadcast_to(r, (RB, 128))
        n2 = u * g2_ref[...].reshape(1, d)
        n2_s[rows, :] = n2.astype(BF)
        n2t_s[:, rows] = n2.T.astype(BF)

    each(loads[5:-1], "start")
    for j in range(8):
        slot_load(0, j).start()

    pairs = ((sbg_s, cg_s, dgg_s, xg_s, yg_s, zg_s), (sbu_s, cu_s, dgu_s, xu_s, yu_s, zu_s))
    rank_rows = lambda q: pl.ds(q * quarter, quarter)

    def core_copies(s):
        bufs = ((sbg_s, cg_s.at[s]), (sbu_s, cu_s.at[s]), (sbd_s, cd_s.at[owner(s)]))
        return [remote(a, b, at_core, C + 4 * j + s) for j, (a, b) in enumerate(bufs)]

    def diag_copies(odd):
        return [
            remote(p[1].at[0, rank_rows(q)], p[2].at[rank_rows(q)], at_y if odd else at_x, DG + 4 * j + q)
            for j, p in enumerate(pairs)
            for q in ((1, 3) if odd else (0, 2))
        ]

    x_copies = lambda: [remote(p[1].at[1], p[3], at_x, XS + j) for j, p in enumerate(pairs)]
    y_copies = lambda: [remote(p[1].at[2], p[4], at_y, YS + j) for j, p in enumerate(pairs)]

    def down_first(q, peer, k, e):
        return remote(cd_s.at[q, rows_at(k, dr)], d1_s.at[q, e], peer, DX + 2 * q + e)

    def step_sums(s, j):
        p = pairs[j]

        def add_ranks(first):
            for q in (first, first + 2):
                add_into(p[1].at[s, rank_rows(q)], p[2].at[rank_rows(q)])

        @pl.when(s == 0)
        def _():
            each(diag_copies(False)[2 * j : 2 * j + 2], "start")
            each(diag_copies(True)[2 * j : 2 * j + 2], "start")

        @pl.when(s == 1)
        def _():
            each(diag_copies(True)[2 * j : 2 * j + 2], "wait_recv")
            add_ranks(1)
            x_copies()[j].start()

        @pl.when(s == 2)
        def _():
            each(diag_copies(False)[2 * j : 2 * j + 2], "wait_recv")
            add_ranks(0)
            y_copies()[j].start()

    saved = (act_s, gu_s, gg_s)

    def spool(s, i, j):
        rows = rows_at(i, RB)
        return pltpu.make_async_copy(
            saved[j].at[rows], spool_h.at[j, s, rows], spool_sem.at[i, j]
        )

    @pl.loop(0, 4)
    def _(p):
        s, b = 3 - p, lax.rem(p, 2)
        each(weights(s, b), "wait")

        @pl.when(p < 3)
        def _():
            each(weights(s - 1, 1 - b), "start")

        @pl.loop(0, n // RB)
        def _(i):
            rows = rows_at(i, RB)

            @pl.when(p > 0)
            def _():
                for j in range(3):
                    spool(s, i, j).wait()

            n2 = n2_s[rows, :]
            pre = mm(n2, wall_s[weight(0, b), :])
            lin = mm(n2, wall_s[weight(1, b), :])
            sg = 1.0 / (1.0 + jnp.exp(-pre))
            silu = pre * sg
            act = (silu * lin).astype(BF)
            act_s[rows, :] = act
            gu_s[rows, :] = silu.astype(BF)
            gg_s[rows, :] = (lin * sg * (1.0 + pre * (1.0 - sg))).astype(BF)
            a_s[rows, :] += mm(act, wall_s[weight(2, b), :])

            @pl.when(p < 3)
            def _():
                for j in range(3):
                    spool(s, i, j).start()

    @pl.loop(0, n // RB)
    def _(i):
        rows = rows_at(i, RB)
        n2_s[rows, :] = a_s[rows, :].astype(BF)

    sends_half = [half == p // 2 for p in peers]
    gets_half = [lax.rem(s, 2) == me // 2 for s in sources]

    def home(buf, out, part, base, k):
        if part == 0:
            src, dst = buf.at[rows_at(peers[k], rows128)], out.at[me]
        else:
            src, dst = buf.at[rows_at(lax.rem(peers[k], 2), rows128, t)], out.at[4 + me // 2]
        if k == 0:
            return pltpu.make_async_copy(src, dst, local_sem.at[base])
        return remote(src, dst, at_z[k], base + k - 1)

    def home_start(buf, out, part, base, local):
        for k in range(4):
            copy = home(buf, out, part, base if k else local, k)
            if part == 0:
                copy.start()
            else:
                pl.when(sends_half[k])(copy.start)

    def home_wait(buf, out, part, base, local):
        for k in range(4):
            copy = home(buf, out, part, base if k else local, k)
            if part == 0:
                copy.wait()
            elif k == 0:
                pl.when(sends_half[0])(copy.wait)
            else:
                pl.when(sends_half[k])(copy.wait_send)
                pl.when(gets_half[k])(copy.wait_recv)

    for k in range(4):
        full, part = cot_copies(k)
        full.wait()
        if k == 0:
            pl.when(sends_part[0])(part.wait)
        else:
            pl.when(sends_part[k])(part.wait_send)
            pl.when(gets_part[k])(part.wait_recv)

    def unspool(s, j):
        return pltpu.make_async_copy(spool_h.at[j, s], saved[j], back_sem.at[j])

    @pl.loop(0, 4)
    def _(s):
        b = lax.rem(s + 1, 2)

        @pl.when(s > 0)
        def _():
            each(weights(s, b), "wait")

        @pl.when(s < 3)
        def _():
            each(weights(s + 1, 1 - b), "start")

        pl.when(s == 3)(loads[-1].start)

        @pl.when(s == 1)
        def _():
            home_start(n2_s, lay6_h, 0, LAY, 0)
            home_start(n2_s, lay6_h, 1, LAY + 3, 1)

        @pl.when(s > 0)
        def _():
            unspool(s, 1).wait()
            unspool(s, 2).wait()

        @pl.loop(0, n // RB)
        def _(i):
            rows = rows_at(i, RB)
            g_act = mm_nt(cot_s[rows, :], wall_s[weight(2, b), :])
            g_up = (g_act * gu_s[rows, :].astype(F32)).astype(BF)
            gu_s[rows, :] = g_up
            g_gate = (g_act * gg_s[rows, :].astype(F32)).astype(BF)
            gg_s[rows, :] = g_gate
            b_s[rows, :] += mm_nt(g_gate, wall_s[weight(0, b), :]) + mm_nt(
                g_up, wall_s[weight(1, b), :]
            )

        @pl.when(s > 0)
        def _():
            each(core_copies(s - 1), "wait_send")

        def product(which, j, put):
            cols = cols_at(which, h)

            @pl.loop(0, d // RB)
            def _(i):
                rows, out = rows_at(i, RB), cols_at(i, RB)
                if j == 2:
                    put(slice(None), out, mm_tn(act_s[:, cols], cot_s[:, out]))
                else:
                    put(rows, slice(None), mm(n2t_s[rows, :], (gg_s, gu_s)[j][:, cols]))

        for j, buf in enumerate((sbg_s, sbu_s, sbd_s)):

            def put(rows, cols, value, buf=buf):
                buf[rows, cols] = value.astype(BF)

            if j == 2:
                pl.when(s > 0)(unspool(s, 0).wait)
            product(1 - core, j, put)
            core_copies(s)[j].start()
        for j, (buf, at) in enumerate(((cg_s, s), (cu_s, s), (cd_s, owner(s)))):
            core_copies(s)[j].wait_recv()

            def put(rows, cols, value, buf=buf, at=at):
                buf[at, rows, cols] = (buf[at, rows, cols].astype(F32) + value).astype(BF)

            product(core, j, put)
            pl.when(s < 3)(unspool(s + 1, (2, 1, 0)[j]).start)
            if j < 2:
                step_sums(s, j)
        mine = owner(s)

        @pl.when(lax.rem(mine, 2) == 0)
        def _():
            down_first(mine, at_x, diag, 0).start()
            down_first(mine, at_x, by_x, 1).start()

        @pl.when(lax.rem(mine, 2) == 1)
        def _():
            down_first(mine, at_y, diag, 0).start()
            down_first(mine, at_y, by_y, 1).start()


    each(win_loads, "start")
    small_s[...] = jnp.zeros_like(small_s)

    @pl.loop(0, n // RB)
    def _(i):
        rows = rows_at(i, RB)
        g, u = b_s[rows, :], u_s[rows, :]
        small_s[14:15, :] += jnp.sum(g * u, axis=0, keepdims=True)
        gh = cot_s[rows, :].astype(F32) + unit_back(g, u, r_s[rows, 0:1], g2_ref[...].reshape(1, d))
        gmix_s[rows, :] = gh.astype(BF)

    each(x_loads, "start")
    pair_at = rows_at(half, RB, n)
    mg_s[pair_at, :] = mm_nt(gmix_s[t:, :], wo_s[...]).astype(BF)
    pair_copy = remote(mg_s.at[pair_at], mg_s.at[pair_at], at_pair, PAIR)
    pair_copy.start()

    each(core_copies(3), "wait_send")

    def pos(q):
        return q // 2 + 2 * (q % 2 if isinstance(q, int) else lax.rem(q, 2))

    def reorder(dst, src, which):
        cols = cols_at(which, h)
        for q in range(4):
            for k in range(4):
                to, fr = (4 * k + pos(q)) * step48, (4 * q + k) * step48
                dst[to : to + step48, :] = src[fr : fr + step48, cols].astype(BF)

    def unit_core(u):
        return remote((sbg_s, sbu_s)[u % 2], c2_s.at[u], at_core, UNIT + 15 * u)

    raw_of = lambda u: raw2_s.at[2 if u == 4 else u % 2]
    two = 2 * step48

    def unit_diag(u):
        return [
            remote(
                c2_s.at[u, rows_at(2 * diag + e, two)],
                rd_s.at[u, pl.ds(e * two, two)],
                (at_x, at_y)[e],
                UNIT + 15 * u + 1 + e,
            )
            for e in range(2)
        ]

    def unit_near(u):
        return [
            remote(c2_s.at[u, rows_at(by_x, quarter)], rx_s.at[u], at_x, UNIT + 15 * u + 3),
            remote(c2_s.at[u, rows_at(by_y, quarter)], ry_s.at[u], at_y, UNIT + 15 * u + 4),
        ]

    def unit_rank(q):
        return rows_at(4 * xy + pos(q), step48)

    def unit_z(u):
        return [
            remote(
                c2_s.at[u, unit_rank(peers[k])], z2_s.at[u, k - 1], at_z[k], UNIT + 15 * u + 4 + k
            )
            for k in range(1, 4)
        ]

    def unit_view(u):
        if u in (0, 4):
            out = owc_h if u == 0 else owo_h
            return lambda k, c: out.at[rows_at(k, step48), cols_at(c, h)]
        return lambda k, c: owi_h.at[rows_at(k, step48), cols_at(3 * c + u - 1, h)]

    def unit_gather(u):
        return gather(c2_s.at[u, unit_rank(me)], unit_view(u), UNIT + 15 * u + 8, 5 + u)

    def unit_gather_core(u):
        return gather_core(unit_view(u), UNIT + 15 * u + 11)

    def unit1(u):
        unit_core(u).wait()

        @pl.loop(0, 4)
        def _(k):
            add_into(c2_s.at[u, rows_at(k, quarter)], raw_of(u).at[rows_at(k, quarter)])

        each(unit_diag(u), "start")

    def unit2(u):
        each(unit_diag(u), "wait")
        add_into(c2_s.at[u, rows_at(2 * by_y, two)], rd_s.at[u, 0:two])
        add_into(c2_s.at[u, rows_at(2 * by_x + 1, two)], rd_s.at[u, two : 2 * two])
        each(unit_near(u), "start")

    def unit3(u):
        each(unit_near(u), "wait")
        at = c2_s.at[u, rows_at(xy, quarter)]
        total = at[...].astype(F32) + rx_s[u].astype(F32) + ry_s[u].astype(F32)
        at[...] = total.astype(BF)
        each(unit_z(u), "start")

    def unit4(u):
        each(unit_z(u), "wait")
        at = c2_s.at[u, unit_rank(me)]
        total = at[...].astype(F32)
        for k in range(3):
            total += z2_s[u, k].astype(F32)
        at[...] = total.astype(BF)
        copies, local = unit_gather(u)
        each(copies, "start")
        local.start()

    def unit5(u):
        copies, local = unit_gather(u)
        each(copies, "wait")
        local.wait()
        each(unit_gather_core(u), "start")

    @pl.loop(0, d // RB)
    def _(i):
        a_s[rows_at(i, RB), :] = mm_tn(mg_s[0:n, cols_at(i, RB)], gmix_s[...])

    reorder(sbg_s, a_s, 1 - core)
    unit_core(4).start()
    reorder(raw_of(4), a_s, core)

    each(x_copies(), "wait_recv")
    for p in pairs:

        @pl.loop(0, 4)
        def _(q, p=p):
            add_into(p[1].at[3, rows_at(q, quarter)], p[3].at[rows_at(q, quarter)])

    @pl.loop(0, t // RB)
    def _(i):
        rows = rows_at(i, RB)
        mg_s[rows, :] = mm_nt(gmix_s[rows, :], wo_s[...]).astype(BF)

    def z_copies(j):
        p = pairs[j]
        return [
            remote(p[1].at[3, rows_at(peers[k], quarter)], p[5].at[k - 1], at_z[k], ZG + 3 * j + k - 1)
            for k in range(1, 4)
        ]

    def y_end(j):
        p = pairs[j]
        y_copies()[j].wait_recv()

        @pl.loop(0, 4)
        def _(q):
            add_into(p[1].at[3, rows_at(q, quarter)], p[4].at[rows_at(q, quarter)])

        each(z_copies(j), "start")

    y_end(0)

    down_second = [
        remote(d1_s.at[q, 0], d2_s.at[q], at_x if q % 2 else at_y, DY + q) for q in range(4)
    ]
    down_z = [
        remote(d1_s.at[peers[k], 1], zd_s.at[k - 1], at_z[k], ZD + k - 1) for k in range(1, 4)
    ]

    def down_first_end():
        for q in range(4):
            for e in range(2):
                remote(d1_s.at[q, e], d1_s.at[q, e], at_x, DX + 2 * q + e).wait()
            add_into(d1_s.at[q, 0], cd_s.at[q, rows_at(by_x if q % 2 else by_y, dr)])
            add_into(d1_s.at[q, 1], cd_s.at[q, rows_at(xy, dr)])
        each(down_second, "start")

    def down_second_end():
        each(down_second, "wait")
        for q in range(4):
            add_into(d1_s.at[q, 1], d2_s.at[q])
        each(down_z, "start")

    def gather(src, view, base, first_local):
        return [
            remote(src, view(xy, core), peer, base + k)
            for k, peer in enumerate((at_x, at_y, at_xy))
        ], pltpu.make_async_copy(src, view(xy, core), local_sem.at[first_local])

    def gather_core(view, base):
        return [remote(view(k, core), view(k, core), at_core, base + k) for k in range(4)]

    view_dg = lambda k, c: odg_h.at[:, cols_at(2 * k + c, h)]
    view_du = lambda k, c: odu_h.at[:, cols_at(2 * k + c, h)]
    view_dd = lambda k, c: odd_h.at[rows_at(4 * c + k, dr)]
    gathers = [
        gather(cg_s.at[3, rows_at(me, quarter)], view_dg, GA, 10),
        gather(cu_s.at[3, rows_at(me, quarter)], view_du, GA + 3, 11),
        gather(d1_s.at[me, 1], view_dd, GA + 6, 12),
    ]
    core_gathers = (
        gather_core(view_dg, GC) + gather_core(view_du, GC + 4) + gather_core(view_dd, GC + 8)
    )

    def keep_norm(u, rows):
        n1t = (u * g1_ref[...].reshape(1, d)).T.astype(BF)
        for q in range(4):
            for k in range(4):
                to, fr = (4 * k + pos(q)) * step48, (4 * q + k) * step48
                n2t_s[to : to + step48, rows] = n1t[fr : fr + step48]

    def token_rows(slot, rows, offset, u, r):
        g = jnp.zeros((RB, d), F32)
        for part in range(3):
            g += mm_nt(wall_s[proj_rows(slot, part, offset, RB), :], wall_s[weight(part, 0), :])
        small_s[0:1, :] += jnp.sum(g * u, axis=0, keepdims=True)
        gmix_s[rows, :] = (
            gmix_s[rows, :].astype(F32) + unit_back(g, u, r, g1_ref[...].reshape(1, d))
        ).astype(BF)

    each(loads[5:], "wait")
    each(x_loads, "wait")

    @pl.loop(0, 2)
    def _(slot):
        share = jnp.where(slot == 0, 1.0, 0.5)
        for j in range(4):
            slot_load(slot, j).wait()
        pl.when(slot == 1)(pair_copy.wait)
        gm_at = pl.ds(pl.multiple_of(slot * n, RB), t)

        @pl.loop(0, d // CB)
        def _(c):
            mult = lanes(mult_ref, CB)
            cols = cols_at(c, CB)
            query = q_s[:, cols].astype(F32)
            gm = mg_s[gm_at, cols].astype(F32)
            a_s[0:t, cols] = gm * filt_s[:, cols].astype(F32)
            spec = mm(tab_s[...], (gm * query).astype(BF)) * isp
            ss = ss_s[:, cols].astype(F32)
            th = th_s[:, cols]
            g_gain = spec[:f] * ss[:f] + spec[f:] * ss[f:]
            g_pre = (g_gain * (1.0 - th * th)).astype(BF)
            gpre_s[:, cols] = g_pre
            weighted = g_pre.astype(F32) * mult
            small_s[13:14, cols] += share * jnp.sum(weighted, axis=0, keepdims=True)
            g = (1.0 + th) * mult
            yy = jnp.concatenate(
                [(g * spec[:f]).astype(BF), (g * spec[f:]).astype(BF)], axis=0
            )
            b_s[0:t, cols] = mm(tabt_s[...], yy)

        @pl.when(slot == 0)
        def _():
            for j in range(4):
                slot_load(1, j).start()
            y_end(1)
            unit1(4)

        @pl.when(slot == 1)
        def _():
            for j, p in enumerate(pairs):
                each(z_copies(j), "wait")
                rows = rows_at(me, quarter)
                total = p[1][3, rows, :].astype(F32)
                for k in range(3):
                    total += p[5][k].astype(F32)
                p[1][3, rows, :] = total.astype(BF)
            for copies, local in gathers[:2]:
                each(copies, "start")
                local.start()
            down_second_end()
            unit3(4)
            home_start(gmix_s, gtok6_h, 0, GT0, 2)

        for j in range(4, 8):
            slot_load(slot, j).wait()

        @pl.loop(0, d // CB)
        def _(c):
            m1, m2 = lanes(m1_ref, CB), lanes(m2_ref, CB)
            cols = cols_at(c, CB)
            g_feat = mm_nt(gpre_s[...], wc_s[cols, :])
            xc = cs_s[:, cols].astype(F32)
            power = (xc[:f] * xc[:f] + xc[f:] * xc[f:]) * isp
            g_pow = g_feat / (1.0 + power) * (lanes(mult_ref, CB) * (2.0 * isp))
            yy = jnp.concatenate(
                [(g_pow * xc[:f]).astype(BF), (g_pow * xc[f:]).astype(BF)], axis=0
            )
            g_cond = mm(tabt_s[...], yy)
            feat = (feat_s[:, cols].astype(F32) * lanes(mult_ref, CB)).astype(BF)
            dwc = share * mm_tn(feat, gpre_s[...])

            @pl.when(slot == 0)
            def _():
                u_s[cols, :] = dwc

            @pl.when(slot == 1)
            def _():
                u_s[cols, :] += dwc

            def finish(part, g_conv, p):
                at = cols_at(c, CB, part * d)
                back, sums = conv_back(g_conv, p, st_ref[:, at], m1, m2)
                for j in range(3):
                    row = 1 + 3 * j + part
                    small_s[row : row + 1, cols] += share * sums[j]
                wall_s[proj_rows(slot, part, 0, t), cols] = back.astype(BF)

            projected = lambda part: wall_s[proj_rows(slot, part, 0, t), cols].astype(F32)
            finish(0, a_s[0:t, cols], projected(0))
            value = v_s[:, cols].astype(F32)
            g_sig = b_s[0:t, cols]
            key = k_s[:, cols].astype(F32)
            finish(1, g_sig * value, projected(1))
            back, sums = conv_back(g_cond, value, ct_ref[:, cols], m1, m2)
            for j in range(3):
                small_s[10 + j : 11 + j, cols] += share * sums[j]
            finish(2, g_sig * key + back, projected(2))

        @pl.when(slot == 0)
        def _():
            for j in range(4, 8):
                slot_load(1, j).start()
            each(win_loads, "wait")
            down_first_end()
            unit2(4)

            @pl.loop(0, t // RB)
            def _(i):
                rows = rows_at(i, RB)
                u, r = unit_rows(cot_s[rows, :].astype(F32))
                keep_norm(u, rows)
                token_rows(0, rows, i * RB, u, r)

    def gathers_end(j):
        each(gathers[j][0], "wait")
        gathers[j][1].wait()
        each(core_gathers[4 * j : 4 * j + 4], "start")

    def win_product(u, which, dst):
        at = 3 * which + u - 1
        part, cols = at // 2, cols_at(lax.rem(at, 2), h)
        blocks = [(0, 0), (0, RB), (1, half * RB)]

        @pl.loop(0, d // RB)
        def _(i):
            rows = rows_at(i, RB)
            dw = jnp.zeros((RB, h), F32)
            for k, (slot, offset) in enumerate(blocks):
                g = wall_s[proj_rows(slot, part, offset, RB), cols]
                dw += mm(n2t_s[rows, k * RB : (k + 1) * RB], g)
            dst[rows, :] = dw.astype(BF)

    reorder(sbg_s, u_s, 1 - core)
    unit_core(0).start()
    reorder(raw_of(0), u_s, core)
    last_rows = slice(t, n)
    u1, r1 = unit_rows(cot_s[last_rows, :].astype(F32))
    keep_norm(u1, last_rows)
    win_product(1, 1 - core, sbu_s)
    unit_core(1).start()
    win_product(1, core, raw_of(1))
    unit1(0)
    win_product(2, 1 - core, sbg_s)
    unit_core(2).start()
    win_product(2, core, raw_of(2))
    unit1(1)
    unit2(0)
    win_product(3, 1 - core, sbu_s)
    unit_core(3).start()
    win_product(3, core, raw_of(3))
    unit1(2)
    unit2(1)
    gathers_end(0)
    gathers_end(1)
    unit3(0)
    each(down_z, "wait")
    total = d1_s[me, 1].astype(F32)
    for k in range(3):
        total += zd_s[k].astype(F32)
    d1_s[me, 1] = total.astype(BF)
    each(gathers[2][0], "start")
    gathers[2][1].start()
    unit4(4)
    u1, r1 = unit_rows(cot_s[last_rows, :].astype(F32))
    token_rows(1, last_rows, half * RB, u1, r1)
    small_c = remote(small_s, sgot_s.at[0], at_core, SMALL)
    small_c.start()
    unit1(3)
    unit2(2)
    unit3(1)
    home_start(gmix_s, gtok6_h, 1, GT1, 3)
    unit4(0)
    small_c.wait()
    ssum_s[0] = small_s[...] + sgot_s[0]
    small_x = remote(ssum_s.at[0], sgot_s.at[1], at_x, SMALL + 1)
    small_x.start()
    unit2(3)
    unit3(2)
    unit4(1)
    unit5(0)
    unit5(4)
    small_x.wait()
    ssum_s[1] = ssum_s[0] + sgot_s[1]
    small_y = remote(ssum_s.at[1], sgot_s.at[2], at_y, SMALL + 2)
    small_y.start()
    unit3(3)
    unit4(2)
    gathers_end(2)
    unit5(1)
    small_y.wait()
    ssum_s[2] = ssum_s[1] + sgot_s[2]
    small_z = [
        remote(ssum_s.at[2], sgot_s.at[2 + k], at_z[k], SMALL + 2 + k) for k in range(1, 4)
    ]
    each(small_z, "start")
    unit4(3)
    unit5(2)
    each(small_z, "wait")
    small_out[...] = ssum_s[2] + sgot_s[3] + sgot_s[4] + sgot_s[5]
    unit5(3)

    each(diag_copies(False) + diag_copies(True) + x_copies() + y_copies(), "wait_send")
    each(core_gathers, "wait")
    for u in range(5):
        each(unit_gather_core(u), "wait")
    home_wait(n2_s, lay6_h, 0, LAY, 0)
    home_wait(n2_s, lay6_h, 1, LAY + 3, 1)
    home_wait(gmix_s, gtok6_h, 0, GT0, 2)
    home_wait(gmix_s, gtok6_h, 1, GT1, 3)


def back(
    side, slots, kind, mixed, xs, cot, w_out, g2, w_gate, w_up, w_down,
    proj, filt, ss, cs, th, feat, query, key, value, st, ct, w_cond, table, table_t, g1, w_in,
):
    t, d = xs.shape[1:]
    n = t + t // 2
    f2 = table.shape[0]
    f = f2 // 2
    h, q4, dr, s48 = d // 2, d // 4, d // 8, d // 16
    hbm = pl.BlockSpec(memory_space=pl.ANY)
    vm = pl.BlockSpec(memory_space=pltpu.VMEM)
    smem = pl.BlockSpec(memory_space=pltpu.SMEM)
    b = lambda *s: pltpu.VMEM(s, BF)
    g = lambda *s: pltpu.VMEM(s, F32)
    return pl.pallas_call(
        functools.partial(back_kernel, side),
        name="back",
        out_shape=tuple(
            jax.ShapeDtypeStruct(s, BF)
            for s in (
                (slots, t // 4, d), (slots, t // 4, d), (q4, 4 * d), (q4, 4 * d), (d, d),
                (q4, d), (q4, d), (q4, 3 * d), (3, 4, n, d),
            )
        )
        + (jax.ShapeDtypeStruct((16, d), F32),),
        in_specs=[smem] + [hbm] * 4 + [vm] + [hbm] * 12 + [vm, vm, hbm, hbm, hbm, vm, hbm],
        out_specs=(hbm,) * 9 + (vm,),
        scratch_shapes=[
            g(n, d), g(n, d), g(n, d), g(n, 128),
            b(n, d), b(d, n), b(n, d), b(n + t, d), b(n, d),
            b(n, d), b(n, d), b(n, d), b(3 * d + 6 * t, d), b(d, d), b(d, d),
            b(f2, t), b(t, f2), g(32, 128), g(32, 128), g(f, 128),
            b(d, h), b(d, h), b(h, d),
            b(4, d, h), b(4, d, h), b(4, h, d),
            b(d, h), b(d, h), b(d, h), b(d, h), b(d, h), b(d, h),
            b(3, q4, h), b(3, q4, h), b(4, 2, dr, d), b(4, dr, d), b(3, dr, d),
            b(t, d), b(f2, d), b(f2, d), g(f, d), b(f, d), b(t, d), b(t, d), b(t, d), b(f, d),
            b(5, d, h), b(3, d, h), b(5, q4, h), b(5, q4, h), b(5, q4, h), b(5, 3, s48, h),
            g(16, d), g(6, 16, d), g(3, 16, d),
            pltpu.SemaphoreType.DMA((21,)),
            pltpu.SemaphoreType.DMA((3, 3)),
            pltpu.SemaphoreType.DMA((3, 3)),
            pltpu.SemaphoreType.DMA((3,)),
            pltpu.SemaphoreType.DMA((169,)),
            pltpu.SemaphoreType.DMA((169,)),
            pltpu.SemaphoreType.DMA((13,)),
        ],
        compiler_params=pltpu.CompilerParams(
            collective_id=1, has_side_effects=True, vmem_limit_bytes=65400 * 1024
        ),
    )(
        kind, mixed, xs, cot, w_out, g2, w_gate, w_up, w_down, proj, filt, ss, cs, th, feat,
        query, key, value, st, ct, w_cond, table, table_t, g1, w_in,
    )


def on_device(
    tokens, kind, ln1_gain, w_in, short_taps, cond_taps, w_cond, cond_bias, w_out, ln2_gain,
    w_gate, w_up, w_down, cotangent,
):
    _, rows, slots, d = tokens.shape
    n = lax.axis_size("seq")
    dp_count = lax.axis_size("dp")
    rank = lax.axis_index("seq")
    tok6 = jnp.transpose(tokens[0], (1, 0, 2))
    cot6 = jnp.transpose(cotangent[0], (1, 0, 2))
    xs, proj, mixed, filt, sig_spec, cond_spec, th, feat, query, key, value, table, table_t = front(
        kind, tok6, ln1_gain, w_in, short_taps, cond_taps, w_cond, cond_bias
    )
    side = math.isqrt(dp_count // 2)
    lay6, gtok6, *sums, _, small = back(
        side, slots, kind, mixed, xs, cot6, w_out, ln2_gain, w_gate, w_up, w_down,
        proj.reshape(-1, d), filt, sig_spec, cond_spec, th, feat, query, key, value, short_taps, cond_taps, w_cond,
        table, table_t, ln1_gain, w_in,
    )
    layer_out = jnp.transpose(lay6, (1, 0, 2))[None]
    grad_tokens = jnp.transpose(gtok6, (1, 0, 2))[None]

    sums = [a.astype(F32) for a in sums]
    if dp_count > 8:
        groups = [
            [
                (y * side + x) * 2 + core
                for y in range(y0, side, 2)
                for x in range(x0, side, 2)
            ]
            for y0 in range(2)
            for x0 in range(2)
            for core in range(2)
        ]
        sums = [lax.psum(a, "dp", axis_index_groups=groups) for a in sums]
        small = lax.psum(small, "dp", axis_index_groups=groups)
    grad_gate, grad_up, grad_down, grad_w_out, grad_w_cond, grad_w_in = sums
    part = lambda a, width: lax.dynamic_slice_in_dim(a, rank * width, width, a.ndim - 1)
    return (
        layer_out,
        grad_tokens,
        part(small[0], d // n),
        grad_w_in,
        part(small[1:10].reshape(3, 3 * d), 3 * d // n),
        part(small[10:13], d // n),
        grad_w_cond,
        part(small[13], d // n),
        grad_w_out,
        part(small[14], d // n),
        grad_gate,
        grad_up,
        grad_down,
    )


def solution(mesh):
    rows = P("dp", "seq", None, None)
    return jax.shard_map(
        on_device,
        mesh=mesh,
        in_specs=(rows, P("dp")) + (P(),) * 11 + (rows,),
        out_specs=(
            rows,
            rows,
            P("seq"),
            P("seq", None),
            P(None, "seq"),
            P(None, "seq"),
            P("seq", None),
            P("seq"),
            P("seq", None),
            P("seq"),
            P("seq", None),
            P("seq", None),
            P("seq", None),
        ),
        check_vma=False,
    )
```
